256 devices in a mesh: sec: 4 (over y_lo, core), tile: 64 (over x, y_hi, z).
Axes of the slice: x: 4, y: 4 (y_hi: 2, y_lo: 2; y = y_hi * 2 + y_lo), z: 8, core: 2. Of those that a mesh axis runs over, the one named last changes fastest.
Arguments:
- parent_old: float32 [1024, 24, 4096], P('tile', None, 'sec'), may hold values from -6 to 6
- nest_state: float32 [4, 1024, 24, 512], P('sec', 'tile'), may hold values from -6 to 6
- diffusion: float32 [24], replicated, may hold values from 0.04 to 0.1
- wind_speed: float32 [2, 24], replicated, may hold values from 0.05 to 0.25
- conversion: float32 [2, 8], replicated, may hold values from 0.05 to 0.4
- vert_mix: float32 [3], replicated, may hold values from 0.5 to 4
- nest_box: int32 [4, 4], replicated, may hold values from 0 to 3968, as said below
Outputs:
- parent_new: float32 [1024, 24, 4096], P('tile', None, 'sec')
- nest_new: float32 [4, 1024, 24, 512], P('sec', 'tile')
The draws below stay inside these ranges and needn't reach their ends.
Inputs may be any that keep to these rules, and one draw needn't show every extreme that they name: `nest_box`: row n belongs to nest n, which lives on section n. Anchors are parent cells and keep the footprint of 256 by 128 parent cells inside the parent grid; live rows lie between 512 and 1024, live columns between 256 and 512; some nest is live everywhere.
All inputs are finite; a program needn't handle non-finite values.
Results may differ from the reference program's by a relative error of at most 0.00002.
Values sent between devices are 32-bit elements; how exact they have to be, the bound alone decides.
A program may use at most 64 MiB of HBM per device.

```python
import math
import jax
import jax.numpy as jnp
from jax import lax

NY = 512
LEV = 8
NSTEP = 4
CHAN = 24
NNEST = 4
PX = 1024
PY = 4096
NX = 1024


def draw_nest_box(key, part):
    quarter_x = NX // 4
    quarter_y = NY // 4
    anchor_x = jax.random.randint(jax.random.fold_in(key, 11), (NNEST,), 0, PX - quarter_x + 1)
    anchor_y = jax.random.randint(jax.random.fold_in(key, 12), (NNEST,), 0, PY - quarter_y + 1)
    extent_x = jax.random.randint(jax.random.fold_in(key, 13), (NNEST,), NX // 2, NX + 1)
    extent_y = jax.random.randint(jax.random.fold_in(key, 14), (NNEST,), NY // 2, NY + 1)
    shuffled = jax.random.permutation(jax.random.fold_in(key, 15), NNEST)
    nest_ids = jnp.arange(NNEST)
    extent_x = jnp.where(nest_ids == shuffled[0], NX, extent_x)
    extent_y = jnp.where(nest_ids == shuffled[0], NY, extent_y)
    anchor_y = jnp.where(nest_ids == shuffled[1], PY - quarter_y, anchor_y)
    anchor_x = jnp.where(nest_ids == shuffled[2], PX - quarter_x, anchor_x)
    return jnp.stack([anchor_x, anchor_y, extent_x, extent_y], axis=1).astype(jnp.int32)


def block_scale(rng, dims, pieces, least, largest):
    factor_of = 1.0
    for position, parts in pieces:
        draws = jax.random.uniform(jax.random.fold_in(jax.random.fold_in(rng, 6), position), (parts,), jnp.float32, least / len(pieces), largest / len(pieces))
        factor_of = factor_of * jnp.repeat(jnp.exp(draws), dims[position] // parts).reshape((-1,) + (1,) * (len(dims) - 1 - position))
    return factor_of


def noise(own_key, dims, deviation, bound, split=(), kind=jnp.bfloat16):
    array = deviation * jax.random.normal(own_key, dims, jnp.float32)
    if split:
        array = array * block_scale(own_key, dims, split, -0.22, 0.18)
    return jnp.clip(array, -bound, bound).astype(kind)


def setup_inputs(seed: int = 0) -> dict:
    key_of = jax.random.split(jax.random.key(seed), 8)
    parent_old = noise(key_of[0], (PX, CHAN, PY), 1.0, 6.0, ((0, 64), (2, 4)), jnp.float32)
    nest_state = noise(key_of[1], (NNEST, NX, CHAN, NY), 1.0, 6.0, ((0, 4), (1, 64)), jnp.float32)
    diffusion = jnp.clip(jax.random.uniform(key_of[2], (CHAN,), jnp.float32, 0.04, 0.1), 0.04, 0.1)
    wind_speed = jnp.clip(jax.random.uniform(key_of[3], (2, CHAN), jnp.float32, 0.05, 0.25), 0.05, 0.25)
    conversion = jnp.clip(jnp.exp(jax.random.uniform(key_of[4], (2, LEV), jnp.float32, math.log(0.05), math.log(0.4))), 0.05, 0.4)
    vert_mix = jnp.clip(jnp.exp(jax.random.uniform(key_of[5], (3,), jnp.float32, math.log(0.5), math.log(4.0))), 0.5, 4.0)
    nest_box = draw_nest_box(jax.random.fold_in(key_of[7], 71), 0)
    return dict(parent_old=parent_old, nest_state=nest_state, diffusion=diffusion, wind_speed=wind_speed, conversion=conversion, vert_mix=vert_mix, nest_box=nest_box)


def horizontal(padded, diffusion, wind_speed):
    center = padded[1:-1, :, 1:-1]
    above_row = padded[:-2, :, 1:-1]
    below_row = padded[2:, :, 1:-1]
    left_col = padded[1:-1, :, :-2]
    right_col = padded[1:-1, :, 2:]
    spread = diffusion[:, None]
    drift_x = wind_speed[0][:, None]
    drift_y = wind_speed[1][:, None]
    return (center + spread * (above_row + below_row + left_col + right_col - 4.0 * center)
            - drift_x * (center - above_row) - drift_y * (center - left_col))


def vertical(column_data, mixing):
    levels = column_data.shape[1]
    off_diag = -mixing
    ratios = []
    partials = []
    for level_idx in range(levels):
        neighbours = 1.0 if level_idx in (0, levels - 1) else 2.0
        pivot_val = 1.0 + neighbours * mixing
        rhs_now = column_data[:, level_idx]
        if level_idx > 0:
            pivot_val = pivot_val - off_diag * ratios[-1]
            rhs_now = rhs_now - off_diag * partials[-1]
        ratios.append(off_diag / pivot_val)
        partials.append(rhs_now / pivot_val)
    solved = [partials[-1]]
    for level_idx in range(levels - 2, -1, -1):
        solved.insert(0, partials[level_idx] - ratios[level_idx] * solved[0])
    return jnp.stack(solved, axis=1)


def physics(fields, conversion, vert_mix):
    row_count, chan_count, col_count = fields.shape
    levels = conversion.shape[1]
    grouped = fields.reshape(row_count, 3, levels, col_count)
    vapour = grouped[:, 0]
    cloud = grouped[:, 1]
    rain_water = grouped[:, 2]
    condense = conversion[0][:, None] * vapour
    vapour = vapour - condense
    cloud = cloud + condense
    fallout = conversion[1][:, None] * cloud
    cloud = cloud - fallout
    rain_water = rain_water + fallout
    solved = [vertical(vapour, vert_mix[0]), vertical(cloud, vert_mix[1]), vertical(rain_water, vert_mix[2])]
    return jnp.stack(solved, axis=1).reshape(row_count, chan_count, col_count)


def upsample(coarse, base, targets, foot_rows, foot_cols, nest_cols):
    low_row = jnp.floor_divide(targets, 4)
    weight_row = ((targets - 4 * low_row).astype(jnp.float32) / 4.0)[:, None, None]
    first_row = jnp.clip(low_row, 0, foot_rows - 1)
    second_row = jnp.clip(low_row + 1, 0, foot_rows - 1)
    lower_vals = jnp.take(coarse, (first_row - base).astype(jnp.int32), axis=0)
    upper_vals = jnp.take(coarse, (second_row - base).astype(jnp.int32), axis=0)
    row_mix = lower_vals + weight_row * (upper_vals - lower_vals)
    col_ids = jnp.arange(nest_cols, dtype=jnp.int32)
    first_col = jnp.floor_divide(col_ids, 4)
    second_col = jnp.minimum(first_col + 1, foot_cols - 1)
    weight_col = (col_ids - 4 * first_col).astype(jnp.float32) / 4.0
    left_vals = jnp.take(row_mix, first_col, axis=2)
    right_vals = jnp.take(row_mix, second_col, axis=2)
    return left_vals + weight_col * (right_vals - left_vals)


def nest_fields(targets, nest_cols, extent_x, extent_y):
    row_ids = targets[:, None]
    col_ids = jnp.arange(nest_cols, dtype=jnp.int32)[None, :]
    live_mask = ((row_ids >= 0) & (row_ids < extent_x) & (col_ids < extent_y)).astype(jnp.float32)
    distance = jnp.minimum(jnp.minimum(row_ids, col_ids),
                           jnp.minimum(extent_x - 1 - row_ids, extent_y - 1 - col_ids))
    distance = jnp.maximum(distance, 0).astype(jnp.float32)
    nudging = 0.1 + 0.4 * jnp.exp(-distance / 3.0)
    return live_mask[:, None, :], nudging[:, None, :]


def nest_step(rows_padded, live_mask, nudging, forcing_now, diffusion, wind_speed, conversion, vert_mix):
    padded = jnp.pad(rows_padded, ((0, 0), (0, 0), (1, 1)))
    moved = physics(horizontal(padded, diffusion, wind_speed), conversion, vert_mix)
    moved = moved + nudging * (forcing_now - moved)
    return moved * live_mask


def reference(parent_old, nest_state, diffusion, wind_speed, conversion, vert_mix, nest_box):
    padded = jnp.pad(parent_old, ((1, 1), (0, 0), (1, 1)))
    parent_new = physics(horizontal(padded, diffusion, wind_speed), conversion, vert_mix)
    foot_rows = NX // 4
    foot_cols = NY // 4
    chan_count = parent_old.shape[1]
    results = []
    for nest_idx in range(NNEST):
        anchor_x = nest_box[nest_idx, 0].astype(jnp.int32)
        anchor_y = nest_box[nest_idx, 1].astype(jnp.int32)
        extent_x = nest_box[nest_idx, 2].astype(jnp.int32)
        extent_y = nest_box[nest_idx, 3].astype(jnp.int32)
        start = (anchor_x, jnp.int32(0), anchor_y)
        old_part = lax.dynamic_slice(parent_old, start, (foot_rows, chan_count, foot_cols))
        new_part = lax.dynamic_slice(parent_new, start, (foot_rows, chan_count, foot_cols))
        both_times = jnp.concatenate([old_part, new_part], axis=1)
        targets = jnp.arange(NX, dtype=jnp.int32)
        forcing = upsample(both_times, jnp.int32(0), targets, foot_rows, foot_cols, NY)
        live_mask, nudging = nest_fields(targets, NY, extent_x, extent_y)
        forcing_old = forcing[:, :chan_count]
        forcing_new = forcing[:, chan_count:]
        nest_now = nest_state[nest_idx] * live_mask
        for step_num in range(NSTEP):
            weight_now = (step_num + 1) / NSTEP
            forcing_now = forcing_old + weight_now * (forcing_new - forcing_old)
            rows_padded = jnp.pad(nest_now, ((1, 1), (0, 0), (0, 0)))
            nest_now = nest_step(rows_padded, live_mask, nudging, forcing_now,
                                 diffusion, wind_speed, conversion, vert_mix)
        results.append(nest_now)
    return parent_new, jnp.stack(results)
```

```python
import itertools

import jax
import jax.numpy as jnp
from jax import lax
from jax.experimental import pallas as pl
from jax.experimental.pallas import tpu as pltpu
from jax.sharding import Mesh
from jax.sharding import PartitionSpec as P

NSTEP = 4
LEV = 8
SEC = ("yl", "co")
TILE = ("tx", "th", "tz")
LANES = 128
SLOT = 56
MESH = pl.DeviceIdType.MESH
F32 = jnp.float32


def vmem():
    return pl.BlockSpec(memory_space=pltpu.VMEM)


def smem():
    return pl.BlockSpec(memory_space=pltpu.SMEM)


def anywhere():
    return pl.BlockSpec(memory_space=pl.ANY)


def section():
    return lax.axis_index("yl") * 2 + lax.axis_index("co")


def tile_number():
    return lax.axis_index("tx") * 16 + lax.axis_index("th") * 8 + lax.axis_index("tz")


def lane_ids():
    return lax.broadcasted_iota(jnp.int32, (LEV, LANES), 1)


def level_ids():
    return lax.broadcasted_iota(jnp.int32, (LEV, LANES), 0)


def spread_out(column):
    return jnp.broadcast_to(column, (LEV, LANES))


def pack_kernel(box, parent, win, edge, pad, extra, sem):
    rows = parent.shape[0]
    cols = parent.shape[2]
    side = 3 * LANES
    sec = section()
    tile = tile_number()
    copy = pltpu.make_async_copy(parent, pad.at[:, :, pl.ds(side, cols)], sem)
    copy.start()
    pad[:, :, 0:side] = jnp.zeros((rows, 24, side), F32)
    pad[:, :, side + cols :] = jnp.zeros((rows, 24, side), F32)
    lane = lane_ids()
    level = level_ids()
    copy.wait()

    for which in range(2):
        at = side if which == 0 else side + cols - 1
        base, off = at // LANES * LANES, at % LANES
        for f in range(3):
            total = jnp.zeros((LEV, LANES), F32)
            for r in range(rows):
                piece = pad[r, pl.ds(8 * f, 8), pl.ds(base, LANES)]
                total = jnp.where(lane == r, spread_out(piece[:, off : off + 1]), total)
            edge[which, pl.ds(8 * f, 8), :] = total

    for order in range(4):
        nest = (order % 2) * 2 + order // 2
        ox = box[nest, 0]
        oy = box[nest, 1]
        start = jnp.clip(oy - cols * sec - 1, -side, cols + LANES - 1) + side
        block = start // LANES
        shift = start - block * LANES + 1
        back = (LANES - shift) % LANES

        def window(r, f):
            parts = []
            for q in range(3):
                piece = pad[r, pl.ds(8 * f, 8), pl.ds(pl.multiple_of((block + q) * LANES, LANES), LANES)]
                parts.append(pltpu.roll(piece, back, 1))
            inner = jnp.where(lane + shift < LANES, parts[0], parts[1])
            right = jnp.where(shift < LANES, parts[1][:, 0:1], parts[2][:, 0:1])
            return inner, parts[0][:, LANES - 1 : LANES], right

        def slot(k, carry):
            packed = jnp.zeros((LEV, LANES), F32)
            for par in range(2):
                r = 2 * k + par
                foot = rows * tile + r - ox
                keep = jnp.where((foot >= 0) & (foot < 256), 1.0, 0.0).astype(F32)
                for f in range(3):
                    inner, left, right = window(r, f)
                    win[order, k, pl.ds(24 * par + 8 * f, 8), :] = inner * keep
                    place = 12 * level + 4 * f + 2 * par
                    packed = jnp.where(lane == place, spread_out(left) * keep, packed)
                    packed = jnp.where(lane == place + 1, spread_out(right) * keep, packed)
            line = jnp.sum(packed, axis=0, keepdims=True)
            win[order, k, 48:56, :] = jnp.where(level == 6, jnp.broadcast_to(line, (LEV, LANES)), 0.0)
            return carry

        lax.fori_loop(0, rows // 2, slot, 0)

        for e, row in enumerate((ox - 1 - rows * tile, ox + 256 - rows * tile)):
            inside = (row >= 0) & (row < rows)
            keep = jnp.where(inside, 1.0, 0.0).astype(F32)
            r = jnp.clip(row, 0, rows - 1)
            for f in range(3):
                inner, _, _ = window(r, f)
                extra[pl.ds(24 * e + 8 * f, 8), :] = inner * keep
        for k in range(8):
            win[order, k, 48:54, :] = extra[6 * k : 6 * k + 6, :]


def move_kernel(box, win, edge, nest, parent, slots, low, high, rowhalo, colhalo, near, comb, gathered, summed, ready, sends,
                sem_s, sem_r, sem1_s, sem1_r, semz_s, semz_r, sem2_s, sem2_r):
    yl, co, tx, th, tz = (lax.axis_index(a) for a in ("yl", "co", "tx", "th", "tz"))
    mine = tx * 2 + th
    sec = yl * 2 + co
    tile = tx * 16 + th * 8 + tz
    here = dict(yl=yl, co=co, tx=tx, th=th, tz=tz)

    def tile_at(t):
        return dict(here, tx=t // 16, th=(t // 8) % 2, tz=t % 8)

    def sec_at(s):
        return dict(here, yl=s // 2, co=s % 2)

    core = dict(here, co=1 - co)
    following, before = tile_at((tile + 1) % 64), tile_at((tile + 63) % 64)
    east, west = sec_at((sec + 1) % 4), sec_at((sec + 3) % 4)
    cross = [
        (dict(here, tx=(tx + dx) % 4, th=(th + dh) % 2, yl=(yl + dl) % 2), dx, dh, dl)
        for dx, dh, dl in itertools.product((2, 1, 3, 0), (1, 0), (1, 0))
        if (dx, dh, dl) != (0, 0, 0)
    ]
    ring = [dict(here, tz=(tz + dz) % 8) for dz in (4, 3, 5, 2, 6, 1, 7)]
    greet = [core, following, before, east, west] + [c[0] for c in cross] + ring
    barrier = pltpu.get_barrier_semaphore()
    for device in greet:
        pl.semaphore_signal(barrier, inc=1, device_id=device, device_id_type=MESH)
    pl.semaphore_wait(barrier, len(greet))

    def send(src, dst, s, r, device):
        copy = pltpu.make_async_remote_copy(src_ref=src, dst_ref=dst, send_sem=s, recv_sem=r, device_id=device, device_id_type=MESH)
        copy.start()
        return copy

    first = send(win.at[pl.ds((1 - co) * 2, 2)], near, sem_s.at[0], sem_r.at[0], core)
    rows = nest.shape[1]
    last = parent.shape[0] - 1
    halos = [
        send(edge.at[1], colhalo.at[0], sem_s.at[1], sem_r.at[1], east),
        send(edge.at[0], colhalo.at[1], sem_s.at[2], sem_r.at[2], west),
        send(nest.at[0, pl.ds(rows - NSTEP, NSTEP)], low, sem_s.at[3], sem_r.at[3], following),
        send(nest.at[0, pl.ds(0, NSTEP)], high, sem_s.at[4], sem_r.at[4], before),
        send(parent.at[last], rowhalo.at[0], sem_s.at[5], sem_r.at[5], following),
        send(parent.at[0], rowhalo.at[1], sem_s.at[6], sem_r.at[6], before),
    ]
    first.wait()

    def combine(k, carry):
        for l in range(2):
            comb[l, k] = win[co * 2 + l, k] + near[l, k]
        return carry

    lax.fori_loop(0, 8, combine, 0)

    copies = []
    for j, (device, dx, dh, dl) in enumerate(cross):
        to = device["tx"] * 2 + device["th"]
        copies.append(send(comb.at[device["yl"], to], gathered.at[tx, yl, th], sem1_s.at[j], sem1_r.at[j], device))
    gathered[tx, yl, th] = comb[yl, mine]
    for copy in copies:
        copy.wait()
    for h in range(2):
        total = gathered[0, 0, h]
        for x, l in itertools.product(range(4), range(2)):
            if (x, l) != (0, 0):
                total = total + gathered[x, l, h]
        summed[tz, h] = total

    copies = [send(summed.at[tz], summed.at[tz], semz_s.at[j], semz_r.at[j], device) for j, device in enumerate(ring)]
    for copy in copies:
        copy.wait()

    lines = summed[0, 0, 48:56, :]
    for z, h in itertools.product(range(8), range(2)):
        if (z, h) != (0, 0):
            lines = lines + summed[z, h, 48:56, :]
    lines = jnp.where(level_ids() < 6, lines, 0.0)
    ox = box[sec, 0]

    def pick(device, where, slot):
        t = device["tx"] * 16 + device["th"] * 8 + tz
        q = ((ox + 4 * t + 254) % 256) // 2
        q = (q + (mine - q + 128) % 8) % 128
        z, h = (q // 8) % 8, q // 64
        where[slot, 0:48, :] = summed[z, h, 0:48, :]
        tail = summed[z, h, 48:56, :]
        where[slot, 48:56, :] = jnp.where(level_ids() < 6, lines, tail)

    copies = []
    j = 0
    for device, dx, dh, dl in cross:
        if dl == 0:
            pick(device, sends, j)
            copies.append(send(sends.at[j], ready.at[mine], sem2_s.at[j], sem2_r.at[j], device))
            j += 1
    pick(here, ready, mine)
    for copy in copies:
        copy.wait()
    for copy in halos:
        copy.wait()
    slots[...] = ready[...]


def fill_coefs(coef, diffusion, wind, conversion, mix):
    level = level_ids()

    def column(read):
        out = jnp.zeros((LEV, LANES), F32)
        for l in range(LEV):
            out = jnp.where(level == l, read(l), out)
        return out

    for f in range(3):
        d = column(lambda l: diffusion[8 * f + l])
        wx = column(lambda l: wind[0, 8 * f + l])
        wy = column(lambda l: wind[1, 8 * f + l])
        coef[f, 0] = 1.0 - 4.0 * d - wx - wy
        coef[f, 1] = d + wx
        coef[f, 2] = d
        coef[f, 3] = d + wy
        m = mix[f] * jnp.ones((LEV, LANES), F32)
        lower = jnp.where(level > 0, -m, 0.0)
        upper = jnp.where(level < LEV - 1, -m, 0.0)
        diag = 1.0 + m * jnp.where((level == 0) | (level == LEV - 1), 1.0, 2.0)
        item = 7
        for s in (1, 2, 4):
            alpha = -lower / pltpu.roll(diag, s, 0)
            gamma = -upper / pltpu.roll(diag, LEV - s, 0)
            new_diag = diag + alpha * pltpu.roll(upper, s, 0) + gamma * pltpu.roll(lower, LEV - s, 0)
            lower, upper = alpha * pltpu.roll(lower, s, 0), gamma * pltpu.roll(upper, LEV - s, 0)
            diag = new_diag
            if s < 4:
                coef[f, item] = alpha
                coef[f, item + 1] = gamma
                item += 2
            else:
                coef[f, item] = 1.0 / diag
                coef[f, item + 1] = (alpha + gamma) / diag
    c0 = column(lambda l: conversion[0, l])
    c1 = column(lambda l: conversion[1, l])
    coef[0, 4] = c0
    coef[0, 5] = 1.0 - c0
    coef[1, 4] = c1
    coef[1, 5] = 1.0 - c1


def solve(coef, f, r):
    r = r + coef[f, 7] * pltpu.roll(r, 1, 0) + coef[f, 8] * pltpu.roll(r, 7, 0)
    r = r + coef[f, 9] * pltpu.roll(r, 2, 0) + coef[f, 10] * pltpu.roll(r, 6, 0)
    return coef[f, 11] * r + coef[f, 12] * pltpu.roll(r, 4, 0)


def physics(coef, vapour, cloud, rain):
    wet = cloud + coef[0, 4] * vapour
    fields = (coef[0, 5] * vapour, coef[1, 5] * wet, rain + coef[1, 4] * wet)
    return [solve(coef, f, fields[f]) for f in range(3)]


def advance(coef, count, north, center, south, first, last):
    lane = lane_ids()
    moved = [[None] * count for _ in range(3)]
    for f in range(3):
        tiles = [center(f, q) for q in range(count)]
        right = [pltpu.roll(t, 1, 1) for t in tiles]
        left = [pltpu.roll(t, LANES - 1, 1) for t in tiles]
        for q in range(count):
            west = jnp.where(lane == 0, first(f) if q == 0 else right[q - 1], right[q])
            east = jnp.where(lane == LANES - 1, last(f) if q == count - 1 else left[q + 1], left[q])
            moved[f][q] = (coef[f, 0] * tiles[q] + coef[f, 1] * north(f, q) + coef[f, 2] * (south(f, q) + east)
                           + coef[f, 3] * west)
    for q in range(count):
        yield q, physics(coef, moved[0][q], moved[1][q], moved[2][q])


def nest_kernel(box, diffusion, wind, conversion, mix, slots, nest, low, high, out, coef, extra, old, new, flat, wide, state_a, state_b,
                keep, pull):
    sec = section()
    t = tile_number()
    rows = nest.shape[1]
    lane = lane_ids()
    level = level_ids()
    ox, ex, ey = box[sec, 0], box[sec, 2], box[sec, 3]
    fill_coefs(coef, diffusion, wind, conversion, mix)

    for k in range(8):
        extra[6 * k : 6 * k + 6, :] = slots[k, 48:54, :]

    def place(j):
        residue = (ox + 4 * t + 254 + j) % 256
        return (residue // 2) % 8, residue % 2

    for j in range(9):
        k, par = place(j)
        for f in range(3):
            old[j, pl.ds(8 * f, 8), :] = slots[k, pl.ds(pl.multiple_of(24 * par + 8 * f, 8), 8), :]

    @pl.when(t == 0)
    def _():
        old[1] = extra[0:24, :]

    @pl.when(t == 63)
    def _():
        old[6] = extra[24:48, :]

    for j in range(1, 8):
        k, par = place(j)
        line = jnp.broadcast_to(slots[k, 54:55, :], (LEV, LANES))

        def outer(f, which):
            at = 12 * level + 4 * f + 2 * par + which
            return spread_out(jnp.sum(jnp.where(lane == at, line, 0.0), axis=1, keepdims=True))

        read = lambda i: lambda f, q: old[i, pl.ds(8 * f, 8), :]
        for q, done in advance(coef, 1, read(j - 1), read(j), read(j + 1), lambda f: outer(f, 0), lambda f: outer(f, 1)):
            for f in range(3):
                new[j - 1, pl.ds(8 * f, 8), :] = done[f]

    @pl.when(t == 63)
    def _():
        old[6] = old[5]
        new[5] = new[4]

    for j in range(7):
        flat[pl.ds(24 * j, 24), :] = old[j + 1]
        flat[pl.ds(168 + 24 * j, 24), :] = new[j]

    cells = lax.broadcasted_iota(jnp.int32, (LANES, 512), 0)
    targets = lax.broadcasted_iota(jnp.int32, (LANES, 512), 1)
    weight = (targets % 4).astype(F32) * 0.25
    low_cell = targets // 4
    high_cell = jnp.minimum(low_cell + 1, LANES - 1)
    mixer = (jnp.where(cells == low_cell, 1.0 - weight, 0.0) + jnp.where(cells == high_cell, weight, 0.0)).astype(jnp.bfloat16)
    part = flat[...]
    total = None
    for _ in range(3):
        rounded = part.astype(jnp.bfloat16)
        product = jnp.dot(rounded, mixer, preferred_element_type=F32)
        total = product if total is None else total + product
        part = part - rounded.astype(F32)
    wide[...] = total

    wide_rows = rows + 2 * NSTEP
    row_id = rows * t - NSTEP + lax.broadcasted_iota(jnp.int32, (wide_rows, 512), 0)
    col_id = lax.broadcasted_iota(jnp.int32, (wide_rows, 512), 1)
    live = jnp.where((row_id >= 0) & (row_id < ex) & (col_id < ey), 1.0, 0.0).astype(F32)
    distance = jnp.minimum(jnp.minimum(row_id, col_id), jnp.minimum(ex - 1 - row_id, ey - 1 - col_id))
    nudging = 0.1 + 0.4 * jnp.exp(jnp.maximum(distance, 0).astype(F32) * (-1.0 / 3.0))
    kept, pulled = live * (1.0 - nudging), live * nudging
    for i in range(wide_rows):
        keep[i] = jnp.broadcast_to(kept[i : i + 1, :], (LEV, 512))
        pull[i] = jnp.broadcast_to(pulled[i : i + 1, :], (LEV, 512))

    def begin(src, i, at):
        alive = jnp.where(
            (rows * t - NSTEP + at >= 0) & (rows * t - NSTEP + at < ex) & (lax.broadcasted_iota(jnp.int32, (24, 512), 1) < ey), 1.0, 0.0
        ).astype(F32)
        state_a[at] = src[i] * alive

    for i in range(NSTEP):
        begin(low, i, i)
        begin(high, i, rows + NSTEP + i)

    def middle(i, carry):
        begin(nest.at[0], i, NSTEP + i)
        return carry

    lax.fori_loop(0, rows, middle, 0)

    zero = jnp.zeros((LEV, LANES), F32)
    states = (state_a, state_b)
    for step in range(1, NSTEP + 1):
        src, dst = states[(step - 1) % 2], states[step % 2]
        share = step / NSTEP

        def one_row(i, carry):
            u = i // 4
            p = (i % 4).astype(F32) * 0.25
            read = lambda k: lambda f, q: src[k, pl.ds(8 * f, 8), pl.ds(LANES * q, LANES)]
            for q, done in advance(coef, 4, read(i - 1), read(i), read(i + 1), lambda f: zero, lambda f: zero):
                columns = pl.ds(LANES * q, LANES)
                k_row, p_row = keep[i, :, columns], pull[i, :, columns]
                for f in range(3):
                    def force(v):
                        first = wide[pl.ds(pl.multiple_of(24 * v + 8 * f, 8), 8), columns]
                        if step == NSTEP:
                            return wide[pl.ds(pl.multiple_of(168 + 24 * v + 8 * f, 8), 8), columns]
                        second = wide[pl.ds(pl.multiple_of(168 + 24 * v + 8 * f, 8), 8), columns]
                        return first + share * (second - first)

                    before, after = force(u), force(u + 1)
                    result = k_row * done[f] + p_row * (before + p * (after - before))
                    if step == NSTEP:
                        out[0, i - NSTEP, pl.ds(8 * f, 8), columns] = result
                    else:
                        dst[i, pl.ds(8 * f, 8), columns] = result
            return carry

        lax.fori_loop(step, wide_rows - step, one_row, 0)


def parent_kernel(diffusion, wind, conversion, mix, parent, rowhalo, colhalo, out, coef):
    sec = section()
    t = tile_number()
    rows = parent.shape[0]
    count = parent.shape[2] // LANES
    lane = lane_ids()
    fill_coefs(coef, diffusion, wind, conversion, mix)
    have_up = jnp.where(t > 0, 1.0, 0.0).astype(F32)
    have_down = jnp.where(t < 63, 1.0, 0.0).astype(F32)
    have_left = jnp.where(sec > 0, 1.0, 0.0).astype(F32)
    have_right = jnp.where(sec < 3, 1.0, 0.0).astype(F32)

    def inner(i):
        return lambda f, q: parent[i, pl.ds(8 * f, 8), pl.ds(LANES * q, LANES)]

    def outer(side, scale):
        return lambda f, q: rowhalo[side, pl.ds(8 * f, 8), pl.ds(LANES * q, LANES)] * scale

    def one_row(i, north, south):
        def edge(side, scale):
            return lambda f: spread_out(
                jnp.sum(jnp.where(lane == i, colhalo[side, pl.ds(8 * f, 8), :], 0.0), axis=1, keepdims=True) * scale)

        for q, done in advance(coef, count, north, inner(i), south, edge(0, have_left), edge(1, have_right)):
            for f in range(3):
                out[i, pl.ds(8 * f, 8), pl.ds(LANES * q, LANES)] = done[f]

    one_row(0, outer(0, have_up), inner(1))

    def middle(i, carry):
        one_row(i, inner(i - 1), inner(i + 1))
        return carry

    lax.fori_loop(1, rows - 1, middle, 0)
    one_row(rows - 1, inner(rows - 2), outer(1, have_down))


def body(parent_old, nest_state, diffusion, wind_speed, conversion, vert_mix, nest_box):
    rows, chan, cols = parent_old.shape
    shape = jax.ShapeDtypeStruct
    win, edge = pl.pallas_call(
        pack_kernel,
        out_shape=(shape((4, 8, SLOT, LANES), F32), shape((2, chan, LANES), F32)),
        in_specs=[smem(), anywhere()],
        out_specs=(vmem(), vmem()),
        scratch_shapes=[pltpu.VMEM((rows, chan, cols + 6 * LANES), F32), pltpu.VMEM((48, LANES), F32), pltpu.SemaphoreType.DMA(())],
        name="pack",
    )(nest_box, parent_old)
    dma = pltpu.SemaphoreType.DMA
    slots, low, high, rowhalo, colhalo = pl.pallas_call(
        move_kernel,
        out_shape=(
            shape((8, SLOT, LANES), F32),
            shape((NSTEP, chan, nest_state.shape[3]), F32),
            shape((NSTEP, chan, nest_state.shape[3]), F32),
            shape((2, chan, cols), F32),
            shape((2, chan, LANES), F32),
        ),
        in_specs=[smem(), vmem(), vmem(), anywhere(), anywhere()],
        out_specs=(vmem(), anywhere(), anywhere(), anywhere(), anywhere()),
        scratch_shapes=[
            pltpu.VMEM((2, 8, SLOT, LANES), F32),
            pltpu.VMEM((2, 8, SLOT, LANES), F32),
            pltpu.VMEM((4, 2, 2, SLOT, LANES), F32),
            pltpu.VMEM((8, 2, SLOT, LANES), F32),
            pltpu.VMEM((8, SLOT, LANES), F32),
            pltpu.VMEM((7, SLOT, LANES), F32),
            dma((7,)), dma((7,)), dma((15,)), dma((15,)), dma((7,)), dma((7,)), dma((7,)), dma((7,)),
        ],
        compiler_params=pltpu.CompilerParams(collective_id=0, has_side_effects=True),
        name="move",
    )(nest_box, win, edge, nest_state, parent_old)
    nest_new = pl.pallas_call(
        nest_kernel,
        out_shape=shape(nest_state.shape, F32),
        in_specs=[smem()] * 5 + [vmem()] * 4,
        out_specs=vmem(),
        scratch_shapes=[
            pltpu.VMEM((3, 13, LEV, LANES), F32),
            pltpu.VMEM((48, LANES), F32),
            pltpu.VMEM((9, chan, LANES), F32),
            pltpu.VMEM((7, chan, LANES), F32),
            pltpu.VMEM((14 * chan, LANES), F32),
            pltpu.VMEM((14 * chan, 512), F32),
            pltpu.VMEM((24, chan, 512), F32),
            pltpu.VMEM((24, chan, 512), F32),
            pltpu.VMEM((24, LEV, 512), F32),
            pltpu.VMEM((24, LEV, 512), F32),
        ],
        name="nest",
    )(nest_box, diffusion, wind_speed, conversion, vert_mix, slots, nest_state, low, high)
    parent_new = pl.pallas_call(
        parent_kernel,
        out_shape=shape(parent_old.shape, F32),
        in_specs=[smem()] * 4 + [vmem()] * 3,
        out_specs=vmem(),
        scratch_shapes=[pltpu.VMEM((3, 13, LEV, LANES), F32)],
        name="parent",
    )(diffusion, wind_speed, conversion, vert_mix, parent_old, rowhalo, colhalo)
    return parent_new, nest_new


def solution(mesh):
    grid = Mesh(mesh.devices.reshape(2, 2, 4, 2, 8), SEC + TILE)
    in_specs = (P(TILE, None, SEC), P(SEC, TILE, None, None), P(), P(), P(), P(), P())
    out_specs = (P(TILE, None, SEC), P(SEC, TILE, None, None))
    return jax.shard_map(body, mesh=grid, in_specs=in_specs, out_specs=out_specs, check_vma=False)
```

```python
import itertools

import jax
import jax.numpy as jnp
from jax import lax
from jax.experimental import pallas as pl
from jax.experimental.pallas import tpu as pltpu
from jax.sharding import Mesh
from jax.sharding import PartitionSpec as P

NSTEP = 4
LEV = 8
SEC = ("yl", "co")
TILE = ("tx", "th", "tz")
LANES = 128
SLOT = 56
MESH = pl.DeviceIdType.MESH
F32 = jnp.float32


def vmem():
    return pl.BlockSpec(memory_space=pltpu.VMEM)


def smem():
    return pl.BlockSpec(memory_space=pltpu.SMEM)


def anywhere():
    return pl.BlockSpec(memory_space=pl.ANY)


def section():
    return lax.axis_index("yl") * 2 + lax.axis_index("co")


def tile_number():
    return lax.axis_index("tx") * 16 + lax.axis_index("th") * 8 + lax.axis_index("tz")


def lane_ids():
    return lax.broadcasted_iota(jnp.int32, (LEV, LANES), 1)


def level_ids():
    return lax.broadcasted_iota(jnp.int32, (LEV, LANES), 0)


def spread_out(column):
    return jnp.broadcast_to(column, (LEV, LANES))


def pack_edges(pad, edge, rows, cols):
    lane = lane_ids()
    for which in range(2):
        at = 0 if which == 0 else cols - 1
        base, off = at // LANES * LANES, at % LANES
        for f in range(3):
            total = jnp.zeros((LEV, LANES), F32)
            for r in range(rows):
                piece = pad[r, pl.ds(8 * f, 8), pl.ds(base, LANES)]
                total = jnp.where(lane == r, spread_out(piece[:, off : off + 1]), total)
            edge[which, pl.ds(8 * f, 8), :] = total


def split_parent(pad, thirds, rows, width):
    def split(k, carry):
        part = pad[pl.ds(2 * k, 2), :, :].reshape(48, width)
        for i in range(3):
            rounded = part.astype(jnp.bfloat16)
            thirds[i, pl.ds(pl.multiple_of(48 * k, 48), 48), :] = rounded
            part = part - rounded.astype(F32)
        return carry

    lax.fori_loop(0, rows // 2, split, 0)


def pack_nest(order, box, thirds, picked, extra, win, rows, cols):
    lane = lane_ids()
    level = level_ids()
    tile = tile_number()
    nest = (order % 2) * 2 + order // 2
    ox = box[nest, 0]
    oy = box[nest, 1]
    from_col = lax.broadcasted_iota(jnp.int32, (cols, 2 * LANES), 0)
    to_col = lax.broadcasted_iota(jnp.int32, (cols, 2 * LANES), 1)
    offset = jnp.where(to_col < LANES, to_col, jnp.where(to_col % 2 == 0, -1, LANES))
    choice = jnp.where(from_col == offset + (oy - cols * section()), 1.0, 0.0).astype(jnp.bfloat16)
    total = None
    for i in range(3):
        product = jnp.dot(thirds[i], choice, preferred_element_type=F32)
        total = product if total is None else total + product
    picked[...] = total.reshape(rows, 24, 2 * LANES)

    for k in range(rows // 2):
        packed = jnp.zeros((LEV, LANES), F32)
        for par in range(2):
            r = 2 * k + par
            foot = rows * tile + r - ox
            keep = jnp.where((foot >= 0) & (foot < 256), 1.0, 0.0).astype(F32)
            for f in range(3):
                win[order, k, pl.ds(24 * par + 8 * f, 8), :] = picked[r, pl.ds(8 * f, 8), 0:LANES] * keep
                here = lane // 2 == 6 * level + 2 * f + par
                packed = jnp.where(here, picked[r, pl.ds(8 * f, 8), LANES : 2 * LANES] * keep, packed)
        line = jnp.sum(packed, axis=0, keepdims=True)
        win[order, k, 48:56, :] = jnp.where(level == 6, jnp.broadcast_to(line, (LEV, LANES)), 0.0)

    for e, row in enumerate((ox - 1 - rows * tile, ox + 256 - rows * tile)):
        for f in range(3):
            total = jnp.zeros((LEV, LANES), F32)
            for r in range(rows):
                total = total + picked[r, pl.ds(8 * f, 8), 0:LANES] * jnp.where(row == r, 1.0, 0.0).astype(F32)
            extra[pl.ds(24 * e + 8 * f, 8), :] = total
    for k in range(8):
        win[order, k, 48:54, :] = extra[6 * k : 6 * k + 6, :]


def move_kernel(box, diffusion, wind, conversion, mix, nest, parent, slots, low, high, parent_out, win, edge, near, comb, gathered,
                summed, ready, sends, rowhalo, colhalo, pad, thirds, picked, extra, coef, result, sem_s, sem_r, sem1_s, sem1_r, semz_s, semz_r,
                sem2_s, sem2_r, sem_l):
    yl, co, tx, th, tz = (lax.axis_index(a) for a in ("yl", "co", "tx", "th", "tz"))
    mine = tx * 2 + th
    sec = yl * 2 + co
    tile = tx * 16 + th * 8 + tz
    here = dict(yl=yl, co=co, tx=tx, th=th, tz=tz)
    rows, chan, cols = parent.shape

    def tile_at(t):
        return dict(here, tx=t // 16, th=(t // 8) % 2, tz=t % 8)

    def sec_at(s):
        return dict(here, yl=s // 2, co=s % 2)

    core = dict(here, co=1 - co)
    following, before = tile_at((tile + 1) % 64), tile_at((tile + 63) % 64)
    east, west = sec_at((sec + 1) % 4), sec_at((sec + 3) % 4)
    cross = [
        (dict(here, tx=(tx + dx) % 4, th=(th + dh) % 2, yl=(yl + dl) % 2), dx, dh, dl)
        for dx, dh, dl in itertools.product((2, 1, 3, 0), (1, 0), (1, 0))
        if (dx, dh, dl) != (0, 0, 0)
    ]
    ring = [dict(here, tz=(tz + dz) % 8) for dz in (4, 3, 5, 2, 6, 1, 7)]
    greet = [core, following, before, east, west] + [c[0] for c in cross] + ring
    barrier = pltpu.get_barrier_semaphore()
    load = pltpu.make_async_copy(parent, pad, sem_l.at[0])
    load.start()
    for device in greet:
        pl.semaphore_signal(barrier, inc=1, device_id=device, device_id_type=MESH)

    load.wait()
    split_parent(pad, thirds, rows, cols)
    pack_edges(pad, edge, rows, cols)

    def pack(order, carry):
        pack_nest(order, box, thirds, picked, extra, win, rows, cols)
        return carry

    lax.fori_loop(0, 4, pack, 0)
    pl.semaphore_wait(barrier, len(greet))

    def make(src, dst, s, r, device):
        return pltpu.make_async_remote_copy(src_ref=src, dst_ref=dst, send_sem=s, recv_sem=r, device_id=device, device_id_type=MESH)

    def send(*parts):
        copy = make(*parts)
        copy.start()
        return copy

    first = send(win.at[pl.ds((1 - co) * 2, 2)], near, sem_s.at[0], sem_r.at[0], core)
    columns = [
        send(edge.at[1], colhalo.at[0], sem_s.at[1], sem_r.at[1], east),
        send(edge.at[0], colhalo.at[1], sem_s.at[2], sem_r.at[2], west),
    ]
    span = nest.shape[1]
    onward = [
        make(parent.at[rows - 1], rowhalo.at[0], sem_s.at[5], sem_r.at[5], following),
        make(nest.at[0, pl.ds(span - NSTEP, NSTEP)], low, sem_s.at[3], sem_r.at[3], following),
    ]
    backward = [
        make(parent.at[0], rowhalo.at[1], sem_s.at[6], sem_r.at[6], before),
        make(nest.at[0, pl.ds(0, NSTEP)], high, sem_s.at[4], sem_r.at[4], before),
    ]

    def start(copies, where):
        @pl.when(where)
        def _():
            for copy in copies:
                copy.start()

    start(onward, tz != 7)
    start(backward, tz != 0)
    fill_coefs(coef, diffusion, wind, conversion, mix)
    first.wait()

    def combine(k, carry):
        for l in range(2):
            comb[l, k] = win[co * 2 + l, k] + near[l, k]
        return carry

    lax.fori_loop(0, 8, combine, 0)

    copies = []
    for j, (device, dx, dh, dl) in enumerate(cross):
        to = device["tx"] * 2 + device["th"]
        copies.append(send(comb.at[device["yl"], to], gathered.at[tx, yl, th], sem1_s.at[j], sem1_r.at[j], device))
    gathered[tx, yl, th] = comb[yl, mine]

    have = [jnp.where(c, 1.0, 0.0).astype(F32) for c in (tile > 0, tile < 63, sec > 0, sec < 3)]
    lane = lane_ids()
    count = cols // LANES

    def inner(i):
        return lambda f, q: pad[i, pl.ds(8 * f, 8), pl.ds(LANES * q, LANES)]

    def outer(which):
        return lambda f, q: rowhalo[which, pl.ds(8 * f, 8), pl.ds(LANES * q, LANES)] * have[which]

    def one_row(i, north, south):
        def rim(which):
            return lambda f: spread_out(
                jnp.sum(jnp.where(lane == i, colhalo[which, pl.ds(8 * f, 8), :], 0.0), axis=1, keepdims=True) * have[2 + which])

        for q, done in advance(coef, count, north, inner(i), south, rim(0), rim(1)):
            for f in range(3):
                result[i, pl.ds(8 * f, 8), pl.ds(LANES * q, LANES)] = done[f]

    def middle(i, carry):
        one_row(i, inner(i - 1), inner(i + 1))
        return carry

    for copy in columns:
        copy.wait()
    lax.fori_loop(1, rows - 1, middle, 0)

    for copy in copies:
        copy.wait()
    for h in range(2):
        total = gathered[0, 0, h]
        for x, l in itertools.product(range(4), range(2)):
            if (x, l) != (0, 0):
                total = total + gathered[x, l, h]
        summed[tz, h] = total

    copies = [send(summed.at[tz], summed.at[tz], semz_s.at[j], semz_r.at[j], device) for j, device in enumerate(ring)]
    start(onward, tz == 7)
    start(backward, tz == 0)
    onward[0].wait()
    backward[0].wait()
    one_row(0, outer(0), inner(1))
    one_row(rows - 1, inner(rows - 2), outer(1))
    store = pltpu.make_async_copy(result, parent_out, sem_l.at[1])
    store.start()
    for copy in copies:
        copy.wait()

    lines = summed[0, 0, 48:56, :]
    for z, h in itertools.product(range(8), range(2)):
        if (z, h) != (0, 0):
            lines = lines + summed[z, h, 48:56, :]
    lines = jnp.where(level_ids() < 6, lines, 0.0)
    ox = box[sec, 0]

    def pick(device, where, slot):
        t = device["tx"] * 16 + device["th"] * 8 + tz
        q = ((ox + 4 * t + 254) % 256) // 2
        q = (q + (mine - q + 128) % 8) % 128
        z, h = (q // 8) % 8, q // 64
        where[slot, 0:48, :] = summed[z, h, 0:48, :]
        tail = summed[z, h, 48:56, :]
        where[slot, 48:56, :] = jnp.where(level_ids() < 6, lines, tail)

    copies = []
    j = 0
    for device, dx, dh, dl in cross:
        if dl == 0:
            pick(device, sends, j)
            copies.append(send(sends.at[j], ready.at[mine], sem2_s.at[j], sem2_r.at[j], device))
            j += 1
    pick(here, ready, mine)
    onward[1].wait()
    backward[1].wait()
    store.wait()
    for copy in copies:
        copy.wait()
    slots[...] = ready[...]


def fill_coefs(coef, diffusion, wind, conversion, mix):
    level = level_ids()

    def column(read):
        out = jnp.zeros((LEV, LANES), F32)
        for l in range(LEV):
            out = jnp.where(level == l, read(l), out)
        return out

    for f in range(3):
        d = column(lambda l: diffusion[8 * f + l])
        wx = column(lambda l: wind[0, 8 * f + l])
        wy = column(lambda l: wind[1, 8 * f + l])
        coef[f, 0] = 1.0 - 4.0 * d - wx - wy
        coef[f, 1] = d + wx
        coef[f, 2] = d
        coef[f, 3] = d + wy
        m = mix[f] * jnp.ones((LEV, LANES), F32)
        lower = jnp.where(level > 0, -m, 0.0)
        upper = jnp.where(level < LEV - 1, -m, 0.0)
        diag = 1.0 + m * jnp.where((level == 0) | (level == LEV - 1), 1.0, 2.0)
        item = 7
        for s in (1, 2, 4):
            alpha = -lower / pltpu.roll(diag, s, 0)
            gamma = -upper / pltpu.roll(diag, LEV - s, 0)
            new_diag = diag + alpha * pltpu.roll(upper, s, 0) + gamma * pltpu.roll(lower, LEV - s, 0)
            lower, upper = alpha * pltpu.roll(lower, s, 0), gamma * pltpu.roll(upper, LEV - s, 0)
            diag = new_diag
            if s < 4:
                coef[f, item] = alpha
                coef[f, item + 1] = gamma
                item += 2
            else:
                coef[f, item] = 1.0 / diag
                coef[f, item + 1] = (alpha + gamma) / diag
    c0 = column(lambda l: conversion[0, l])
    c1 = column(lambda l: conversion[1, l])
    coef[0, 4] = c0
    coef[0, 5] = 1.0 - c0
    coef[1, 4] = c1
    coef[1, 5] = 1.0 - c1


def solve(coef, f, r):
    r = r + coef[f, 7] * pltpu.roll(r, 1, 0) + coef[f, 8] * pltpu.roll(r, 7, 0)
    r = r + coef[f, 9] * pltpu.roll(r, 2, 0) + coef[f, 10] * pltpu.roll(r, 6, 0)
    return coef[f, 11] * r + coef[f, 12] * pltpu.roll(r, 4, 0)


def physics(coef, vapour, cloud, rain):
    wet = cloud + coef[0, 4] * vapour
    fields = (coef[0, 5] * vapour, coef[1, 5] * wet, rain + coef[1, 4] * wet)
    return [solve(coef, f, fields[f]) for f in range(3)]


def advance(coef, count, north, center, south, first, last):
    lane = lane_ids()
    tile, right, left = {}, {}, {}

    def read(f, q):
        if (f, q) not in tile:
            tile[f, q] = center(f, q)
            right[f, q] = pltpu.roll(tile[f, q], 1, 1)
            left[f, q] = pltpu.roll(tile[f, q], LANES - 1, 1)

    for q in range(count):
        moved = []
        for f in range(3):
            read(f, q)
            if q + 1 < count:
                read(f, q + 1)
            west = jnp.where(lane == 0, first(f) if q == 0 else right[f, q - 1], right[f, q])
            east = jnp.where(lane == LANES - 1, last(f) if q == count - 1 else left[f, q + 1], left[f, q])
            moved.append(coef[f, 0] * tile[f, q] + coef[f, 1] * north(f, q) + coef[f, 2] * (south(f, q) + east) + coef[f, 3] * west)
        yield q, physics(coef, *moved)


def nest_kernel(box, diffusion, wind, conversion, mix, slots, nest, low, high, parent_step, out, parent_out, coef, extra, old, new, flat,
                wide, state_a, state_b, keep, pull, passed, sem):
    take = pltpu.make_async_copy(parent_step, passed, sem.at[0])
    give = pltpu.make_async_copy(passed, parent_out, sem.at[1])
    take.start()
    sec = section()
    t = tile_number()
    rows = nest.shape[1]
    lane = lane_ids()
    level = level_ids()
    ox, ex, ey = box[sec, 0], box[sec, 2], box[sec, 3]
    fill_coefs(coef, diffusion, wind, conversion, mix)

    for k in range(8):
        extra[6 * k : 6 * k + 6, :] = slots[k, 48:54, :]

    def place(j):
        residue = (ox + 4 * t + 254 + j) % 256
        return (residue // 2) % 8, residue % 2

    for j in range(9):
        k, par = place(j)
        for f in range(3):
            old[j, pl.ds(8 * f, 8), :] = slots[k, pl.ds(pl.multiple_of(24 * par + 8 * f, 8), 8), :]

    @pl.when(t == 0)
    def _():
        old[1] = extra[0:24, :]

    @pl.when(t == 63)
    def _():
        old[6] = extra[24:48, :]

    for j in range(1, 8):
        k, par = place(j)
        line = jnp.broadcast_to(slots[k, 54:55, :], (LEV, LANES))

        def outer(f, which):
            at = 12 * level + 4 * f + 2 * par + which
            return spread_out(jnp.sum(jnp.where(lane == at, line, 0.0), axis=1, keepdims=True))

        read = lambda i: lambda f, q: old[i, pl.ds(8 * f, 8), :]
        for q, done in advance(coef, 1, read(j - 1), read(j), read(j + 1), lambda f: outer(f, 0), lambda f: outer(f, 1)):
            for f in range(3):
                new[j - 1, pl.ds(8 * f, 8), :] = done[f]

    @pl.when(t == 63)
    def _():
        old[6] = old[5]
        new[5] = new[4]

    for j in range(7):
        flat[pl.ds(24 * j, 24), :] = old[j + 1]
        flat[pl.ds(168 + 24 * j, 24), :] = new[j]

    cells = lax.broadcasted_iota(jnp.int32, (LANES, 512), 0)
    targets = lax.broadcasted_iota(jnp.int32, (LANES, 512), 1)
    weight = (targets % 4).astype(F32) * 0.25
    low_cell = targets // 4
    high_cell = jnp.minimum(low_cell + 1, LANES - 1)
    mixer = (jnp.where(cells == low_cell, 1.0 - weight, 0.0) + jnp.where(cells == high_cell, weight, 0.0)).astype(jnp.bfloat16)
    part = flat[...]
    total = None
    for _ in range(3):
        rounded = part.astype(jnp.bfloat16)
        product = jnp.dot(rounded, mixer, preferred_element_type=F32)
        total = product if total is None else total + product
        part = part - rounded.astype(F32)
    wide[...] = total
    take.wait()
    give.start()

    wide_rows = rows + 2 * NSTEP
    row_id = rows * t - NSTEP + lax.broadcasted_iota(jnp.int32, (wide_rows, 512), 0)
    col_id = lax.broadcasted_iota(jnp.int32, (wide_rows, 512), 1)
    live = jnp.where((row_id >= 0) & (row_id < ex) & (col_id < ey), 1.0, 0.0).astype(F32)
    distance = jnp.minimum(jnp.minimum(row_id, col_id), jnp.minimum(ex - 1 - row_id, ey - 1 - col_id))
    nudging = 0.1 + 0.4 * jnp.exp(jnp.maximum(distance, 0).astype(F32) * (-1.0 / 3.0))
    kept, pulled = live * (1.0 - nudging), live * nudging
    for i in range(wide_rows):
        keep[i] = jnp.broadcast_to(kept[i : i + 1, :], (LEV, 512))
        pull[i] = jnp.broadcast_to(pulled[i : i + 1, :], (LEV, 512))

    def begin(src, i, at):
        alive = jnp.where(
            (rows * t - NSTEP + at >= 0) & (rows * t - NSTEP + at < ex) & (lax.broadcasted_iota(jnp.int32, (24, 512), 1) < ey), 1.0, 0.0
        ).astype(F32)
        state_a[at] = src[i] * alive

    for i in range(NSTEP):
        begin(low, i, i)
        begin(high, i, rows + NSTEP + i)

    def middle(i, carry):
        begin(nest.at[0], i, NSTEP + i)
        return carry

    lax.fori_loop(0, rows, middle, 0)

    zero = jnp.zeros((LEV, LANES), F32)
    states = (state_a, state_b)
    for step in range(1, NSTEP + 1):
        src, dst = states[(step - 1) % 2], states[step % 2]
        share = step / NSTEP

        def one_row(i, carry):
            u = i // 4
            p = (i % 4).astype(F32) * 0.25
            read = lambda k: lambda f, q: src[k, pl.ds(8 * f, 8), pl.ds(LANES * q, LANES)]
            for q, done in advance(coef, 4, read(i - 1), read(i), read(i + 1), lambda f: zero, lambda f: zero):
                columns = pl.ds(LANES * q, LANES)
                k_row, p_row = keep[i, :, columns], pull[i, :, columns]
                for f in range(3):
                    def force(v):
                        first = wide[pl.ds(pl.multiple_of(24 * v + 8 * f, 8), 8), columns]
                        if step == NSTEP:
                            return wide[pl.ds(pl.multiple_of(168 + 24 * v + 8 * f, 8), 8), columns]
                        second = wide[pl.ds(pl.multiple_of(168 + 24 * v + 8 * f, 8), 8), columns]
                        return first + share * (second - first)

                    before, after = force(u), force(u + 1)
                    result = k_row * done[f] + p_row * (before + p * (after - before))
                    if step == NSTEP:
                        out[0, i - NSTEP, pl.ds(8 * f, 8), columns] = result
                    else:
                        dst[i, pl.ds(8 * f, 8), columns] = result
            return carry

        lax.fori_loop(step, wide_rows - step, one_row, 0)
    give.wait()


def body(parent_old, nest_state, diffusion, wind_speed, conversion, vert_mix, nest_box):
    rows, chan, cols = parent_old.shape
    shape = jax.ShapeDtypeStruct
    dma = pltpu.SemaphoreType.DMA
    slots, low, high, parent_step = pl.pallas_call(
        move_kernel,
        out_shape=(
            shape((8, SLOT, LANES), F32),
            shape((NSTEP, chan, nest_state.shape[3]), F32),
            shape((NSTEP, chan, nest_state.shape[3]), F32),
            shape(parent_old.shape, F32),
        ),
        in_specs=[smem()] * 5 + [anywhere()] * 2,
        out_specs=(vmem(), anywhere(), anywhere(), anywhere()),
        scratch_shapes=[
            pltpu.VMEM((4, 8, SLOT, LANES), F32),
            pltpu.VMEM((2, chan, LANES), F32),
            pltpu.VMEM((2, 8, SLOT, LANES), F32),
            pltpu.VMEM((2, 8, SLOT, LANES), F32),
            pltpu.VMEM((4, 2, 2, SLOT, LANES), F32),
            pltpu.VMEM((8, 2, SLOT, LANES), F32),
            pltpu.VMEM((8, SLOT, LANES), F32),
            pltpu.VMEM((7, SLOT, LANES), F32),
            pltpu.VMEM((2, chan, cols), F32),
            pltpu.VMEM((2, chan, LANES), F32),
            pltpu.VMEM((rows, chan, cols), F32),
            pltpu.VMEM((3, rows * chan, cols), jnp.bfloat16),
            pltpu.VMEM((rows, chan, 2 * LANES), F32),
            pltpu.VMEM((48, LANES), F32),
            pltpu.VMEM((3, 13, LEV, LANES), F32),
            pltpu.VMEM((rows, chan, cols), F32),
            dma((7,)), dma((7,)), dma((15,)), dma((15,)), dma((7,)), dma((7,)), dma((7,)), dma((7,)), dma((2,)),
        ],
        compiler_params=pltpu.CompilerParams(collective_id=0, has_side_effects=True),
        name="move",
    )(nest_box, diffusion, wind_speed, conversion, vert_mix, nest_state, parent_old)
    nest_new, parent_new = pl.pallas_call(
        nest_kernel,
        out_shape=(shape(nest_state.shape, F32), shape(parent_old.shape, F32)),
        in_specs=[smem()] * 5 + [vmem()] * 4 + [anywhere()],
        out_specs=(vmem(), anywhere()),
        scratch_shapes=[
            pltpu.VMEM((3, 13, LEV, LANES), F32),
            pltpu.VMEM((48, LANES), F32),
            pltpu.VMEM((9, chan, LANES), F32),
            pltpu.VMEM((7, chan, LANES), F32),
            pltpu.VMEM((14 * chan, LANES), F32),
            pltpu.VMEM((14 * chan, 512), F32),
            pltpu.VMEM((24, chan, 512), F32),
            pltpu.VMEM((24, chan, 512), F32),
            pltpu.VMEM((24, LEV, 512), F32),
            pltpu.VMEM((24, LEV, 512), F32),
            pltpu.VMEM((rows, chan, cols), F32),
            dma((2,)),
        ],
        name="nest",
    )(nest_box, diffusion, wind_speed, conversion, vert_mix, slots, nest_state, low, high, parent_step)
    return parent_new, nest_new


def solution(mesh):
    grid = Mesh(mesh.devices.reshape(2, 2, 4, 2, 8), SEC + TILE)
    in_specs = (P(TILE, None, SEC), P(SEC, TILE, None, None), P(), P(), P(), P(), P())
    out_specs = (P(TILE, None, SEC), P(SEC, TILE, None, None))
    return jax.shard_map(body, mesh=grid, in_specs=in_specs, out_specs=out_specs, check_vma=False)
```

```python
import itertools

import jax
import jax.numpy as jnp
from jax import lax
from jax.experimental import pallas as pl
from jax.experimental.pallas import tpu as pltpu
from jax.sharding import Mesh
from jax.sharding import PartitionSpec as P

NSTEP = 4
LEV = 8
SEC = ("yl", "co")
TILE = ("tx", "th", "tz")
LANES = 128
SLOT = (7, 8, 128)
APRON = 2
MESH = pl.DeviceIdType.MESH
F32 = jnp.float32


def vmem():
    return pl.BlockSpec(memory_space=pltpu.VMEM)


def smem():
    return pl.BlockSpec(memory_space=pltpu.SMEM)


def anywhere():
    return pl.BlockSpec(memory_space=pl.ANY)


def section():
    return lax.axis_index("yl") * 2 + lax.axis_index("co")


def tile_number():
    return lax.axis_index("tx") * 16 + lax.axis_index("th") * 8 + lax.axis_index("tz")


def lane_ids():
    return lax.broadcasted_iota(jnp.int32, (LEV, LANES), 1)


def level_ids():
    return lax.broadcasted_iota(jnp.int32, (LEV, LANES), 0)


def spread_out(column):
    return jnp.broadcast_to(column, (LEV, LANES))


def pack_edges(pad, edge, rows, count):
    lane = lane_ids()
    for which in range(2):
        block, off = (APRON, 0) if which == 0 else (APRON + count - 1, LANES - 1)
        for f in range(3):
            total = jnp.zeros((LEV, LANES), F32)
            for r in range(rows):
                piece = pad[block, r, pl.ds(8 * f, 8), :]
                total = jnp.where(lane == r, spread_out(piece[:, off : off + 1]), total)
            edge[which, pl.ds(8 * f, 8), :] = total


def pack_nest(order, box, pad, extra, win, rows, cols):
    lane = lane_ids()
    level = level_ids()
    tile = tile_number()
    nest = (order % 2) * 2 + order // 2
    ox = box[nest, 0]
    oy = box[nest, 1]
    start = jnp.clip(oy - cols * section() - 1, -APRON * LANES, cols) + APRON * LANES
    block = start // LANES
    shift = start - block * LANES + 1

    back = (LANES - shift) % LANES

    def turned(piece):
        return pltpu.roll(piece, back, 1)

    def window(r, f):
        near = turned(pad[block, r, pl.ds(8 * f, 8), :])
        next_piece = pad[block + 1, r, pl.ds(8 * f, 8), :]
        far = turned(next_piece)
        return jnp.where(lane + shift < LANES, near, far), near, far

    for k in range(rows // 2):
        packed = jnp.zeros((LEV, LANES), F32)
        for par in range(2):
            r = 2 * k + par
            foot = rows * tile + r - ox
            keep = jnp.where((foot >= 0) & (foot < 256), 1.0, 0.0).astype(F32)
            for f in range(3):
                inner, near, far = window(r, f)
                win[order, k, 3 * par + f] = inner * keep
                far = jnp.where(shift < LANES, far, pad[block + 2, r, pl.ds(8 * f, 8), :])
                pair = jnp.where(lane % 2 == 0, spread_out(near[:, LANES - 1 : LANES]), spread_out(far[:, 0:1]))
                packed = jnp.where(lane // 2 == 6 * level + 2 * f + par, pair * keep, packed)
        line = jnp.sum(packed, axis=0, keepdims=True)
        win[order, k, 6] = jnp.where(level == 6, jnp.broadcast_to(line, (LEV, LANES)), 0.0)

    for e, row in enumerate((ox - 1 - rows * tile, ox + 256 - rows * tile)):
        keep = jnp.where((row >= 0) & (row < rows), 1.0, 0.0).astype(F32)
        r = jnp.clip(row, 0, rows - 1)
        for f in range(3):
            extra[pl.ds(24 * e + 8 * f, 8), :] = window(r, f)[0] * keep
    for k in range(8):
        win[order, k, 6, 0:6, :] = extra[6 * k : 6 * k + 6, :]


def step_kernel(box, diffusion, wind, conversion, mix, nest, parent, parent_out, nest_out, win, edge, near, comb, gathered, summed,
                ready, sends, rowhalo, colhalo, pad, extra, coef, result, own, low, high, state_a, state_b, keep, pull, mixer, old, new,
                flat, wide, base, drift, sem_s, sem_r, sem1_s, sem1_r, semz_s, semz_r, sem2_s, sem2_r, sem_p, sem_l):
    yl, co, tx, th, tz = (lax.axis_index(a) for a in ("yl", "co", "tx", "th", "tz"))
    mine = tx * 2 + th
    sec = yl * 2 + co
    tile = tx * 16 + th * 8 + tz
    here = dict(yl=yl, co=co, tx=tx, th=th, tz=tz)
    rows, chan, cols = parent.shape
    count = cols // LANES
    span, width = nest.shape[1], nest.shape[3]
    tall = span + 2 * NSTEP
    lane = lane_ids()
    level = level_ids()

    def tile_at(t):
        return dict(here, tx=t // 16, th=(t // 8) % 2, tz=t % 8)

    def sec_at(s):
        return dict(here, yl=s // 2, co=s % 2)

    core = dict(here, co=1 - co)
    following, before = tile_at((tile + 1) % 64), tile_at((tile + 63) % 64)
    east, west = sec_at((sec + 1) % 4), sec_at((sec + 3) % 4)
    cross = [
        (dict(here, tx=(tx + dx) % 4, th=(th + dh) % 2, yl=(yl + dl) % 2), dx, dh, dl)
        for dx, dh, dl in itertools.product((2, 1, 3, 0), (1, 0), (1, 0))
        if (dx, dh, dl) != (0, 0, 0)
    ]
    ring = [dict(here, tz=(tz + dz) % 8) for dz in (4, 3, 5, 2, 6, 1, 7)]
    greet = [core, following, before, east, west] + [c[0] for c in cross] + ring
    barrier = pltpu.get_barrier_semaphore()
    loads = [
        pltpu.make_async_copy(parent.at[:, :, pl.ds(LANES * q, LANES)], pad.at[APRON + q], sem_p.at[q]) for q in range(count)
    ]
    for copy in loads:
        copy.start()
    load_own = pltpu.make_async_copy(nest.at[0], own, sem_l.at[0])
    load_own.start()
    for device in greet:
        pl.semaphore_signal(barrier, inc=1, device_id=device, device_id_type=MESH)

    def empty(i, carry):
        for q in (0, 1, APRON + count, APRON + count + 1, APRON + count + 2):
            pad[q, i] = jnp.zeros((chan, LANES), F32)
        return carry

    lax.fori_loop(0, rows, empty, 0)
    for copy in loads:
        copy.wait()

    def pack(order, carry):
        pack_nest(order, box, pad, extra, win, rows, cols)
        return carry

    lax.fori_loop(0, 4, pack, 0)
    pl.semaphore_wait(barrier, len(greet))

    def make(src, dst, s, r, device):
        return pltpu.make_async_remote_copy(src_ref=src, dst_ref=dst, send_sem=s, recv_sem=r, device_id=device, device_id_type=MESH)

    def send(*parts):
        copy = make(*parts)
        copy.start()
        return copy

    first = send(win.at[pl.ds((1 - co) * 2, 2)], near, sem_s.at[0], sem_r.at[0], core)
    onward = [
        make(parent.at[rows - 1], rowhalo.at[0], sem_s.at[5], sem_r.at[5], following),
        make(nest.at[0, pl.ds(span - NSTEP, NSTEP)], low, sem_s.at[3], sem_r.at[3], following),
    ]
    backward = [
        make(parent.at[0], rowhalo.at[1], sem_s.at[6], sem_r.at[6], before),
        make(nest.at[0, pl.ds(0, NSTEP)], high, sem_s.at[4], sem_r.at[4], before),
    ]

    def start(copies, where):
        @pl.when(where)
        def _():
            for copy in copies:
                copy.start()

    start(onward, tz != 7)
    start(backward, tz != 0)
    pack_edges(pad, edge, rows, count)
    columns = [
        send(edge.at[1], colhalo.at[0], sem_s.at[1], sem_r.at[1], east),
        send(edge.at[0], colhalo.at[1], sem_s.at[2], sem_r.at[2], west),
    ]
    fill_coefs(coef, diffusion, wind, conversion, mix)
    first.wait()

    def combine(k, carry):
        for l in range(2):
            comb[l, k] = win[co * 2 + l, k] + near[l, k]
        return carry

    lax.fori_loop(0, 8, combine, 0)

    copies = []
    for j, (device, dx, dh, dl) in enumerate(cross):
        to = device["tx"] * 2 + device["th"]
        copies.append(send(comb.at[device["yl"], to], gathered.at[tx, yl, th], sem1_s.at[j], sem1_r.at[j], device))
    gathered[tx, yl, th] = comb[yl, mine]

    have = [jnp.where(c, 1.0, 0.0).astype(F32) for c in (tile > 0, tile < 63, sec > 0, sec < 3)]

    def inner(i):
        return lambda f, q: pad[APRON + q, i, pl.ds(8 * f, 8), :]

    def outer(which):
        return lambda f, q: rowhalo[which, pl.ds(8 * f, 8), pl.ds(LANES * q, LANES)] * have[which]

    def parent_row(i, north, south):
        def rim(which):
            return lambda f: spread_out(
                jnp.sum(jnp.where(lane == i, colhalo[which, pl.ds(8 * f, 8), :], 0.0), axis=1, keepdims=True) * have[2 + which])

        for q, done in advance(coef, count, north, inner(i), south, rim(0), rim(1)):
            for f in range(3):
                result[i, pl.ds(8 * f, 8), pl.ds(LANES * q, LANES)] = done[f]

    def parent_rows(i, carry):
        parent_row(i, inner(i - 1), inner(i + 1))
        return carry

    for copy in columns:
        copy.wait()
    lax.fori_loop(1, rows - 1, parent_rows, 0)

    ox, ex, ey = box[sec, 0], box[sec, 2], box[sec, 3]
    row_id = span * tile - NSTEP + lax.broadcasted_iota(jnp.int32, (tall, width), 0)
    col_id = lax.broadcasted_iota(jnp.int32, (tall, width), 1)
    live = jnp.where((row_id >= 0) & (row_id < ex) & (col_id < ey), 1.0, 0.0).astype(F32)
    distance = jnp.minimum(jnp.minimum(row_id, col_id), jnp.minimum(ex - 1 - row_id, ey - 1 - col_id))
    nudging = 0.1 + 0.4 * jnp.exp(jnp.maximum(distance, 0).astype(F32) * (-1.0 / 3.0))
    kept, pulled = live * (1.0 - nudging), live * nudging
    for i in range(tall):
        keep[i] = jnp.broadcast_to(kept[i : i + 1, :], (LEV, width))
        pull[i] = jnp.broadcast_to(pulled[i : i + 1, :], (LEV, width))

    def begin(src, i, at):
        number = span * tile - NSTEP + at
        alive = jnp.where((number >= 0) & (number < ex) & (lax.broadcasted_iota(jnp.int32, (chan, width), 1) < ey), 1.0, 0.0)
        state_a[at] = src[i] * alive.astype(F32)

    def begin_own(i, carry):
        begin(own, i, NSTEP + i)
        return carry

    load_own.wait()
    lax.fori_loop(0, span, begin_own, 0)
    zero = jnp.zeros((LEV, LANES), F32)
    blocks = width // LANES

    def nest_row(src, i):
        read = lambda k: lambda f, q: src[k, pl.ds(8 * f, 8), pl.ds(LANES * q, LANES)]
        yield from advance(coef, blocks, read(i - 1), read(i), read(i + 1), lambda f: zero, lambda f: zero)

    def first_row(i):
        for q, done in nest_row(state_a, i):
            for f in range(3):
                state_b[i, pl.ds(8 * f, 8), pl.ds(LANES * q, LANES)] = done[f]

    def first_rows(first):
        def pair(m, carry):
            first_row(first + 2 * m)
            first_row(first + 2 * m + 1)
            return carry

        return pair

    lax.fori_loop(0, span // 2 - 1, first_rows(NSTEP + 1), 0)

    cells = lax.broadcasted_iota(jnp.int32, (LANES, width), 0)
    targets = lax.broadcasted_iota(jnp.int32, (LANES, width), 1)
    weight = (targets % 4).astype(F32) * 0.25
    low_cell = targets // 4
    high_cell = jnp.minimum(low_cell + 1, LANES - 1)
    mixed = (jnp.where(cells == low_cell, 1.0 - weight, 0.0) + jnp.where(cells == high_cell, weight, 0.0)).astype(jnp.bfloat16)
    for i in range(3):
        mixer[LANES * i : LANES * (i + 1), :] = mixed

    for copy in copies:
        copy.wait()
    for h in range(2):
        total = gathered[0, 0, h]
        for x, l in itertools.product(range(4), range(2)):
            if (x, l) != (0, 0):
                total = total + gathered[x, l, h]
        summed[tz, h] = total

    copies = [send(summed.at[tz], summed.at[tz], semz_s.at[j], semz_r.at[j], device) for j, device in enumerate(ring)]
    start(onward, tz == 7)
    start(backward, tz == 0)

    onward[0].wait()
    backward[0].wait()
    parent_row(0, outer(0), inner(1))
    parent_row(rows - 1, inner(rows - 2), outer(1))
    store = pltpu.make_async_copy(result, parent_out, sem_l.at[1])
    store.start()
    onward[1].wait()
    backward[1].wait()
    for i in range(NSTEP):
        begin(low, i, i)
        begin(high, i, span + NSTEP + i)
    lax.fori_loop(0, 2, first_rows(1), 0)
    lax.fori_loop(0, 2, first_rows(span + NSTEP - 1), 0)
    for copy in copies:
        copy.wait()

    lines = summed[0, 0, 6]
    for z, h in itertools.product(range(8), range(2)):
        if (z, h) != (0, 0):
            lines = lines + summed[z, h, 6]

    def pick(device, where, slot):
        t = device["tx"] * 16 + device["th"] * 8 + tz
        q = ((ox + 4 * t + 254) % 256) // 2
        q = (q + (mine - q + 128) % 8) % 128
        z, h = (q // 8) % 8, q // 64
        where[slot, 0:6] = summed[z, h, 0:6]
        where[slot, 6] = jnp.where(level < 6, lines, summed[z, h, 6])

    copies = []
    j = 0
    for device, dx, dh, dl in cross:
        if dl == 0:
            pick(device, sends, j)
            copies.append(send(sends.at[j], ready.at[mine], sem2_s.at[j], sem2_r.at[j], device))
            j += 1
    pick(here, ready, mine)
    store.wait()
    for copy in copies:
        copy.wait()

    for k in range(8):
        extra[6 * k : 6 * k + 6, :] = ready[k, 6, 0:6, :]

    def place(j):
        residue = (ox + 4 * tile + 254 + j) % 256
        return (residue // 2) % 8, residue % 2

    for j in range(9):
        k, par = place(j)
        for f in range(3):
            old[j, pl.ds(8 * f, 8), :] = ready[k, 3 * par + f]

    @pl.when(tile == 0)
    def _():
        old[1] = extra[0:24, :]

    @pl.when(tile == 63)
    def _():
        old[6] = extra[24:48, :]

    for j in range(1, 8):
        k, par = place(j)
        line = jnp.broadcast_to(ready[k, 6][6:7, :], (LEV, LANES))

        def beyond(which):
            def column(f):
                at = 12 * level + 4 * f + 2 * par + which
                return spread_out(jnp.sum(jnp.where(lane == at, line, 0.0), axis=1, keepdims=True))

            return column

        read = lambda i: lambda f, q: old[i, pl.ds(8 * f, 8), :]
        for q, done in advance(coef, 1, read(j - 1), read(j), read(j + 1), beyond(0), beyond(1)):
            for f in range(3):
                new[j - 1, pl.ds(8 * f, 8), :] = done[f]

    @pl.when(tile == 63)
    def _():
        old[6] = old[5]
        new[5] = new[4]

    for j in range(7):
        part = jnp.concatenate([old[j + 1], (new[j] - old[j + 1]) * (1.0 / NSTEP)], axis=0)
        for i in range(3):
            rounded = part.astype(jnp.bfloat16)
            flat[pl.ds(48 * j, 48), LANES * i : LANES * (i + 1)] = rounded
            part = part - rounded.astype(F32)
    wide[...] = jnp.dot(flat[...], mixer[...], preferred_element_type=F32).reshape(7, 2 * chan, width)

    def pulls(u, carry):
        for q in range(blocks):
            columns = pl.ds(LANES * q, LANES)
            for f in range(3):
                at, to = pl.ds(8 * f, 8), pl.ds(chan + 8 * f, 8)
                from_old, from_change = wide[u, at, columns], wide[u, to, columns]
                over_old, over_change = wide[u + 1, at, columns] - from_old, wide[u + 1, to, columns] - from_change
                for p in range(4):
                    i = 4 * u + p
                    p_row = pull[i, :, columns]
                    now, change = (from_old, from_change) if p == 0 else (from_old + 0.25 * p * over_old, from_change + 0.25 * p * over_change)
                    now, change = p_row * now, p_row * change
                    base[i, at, columns] = now
                    drift[i, at, columns] = change
                    state_b[i, at, columns] = keep[i, :, columns] * state_b[i, at, columns] + (now + change)
        return carry

    state_b[0] = jnp.zeros((chan, width), F32)
    state_b[tall - 1] = jnp.zeros((chan, width), F32)
    lax.fori_loop(0, tall // 4, pulls, 0)

    def step_pairs(src, dst, step, first):
        def pair(m, carry):
            for i in (first + 2 * m, first + 2 * m + 1):
                for q, done in nest_row(src, i):
                    columns = pl.ds(LANES * q, LANES)
                    k_row = keep[i, :, columns]
                    for f in range(3):
                        at = pl.ds(8 * f, 8)
                        dst[i, at, columns] = k_row * done[f] + (base[i, at, columns] + float(step) * drift[i, at, columns])
            return carry

        return pair

    lax.fori_loop(0, (tall - 4) // 2, step_pairs(state_b, state_a, 2, 2), 0)
    lax.fori_loop(0, (tall - 6) // 2, step_pairs(state_a, state_b, 3, 3), 0)
    half = span // 2
    parts = []
    for part in range(2):
        lax.fori_loop(0, half // 2, step_pairs(state_b, state_a, 4, NSTEP + half * part), 0)
        parts.append(pltpu.make_async_copy(state_a.at[pl.ds(NSTEP + half * part, half)], nest_out.at[0, pl.ds(half * part, half)], sem_l.at[2 + part]))
        parts[-1].start()
    for copy in parts:
        copy.wait()


def fill_coefs(coef, diffusion, wind, conversion, mix):
    level = level_ids()

    def column(read):
        out = jnp.zeros((LEV, LANES), F32)
        for l in range(LEV):
            out = jnp.where(level == l, read(l), out)
        return out

    for f in range(3):
        d = column(lambda l: diffusion[8 * f + l])
        wx = column(lambda l: wind[0, 8 * f + l])
        wy = column(lambda l: wind[1, 8 * f + l])
        coef[f, 0] = 1.0 - 4.0 * d - wx - wy
        coef[f, 1] = d + wx
        coef[f, 2] = d
        coef[f, 3] = d + wy
        m = mix[f] * jnp.ones((LEV, LANES), F32)
        lower = jnp.where(level > 0, -m, 0.0)
        upper = jnp.where(level < LEV - 1, -m, 0.0)
        diag = 1.0 + m * jnp.where((level == 0) | (level == LEV - 1), 1.0, 2.0)
        item = 7
        for s in (1, 2, 4):
            alpha = -lower / pltpu.roll(diag, s, 0)
            gamma = -upper / pltpu.roll(diag, LEV - s, 0)
            new_diag = diag + alpha * pltpu.roll(upper, s, 0) + gamma * pltpu.roll(lower, LEV - s, 0)
            lower, upper = alpha * pltpu.roll(lower, s, 0), gamma * pltpu.roll(upper, LEV - s, 0)
            diag = new_diag
            if s < 4:
                coef[f, item] = alpha
                coef[f, item + 1] = gamma
                item += 2
            else:
                coef[f, item] = 1.0 / diag
                coef[f, item + 1] = (alpha + gamma) / diag
    c0 = column(lambda l: conversion[0, l])
    c1 = column(lambda l: conversion[1, l])
    coef[0, 4] = c0
    coef[0, 5] = 1.0 - c0
    coef[1, 4] = c1
    coef[1, 5] = 1.0 - c1


def solve(coef, f, r):
    r = r + coef[f, 7] * pltpu.roll(r, 1, 0) + coef[f, 8] * pltpu.roll(r, 7, 0)
    r = r + coef[f, 9] * pltpu.roll(r, 2, 0) + coef[f, 10] * pltpu.roll(r, 6, 0)
    return coef[f, 11] * r + coef[f, 12] * pltpu.roll(r, 4, 0)


def physics(coef, vapour, cloud, rain):
    wet = cloud + coef[0, 4] * vapour
    fields = (coef[0, 5] * vapour, coef[1, 5] * wet, rain + coef[1, 4] * wet)
    return [solve(coef, f, fields[f]) for f in range(3)]


def advance(coef, count, north, center, south, first, last):
    lane = lane_ids()
    tile, right, left = {}, {}, {}

    def read(f, q):
        if (f, q) not in tile:
            tile[f, q] = center(f, q)
            right[f, q] = pltpu.roll(tile[f, q], 1, 1)
            left[f, q] = pltpu.roll(tile[f, q], LANES - 1, 1)

    for q in range(count):
        moved = []
        for f in range(3):
            read(f, q)
            if q + 1 < count:
                read(f, q + 1)
            west = jnp.where(lane == 0, first(f) if q == 0 else right[f, q - 1], right[f, q])
            east = jnp.where(lane == LANES - 1, last(f) if q == count - 1 else left[f, q + 1], left[f, q])
            moved.append(coef[f, 0] * tile[f, q] + coef[f, 1] * north(f, q) + coef[f, 2] * (south(f, q) + east) + coef[f, 3] * west)
        yield q, physics(coef, *moved)


def body(parent_old, nest_state, diffusion, wind_speed, conversion, vert_mix, nest_box):
    rows, chan, cols = parent_old.shape
    span, width = nest_state.shape[1], nest_state.shape[3]
    tall = span + 2 * NSTEP
    shape = jax.ShapeDtypeStruct
    dma = pltpu.SemaphoreType.DMA

    def room(*dims, kind=F32):
        return pltpu.VMEM(dims, kind)

    return pl.pallas_call(
        step_kernel,
        out_shape=(shape(parent_old.shape, F32), shape(nest_state.shape, F32)),
        in_specs=[smem()] * 5 + [anywhere()] * 2,
        out_specs=(anywhere(), anywhere()),
        scratch_shapes=[
            room(4, 8, *SLOT), room(2, chan, LANES), room(2, 8, *SLOT), room(2, 8, *SLOT), room(4, 2, 2, *SLOT), room(8, 2, *SLOT),
            room(8, *SLOT), room(7, *SLOT), room(2, chan, cols), room(2, chan, LANES),
            room(cols // LANES + 5, rows, chan, LANES), room(48, LANES), room(3, 13, LEV, LANES), room(rows, chan, cols),
            room(span, chan, width), room(NSTEP, chan, width), room(NSTEP, chan, width), room(tall, chan, width), room(tall, chan, width),
            room(tall, LEV, width), room(tall, LEV, width), room(3 * LANES, width, kind=jnp.bfloat16),
            room(9, chan, LANES), room(7, chan, LANES), room(14 * chan, 3 * LANES, kind=jnp.bfloat16), room(7, 2 * chan, width),
            room(tall, chan, width), room(tall, chan, width),
            dma((7,)), dma((7,)), dma((15,)), dma((15,)), dma((7,)), dma((7,)), dma((7,)), dma((7,)), dma((cols // LANES,)), dma((4,)),
        ],
        compiler_params=pltpu.CompilerParams(collective_id=0, has_side_effects=True),
        name="step",
    )(nest_box, diffusion, wind_speed, conversion, vert_mix, nest_state, parent_old)


def solution(mesh):
    grid = Mesh(mesh.devices.reshape(2, 2, 4, 2, 8), SEC + TILE)
    in_specs = (P(TILE, None, SEC), P(SEC, TILE, None, None), P(), P(), P(), P(), P())
    out_specs = (P(TILE, None, SEC), P(SEC, TILE, None, None))
    return jax.shard_map(body, mesh=grid, in_specs=in_specs, out_specs=out_specs, check_vma=False)
```

```python
import itertools

import jax
import jax.numpy as jnp
from jax import lax
from jax.experimental import pallas as pl
from jax.experimental.pallas import tpu as pltpu
from jax.sharding import Mesh
from jax.sharding import PartitionSpec as P

NSTEP = 4
LEV = 8
SEC = ("yl", "co")
TILE = ("tx", "th", "tz")
LANES = 128
SLOT = (7, 8, 128)
APRON = 2
MESH = pl.DeviceIdType.MESH
F32 = jnp.float32


def vmem():
    return pl.BlockSpec(memory_space=pltpu.VMEM)


def smem():
    return pl.BlockSpec(memory_space=pltpu.SMEM)


def anywhere():
    return pl.BlockSpec(memory_space=pl.ANY)


def section():
    return lax.axis_index("yl") * 2 + lax.axis_index("co")


def tile_number():
    return lax.axis_index("tx") * 16 + lax.axis_index("th") * 8 + lax.axis_index("tz")


def lane_ids():
    return lax.broadcasted_iota(jnp.int32, (LEV, LANES), 1)


def level_ids():
    return lax.broadcasted_iota(jnp.int32, (LEV, LANES), 0)


def spread_out(column):
    return jnp.broadcast_to(column, (LEV, LANES))


def pack_edges(pad, edge, rows, count):
    lane = lane_ids()
    for which in range(2):
        block, off = (APRON, 0) if which == 0 else (APRON + count - 1, LANES - 1)
        for f in range(3):
            total = jnp.zeros((LEV, LANES), F32)
            for r in range(rows):
                piece = pad[block, r, pl.ds(8 * f, 8), :]
                total = jnp.where(lane == r, spread_out(piece[:, off : off + 1]), total)
            edge[which, pl.ds(8 * f, 8), :] = total


def pack_nest(order, box, pad, extra, win, rows, cols):
    lane = lane_ids()
    level = level_ids()
    tile = tile_number()
    nest = (order % 2) * 2 + order // 2
    ox = box[nest, 0]
    oy = box[nest, 1]
    start = jnp.clip(oy - cols * section() - 1, -APRON * LANES, cols) + APRON * LANES
    block = start // LANES
    shift = start - block * LANES + 1

    back = (LANES - shift) % LANES

    def turned(piece):
        return pltpu.roll(piece, back, 1)

    def window(r, f):
        near = turned(pad[block, r, pl.ds(8 * f, 8), :])
        next_piece = pad[block + 1, r, pl.ds(8 * f, 8), :]
        far = turned(next_piece)
        return jnp.where(lane + shift < LANES, near, far), near, far

    for k in range(rows // 2):
        packed = jnp.zeros((LEV, LANES), F32)
        for par in range(2):
            r = 2 * k + par
            foot = rows * tile + r - ox
            keep = jnp.where((foot >= 0) & (foot < 256), 1.0, 0.0).astype(F32)
            for f in range(3):
                inner, near, far = window(r, f)
                win[order, k, 3 * par + f] = inner * keep
                far = jnp.where(shift < LANES, far, pad[block + 2, r, pl.ds(8 * f, 8), :])
                pair = jnp.where(lane % 2 == 0, spread_out(near[:, LANES - 1 : LANES]), spread_out(far[:, 0:1]))
                packed = jnp.where(lane // 2 == 6 * level + 2 * f + par, pair * keep, packed)
        line = jnp.sum(packed, axis=0, keepdims=True)
        win[order, k, 6] = jnp.where(level == 6, jnp.broadcast_to(line, (LEV, LANES)), 0.0)

    for e, row in enumerate((ox - 1 - rows * tile, ox + 256 - rows * tile)):
        keep = jnp.where((row >= 0) & (row < rows), 1.0, 0.0).astype(F32)
        r = jnp.clip(row, 0, rows - 1)
        for f in range(3):
            extra[pl.ds(24 * e + 8 * f, 8), :] = window(r, f)[0] * keep
    for k in range(8):
        win[order, k, 6, 0:6, :] = extra[6 * k : 6 * k + 6, :]


def step_kernel(box, diffusion, wind, conversion, mix, nest, parent, parent_out, slots_out, moved_out, keep_out, pull_out, mixer_out,
                coef_out, win, edge, near, comb, gathered, summed,
                ready, sends, rowhalo, colhalo, pad, extra, coef, result, own, low, high, state_a, state_b, keep, pull, mixer,
                sem_s, sem_r, sem1_s, sem1_r, semz_s, semz_r, sem2_s, sem2_r, sem_p, sem_l):
    yl, co, tx, th, tz = (lax.axis_index(a) for a in ("yl", "co", "tx", "th", "tz"))
    mine = tx * 2 + th
    sec = yl * 2 + co
    tile = tx * 16 + th * 8 + tz
    here = dict(yl=yl, co=co, tx=tx, th=th, tz=tz)
    rows, chan, cols = parent.shape
    count = cols // LANES
    span, width = nest.shape[1], nest.shape[3]
    tall = span + 2 * NSTEP
    lane = lane_ids()
    level = level_ids()

    def tile_at(t):
        return dict(here, tx=t // 16, th=(t // 8) % 2, tz=t % 8)

    def sec_at(s):
        return dict(here, yl=s // 2, co=s % 2)

    core = dict(here, co=1 - co)
    following, before = tile_at((tile + 1) % 64), tile_at((tile + 63) % 64)
    east, west = sec_at((sec + 1) % 4), sec_at((sec + 3) % 4)
    cross = [
        (dict(here, tx=(tx + dx) % 4, th=(th + dh) % 2, yl=(yl + dl) % 2), dx, dh, dl)
        for dx, dh, dl in itertools.product((2, 1, 3, 0), (1, 0), (1, 0))
        if (dx, dh, dl) != (0, 0, 0)
    ]
    ring = [dict(here, tz=(tz + dz) % 8) for dz in (4, 3, 5, 2, 6, 1, 7)]
    greet = [core, following, before, east, west] + [c[0] for c in cross] + ring
    barrier = pltpu.get_barrier_semaphore()
    loads = [
        pltpu.make_async_copy(parent.at[:, :, pl.ds(LANES * q, LANES)], pad.at[APRON + q], sem_p.at[q]) for q in range(count)
    ]
    for copy in loads:
        copy.start()
    load_own = pltpu.make_async_copy(nest.at[0], own, sem_l.at[0])
    load_own.start()
    for device in greet:
        pl.semaphore_signal(barrier, inc=1, device_id=device, device_id_type=MESH)

    def empty(i, carry):
        for q in (0, 1, APRON + count, APRON + count + 1, APRON + count + 2):
            pad[q, i] = jnp.zeros((chan, LANES), F32)
        return carry

    lax.fori_loop(0, rows, empty, 0)
    for copy in loads:
        copy.wait()

    def pack(order, carry):
        pack_nest(order, box, pad, extra, win, rows, cols)
        return carry

    lax.fori_loop((1 - co) * 2, (1 - co) * 2 + 2, pack, 0)
    pl.semaphore_wait(barrier, len(greet))

    def make(src, dst, s, r, device):
        return pltpu.make_async_remote_copy(src_ref=src, dst_ref=dst, send_sem=s, recv_sem=r, device_id=device, device_id_type=MESH)

    def send(*parts):
        copy = make(*parts)
        copy.start()
        return copy

    first = send(win.at[pl.ds((1 - co) * 2, 2)], near, sem_s.at[0], sem_r.at[0], core)
    onward = [
        make(parent.at[rows - 1], rowhalo.at[0], sem_s.at[5], sem_r.at[5], following),
        make(nest.at[0, pl.ds(span - NSTEP, NSTEP)], low, sem_s.at[3], sem_r.at[3], following),
    ]
    backward = [
        make(parent.at[0], rowhalo.at[1], sem_s.at[6], sem_r.at[6], before),
        make(nest.at[0, pl.ds(0, NSTEP)], high, sem_s.at[4], sem_r.at[4], before),
    ]

    for copy in onward + backward:
        copy.start()
    lax.fori_loop(co * 2, co * 2 + 2, pack, 0)
    pack_edges(pad, edge, rows, count)
    columns = [
        send(edge.at[1], colhalo.at[0], sem_s.at[1], sem_r.at[1], east),
        send(edge.at[0], colhalo.at[1], sem_s.at[2], sem_r.at[2], west),
    ]
    fill_coefs(coef, diffusion, wind, conversion, mix)
    first.wait()

    def combine(k, carry):
        for l in range(2):
            comb[l, k] = win[co * 2 + l, k] + near[l, k]
        return carry

    lax.fori_loop(0, 8, combine, 0)

    copies = []
    for j, (device, dx, dh, dl) in enumerate(cross):
        to = device["tx"] * 2 + device["th"]
        copies.append(send(comb.at[device["yl"], to], gathered.at[tx, yl, th], sem1_s.at[j], sem1_r.at[j], device))
    gathered[tx, yl, th] = comb[yl, mine]

    have = [jnp.where(c, 1.0, 0.0).astype(F32) for c in (tile > 0, tile < 63, sec > 0, sec < 3)]

    def inner(i):
        return lambda f, q: pad[APRON + q, i, pl.ds(8 * f, 8), :]

    def outer(which):
        return lambda f, q: rowhalo[which, pl.ds(8 * f, 8), pl.ds(LANES * q, LANES)] * have[which]

    def parent_row(i, north, south):
        def rim(which):
            return lambda f: spread_out(
                jnp.sum(jnp.where(lane == i, colhalo[which, pl.ds(8 * f, 8), :], 0.0), axis=1, keepdims=True) * have[2 + which])

        for q, done in advance(coef, count, north, inner(i), south, rim(0), rim(1)):
            for f in range(3):
                result[i, pl.ds(8 * f, 8), pl.ds(LANES * q, LANES)] = done[f]

    def parent_rows(i, carry):
        parent_row(i, inner(i - 1), inner(i + 1))
        return carry

    for copy in columns:
        copy.wait()
    lax.fori_loop(1, rows - 1, parent_rows, 0)

    ox, ex, ey = box[sec, 0], box[sec, 2], box[sec, 3]
    row_id = span * tile - NSTEP + lax.broadcasted_iota(jnp.int32, (tall, width), 0)
    col_id = lax.broadcasted_iota(jnp.int32, (tall, width), 1)
    live = jnp.where((row_id >= 0) & (row_id < ex) & (col_id < ey), 1.0, 0.0).astype(F32)
    distance = jnp.minimum(jnp.minimum(row_id, col_id), jnp.minimum(ex - 1 - row_id, ey - 1 - col_id))
    nudging = 0.1 + 0.4 * jnp.exp(jnp.maximum(distance, 0).astype(F32) * (-1.0 / 3.0))
    kept, pulled = live * (1.0 - nudging), live * nudging
    for i in range(tall):
        keep[i] = jnp.broadcast_to(kept[i : i + 1, :], (LEV, width))
        pull[i] = jnp.broadcast_to(pulled[i : i + 1, :], (LEV, width))

    def begin(src, i, at):
        number = span * tile - NSTEP + at
        alive = jnp.where((number >= 0) & (number < ex) & (lax.broadcasted_iota(jnp.int32, (chan, width), 1) < ey), 1.0, 0.0)
        state_a[at] = src[i] * alive.astype(F32)

    def begin_own(i, carry):
        begin(own, i, NSTEP + i)
        return carry

    load_own.wait()
    lax.fori_loop(0, span, begin_own, 0)

    def first_row(i):
        for q, done in nest_row(coef, state_a, i):
            for f in range(3):
                state_b[i, pl.ds(8 * f, 8), pl.ds(LANES * q, LANES)] = done[f]

    def first_rows(first):
        def pair(m, carry):
            first_row(first + 2 * m)
            first_row(first + 2 * m + 1)
            return carry

        return pair

    lax.fori_loop(0, span // 2 - 1, first_rows(NSTEP + 1), 0)

    cells = lax.broadcasted_iota(jnp.int32, (LANES, width), 0)
    targets = lax.broadcasted_iota(jnp.int32, (LANES, width), 1)
    weight = (targets % 4).astype(F32) * 0.25
    low_cell = targets // 4
    high_cell = jnp.minimum(low_cell + 1, LANES - 1)
    mixed = (jnp.where(cells == low_cell, 1.0 - weight, 0.0) + jnp.where(cells == high_cell, weight, 0.0)).astype(jnp.bfloat16)
    for i in range(3):
        mixer[LANES * i : LANES * (i + 1), :] = mixed

    for copy in copies:
        copy.wait()
    for h in range(2):
        total = gathered[0, 0, h]
        for x, l in itertools.product(range(4), range(2)):
            if (x, l) != (0, 0):
                total = total + gathered[x, l, h]
        summed[tz, h] = total

    copies = [send(summed.at[tz], summed.at[tz], semz_s.at[j], semz_r.at[j], device) for j, device in enumerate(ring)]
    out_moved, out_keep, out_pull = (
        pltpu.make_async_copy(src, dst, sem_l.at[i])
        for i, (src, dst) in enumerate(((state_b, moved_out), (keep, keep_out), (pull, pull_out)), 2)
    )
    out_keep.start()
    out_pull.start()
    out_mixer = pltpu.make_async_copy(mixer, mixer_out, sem_l.at[5])
    out_mixer.start()
    out_coef = pltpu.make_async_copy(coef, coef_out, sem_l.at[6])
    out_coef.start()
    for copy in copies:
        copy.wait()

    lines = summed[0, 0, 6]
    for z, h in itertools.product(range(8), range(2)):
        if (z, h) != (0, 0):
            lines = lines + summed[z, h, 6]

    def pick(device, where, slot):
        t = device["tx"] * 16 + device["th"] * 8 + tz
        q = ((ox + 4 * t + 254) % 256) // 2
        q = (q + (mine - q + 128) % 8) % 128
        z, h = (q // 8) % 8, q // 64
        where[slot, 0:6] = summed[z, h, 0:6]
        where[slot, 6] = jnp.where(level < 6, lines, summed[z, h, 6])

    copies = []
    j = 0
    for device, dx, dh, dl in cross:
        if dl == 0:
            pick(device, sends, j)
            copies.append(send(sends.at[j], ready.at[mine], sem2_s.at[j], sem2_r.at[j], device))
            j += 1
    pick(here, ready, mine)

    onward[0].wait()
    backward[0].wait()
    parent_row(0, outer(0), inner(1))
    parent_row(rows - 1, inner(rows - 2), outer(1))
    state_b[0] = jnp.zeros((chan, width), F32)
    state_b[tall - 1] = jnp.zeros((chan, width), F32)
    store = pltpu.make_async_copy(result, parent_out, sem_l.at[1])
    store.start()
    onward[1].wait()
    backward[1].wait()
    for i in range(NSTEP):
        begin(low, i, i)
        begin(high, i, span + NSTEP + i)
    lax.fori_loop(0, 2, first_rows(1), 0)
    lax.fori_loop(0, 2, first_rows(span + NSTEP - 1), 0)
    out_moved.start()
    for copy in (store, out_keep, out_pull, out_mixer, out_coef, out_moved):
        copy.wait()
    for copy in copies:
        copy.wait()
    finish = pltpu.make_async_copy(ready, slots_out, sem_l.at[7])
    finish.start()
    finish.wait()


def fill_coefs(coef, diffusion, wind, conversion, mix):
    level = level_ids()

    def column(read):
        out = jnp.zeros((LEV, LANES), F32)
        for l in range(LEV):
            out = jnp.where(level == l, read(l), out)
        return out

    for f in range(3):
        d = column(lambda l: diffusion[8 * f + l])
        wx = column(lambda l: wind[0, 8 * f + l])
        wy = column(lambda l: wind[1, 8 * f + l])
        coef[f, 0] = 1.0 - 4.0 * d - wx - wy
        coef[f, 1] = d + wx
        coef[f, 2] = d
        coef[f, 3] = d + wy
        m = mix[f] * jnp.ones((LEV, LANES), F32)
        lower = jnp.where(level > 0, -m, 0.0)
        upper = jnp.where(level < LEV - 1, -m, 0.0)
        diag = 1.0 + m * jnp.where((level == 0) | (level == LEV - 1), 1.0, 2.0)
        item = 7
        for s in (1, 2, 4):
            alpha = -lower / pltpu.roll(diag, s, 0)
            gamma = -upper / pltpu.roll(diag, LEV - s, 0)
            new_diag = diag + alpha * pltpu.roll(upper, s, 0) + gamma * pltpu.roll(lower, LEV - s, 0)
            lower, upper = alpha * pltpu.roll(lower, s, 0), gamma * pltpu.roll(upper, LEV - s, 0)
            diag = new_diag
            if s < 4:
                coef[f, item] = alpha
                coef[f, item + 1] = gamma
                item += 2
            else:
                coef[f, item] = 1.0 / diag
                coef[f, item + 1] = (alpha + gamma) / diag
    c0 = column(lambda l: conversion[0, l])
    c1 = column(lambda l: conversion[1, l])
    coef[0, 4] = c0
    coef[0, 5] = 1.0 - c0
    coef[1, 4] = c1
    coef[1, 5] = 1.0 - c1


def solve(coef, f, r):
    r = r + coef[f, 7] * pltpu.roll(r, 1, 0) + coef[f, 8] * pltpu.roll(r, 7, 0)
    r = r + coef[f, 9] * pltpu.roll(r, 2, 0) + coef[f, 10] * pltpu.roll(r, 6, 0)
    return coef[f, 11] * r + coef[f, 12] * pltpu.roll(r, 4, 0)


def physics(coef, vapour, cloud, rain):
    wet = cloud + coef[0, 4] * vapour
    fields = (coef[0, 5] * vapour, coef[1, 5] * wet, rain + coef[1, 4] * wet)
    return [solve(coef, f, fields[f]) for f in range(3)]


def advance(coef, count, north, center, south, first, last):
    lane = lane_ids()
    tile, right, left = {}, {}, {}

    def read(f, q):
        if (f, q) not in tile:
            tile[f, q] = center(f, q)
            right[f, q] = pltpu.roll(tile[f, q], 1, 1)
            left[f, q] = pltpu.roll(tile[f, q], LANES - 1, 1)

    for q in range(count):
        moved = []
        for f in range(3):
            read(f, q)
            if q + 1 < count:
                read(f, q + 1)
            west = jnp.where(lane == 0, first(f) if q == 0 else right[f, q - 1], right[f, q])
            east = jnp.where(lane == LANES - 1, last(f) if q == count - 1 else left[f, q + 1], left[f, q])
            moved.append(coef[f, 0] * tile[f, q] + coef[f, 1] * north(f, q) + coef[f, 2] * (south(f, q) + east) + coef[f, 3] * west)
        yield q, physics(coef, *moved)


def nest_row(coef, src, i):
    zero = jnp.zeros((LEV, LANES), F32)
    read = lambda k: lambda f, q: src[k, pl.ds(8 * f, 8), pl.ds(LANES * q, LANES)]
    yield from advance(coef, src.shape[2] // LANES, read(i - 1), read(i), read(i + 1), lambda f: zero, lambda f: zero)


def nest_kernel(box, slots, moved, keep_in, pull_in, mixer_in, coef_in, parent_step, nest_out, parent_out, ready, state_b, keep, pull,
                mixer, coef, state_a, passed, extra, old, new, flat, wide, base, drift, sem):
    first = [pltpu.make_async_copy(slots, ready, sem.at[0]), pltpu.make_async_copy(coef_in, coef, sem.at[1])]
    rest = [
        pltpu.make_async_copy(moved, state_b, sem.at[2]),
        pltpu.make_async_copy(keep_in, keep, sem.at[3]),
        pltpu.make_async_copy(pull_in, pull, sem.at[4]),
        pltpu.make_async_copy(mixer_in, mixer, sem.at[5]),
    ]
    take = pltpu.make_async_copy(parent_step, passed, sem.at[6])
    give = pltpu.make_async_copy(passed, parent_out, sem.at[7])
    for copy in first + rest[3:] + rest[:3] + [take]:
        copy.start()
    tile = tile_number()
    ox = box[section(), 0]
    tall, chan, width = state_a.shape
    span = tall - 2 * NSTEP
    blocks = width // LANES
    lane = lane_ids()
    level = level_ids()
    for copy in first:
        copy.wait()

    for k in range(8):
        extra[6 * k : 6 * k + 6, :] = ready[k, 6, 0:6, :]

    def place(j):
        residue = (ox + 4 * tile + 254 + j) % 256
        return (residue // 2) % 8, residue % 2

    for j in range(9):
        k, par = place(j)
        for f in range(3):
            old[j, pl.ds(8 * f, 8), :] = ready[k, 3 * par + f]

    @pl.when(tile == 0)
    def _():
        old[1] = extra[0:24, :]

    @pl.when(tile == 63)
    def _():
        old[6] = extra[24:48, :]

    for j in range(1, 8):
        k, par = place(j)
        line = jnp.broadcast_to(ready[k, 6][6:7, :], (LEV, LANES))

        def beyond(which):
            def column(f):
                at = 12 * level + 4 * f + 2 * par + which
                return spread_out(jnp.sum(jnp.where(lane == at, line, 0.0), axis=1, keepdims=True))

            return column

        read = lambda i: lambda f, q: old[i, pl.ds(8 * f, 8), :]
        for q, done in advance(coef, 1, read(j - 1), read(j), read(j + 1), beyond(0), beyond(1)):
            for f in range(3):
                new[j - 1, pl.ds(8 * f, 8), :] = done[f]

    @pl.when(tile == 63)
    def _():
        old[6] = old[5]
        new[5] = new[4]

    for j in range(7):
        part = jnp.concatenate([old[j + 1], (new[j] - old[j + 1]) * (1.0 / NSTEP)], axis=0)
        for i in range(3):
            rounded = part.astype(jnp.bfloat16)
            flat[pl.ds(48 * j, 48), LANES * i : LANES * (i + 1)] = rounded
            part = part - rounded.astype(F32)
    rest[3].wait()
    wide[...] = jnp.dot(flat[...], mixer[...], preferred_element_type=F32).reshape(7, 2 * chan, width)

    take.wait()
    give.start()

    def pulls(u, carry):
        for q in range(blocks):
            columns = pl.ds(LANES * q, LANES)
            for f in range(3):
                at, to = pl.ds(8 * f, 8), pl.ds(chan + 8 * f, 8)
                from_old, from_change = wide[u, at, columns], wide[u, to, columns]
                over_old, over_change = wide[u + 1, at, columns] - from_old, wide[u + 1, to, columns] - from_change
                for p in range(4):
                    i = 4 * u + p
                    p_row = pull[i, :, columns]
                    now, change = (from_old, from_change) if p == 0 else (from_old + 0.25 * p * over_old, from_change + 0.25 * p * over_change)
                    now, change = p_row * now, p_row * change
                    base[i, at, columns] = now
                    drift[i, at, columns] = change
                    state_b[i, at, columns] = keep[i, :, columns] * state_b[i, at, columns] + (now + change)
        return carry

    for copy in rest[:3]:
        copy.wait()
    lax.fori_loop(0, tall // 4, pulls, 0)

    def step_pairs(src, dst, step, first):
        def pair(m, carry):
            for i in (first + 2 * m, first + 2 * m + 1):
                for q, done in nest_row(coef, src, i):
                    columns = pl.ds(LANES * q, LANES)
                    k_row = keep[i, :, columns]
                    for f in range(3):
                        at = pl.ds(8 * f, 8)
                        dst[i, at, columns] = k_row * done[f] + (base[i, at, columns] + float(step) * drift[i, at, columns])
            return carry

        return pair

    lax.fori_loop(0, (tall - 4) // 2, step_pairs(state_b, state_a, 2, 2), 0)
    lax.fori_loop(0, (tall - 6) // 2, step_pairs(state_a, state_b, 3, 3), 0)
    half = span // 2
    parts = []
    for part in range(2):
        lax.fori_loop(0, half // 2, step_pairs(state_b, state_a, 4, NSTEP + half * part), 0)
        parts.append(pltpu.make_async_copy(state_a.at[pl.ds(NSTEP + half * part, half)], nest_out.at[0, pl.ds(half * part, half)], sem.at[8 + part]))
        parts[-1].start()
    for copy in parts:
        copy.wait()
    give.wait()


def body(parent_old, nest_state, diffusion, wind_speed, conversion, vert_mix, nest_box):
    rows, chan, cols = parent_old.shape
    span, width = nest_state.shape[1], nest_state.shape[3]
    tall = span + 2 * NSTEP
    shape = jax.ShapeDtypeStruct
    dma = pltpu.SemaphoreType.DMA

    def room(*dims, kind=F32):
        return pltpu.VMEM(dims, kind)

    parent_step, slots, moved, keep, pull, mixer, coef = pl.pallas_call(
        step_kernel,
        out_shape=(
            shape(parent_old.shape, F32), shape((8, *SLOT), F32), shape((tall, chan, width), F32), shape((tall, LEV, width), F32),
            shape((tall, LEV, width), F32), shape((3 * LANES, width), jnp.bfloat16), shape((3, 13, LEV, LANES), F32),
        ),
        in_specs=[smem()] * 5 + [anywhere()] * 2,
        out_specs=(anywhere(),) * 7,
        scratch_shapes=[
            room(4, 8, *SLOT), room(2, chan, LANES), room(2, 8, *SLOT), room(2, 8, *SLOT), room(4, 2, 2, *SLOT), room(8, 2, *SLOT),
            room(8, *SLOT), room(7, *SLOT), room(2, chan, cols), room(2, chan, LANES),
            room(cols // LANES + 5, rows, chan, LANES), room(48, LANES), room(3, 13, LEV, LANES), room(rows, chan, cols),
            room(span, chan, width), room(NSTEP, chan, width), room(NSTEP, chan, width), room(tall, chan, width), room(tall, chan, width),
            room(tall, LEV, width), room(tall, LEV, width), room(3 * LANES, width, kind=jnp.bfloat16),
            dma((7,)), dma((7,)), dma((15,)), dma((15,)), dma((7,)), dma((7,)), dma((7,)), dma((7,)), dma((cols // LANES,)), dma((8,)),
        ],
        compiler_params=pltpu.CompilerParams(collective_id=0, has_side_effects=True),
        name="step",
    )(nest_box, diffusion, wind_speed, conversion, vert_mix, nest_state, parent_old)
    nest_new, parent_new = pl.pallas_call(
        nest_kernel,
        out_shape=(shape(nest_state.shape, F32), shape(parent_old.shape, F32)),
        in_specs=[smem()] + [anywhere()] * 7,
        out_specs=(anywhere(), anywhere()),
        scratch_shapes=[
            room(8, *SLOT), room(tall, chan, width), room(tall, LEV, width), room(tall, LEV, width),
            room(3 * LANES, width, kind=jnp.bfloat16), room(3, 13, LEV, LANES), room(tall, chan, width), room(rows, chan, cols),
            room(48, LANES), room(9, chan, LANES), room(7, chan, LANES), room(14 * chan, 3 * LANES, kind=jnp.bfloat16),
            room(7, 2 * chan, width), room(tall, chan, width), room(tall, chan, width), dma((10,)),
        ],
        name="nest",
    )(nest_box, slots, moved, keep, pull, mixer, coef, parent_step)
    return parent_new, nest_new


def solution(mesh):
    grid = Mesh(mesh.devices.reshape(2, 2, 4, 2, 8), SEC + TILE)
    in_specs = (P(TILE, None, SEC), P(SEC, TILE, None, None), P(), P(), P(), P(), P())
    out_specs = (P(TILE, None, SEC), P(SEC, TILE, None, None))
    return jax.shard_map(body, mesh=grid, in_specs=in_specs, out_specs=out_specs, check_vma=False)
```

```python
import itertools

import jax
import jax.numpy as jnp
from jax import lax
from jax.experimental import pallas as pl
from jax.experimental.pallas import tpu as pltpu
from jax.sharding import Mesh
from jax.sharding import PartitionSpec as P

NSTEP = 4
LEV = 8
SEC = ("yl", "co")
TILE = ("tx", "th", "tz")
LANES = 128
SLOT = (7, 8, 128)
APRON = 2
MESH = pl.DeviceIdType.MESH
F32 = jnp.float32


def vmem():
    return pl.BlockSpec(memory_space=pltpu.VMEM)


def smem():
    return pl.BlockSpec(memory_space=pltpu.SMEM)


def anywhere():
    return pl.BlockSpec(memory_space=pl.ANY)


def section():
    return lax.axis_index("yl") * 2 + lax.axis_index("co")


def tile_number():
    return lax.axis_index("tx") * 16 + lax.axis_index("th") * 8 + lax.axis_index("tz")


def lane_ids():
    return lax.broadcasted_iota(jnp.int32, (LEV, LANES), 1)


def level_ids():
    return lax.broadcasted_iota(jnp.int32, (LEV, LANES), 0)


def spread_out(column):
    return jnp.broadcast_to(column, (LEV, LANES))


def pack_edges(pad, edge, rows, count):
    lane = lane_ids()
    for which in range(2):
        block, off = (APRON, 0) if which == 0 else (APRON + count - 1, LANES - 1)
        for f in range(3):
            total = jnp.zeros((LEV, LANES), F32)
            for r in range(rows):
                piece = pad[block, r, pl.ds(8 * f, 8), :]
                total = jnp.where(lane == r, spread_out(piece[:, off : off + 1]), total)
            edge[which, pl.ds(8 * f, 8), :] = total


def pack_nest(order, box, pad, extra, win, rows, cols):
    lane = lane_ids()
    level = level_ids()
    tile = tile_number()
    nest = (order % 2) * 2 + order // 2
    ox = box[nest, 0]
    oy = box[nest, 1]
    start = jnp.clip(oy - cols * section() - 1, -APRON * LANES, cols) + APRON * LANES
    block = start // LANES
    shift = start - block * LANES + 1

    back = (LANES - shift) % LANES

    def turned(piece):
        return pltpu.roll(piece, back, 1)

    def window(r, f):
        near = turned(pad[block, r, pl.ds(8 * f, 8), :])
        next_piece = pad[block + 1, r, pl.ds(8 * f, 8), :]
        far = turned(next_piece)
        return jnp.where(lane + shift < LANES, near, far), near, far

    for k in range(rows // 2):
        packed = jnp.zeros((LEV, LANES), F32)
        for par in range(2):
            r = 2 * k + par
            foot = rows * tile + r - ox
            keep = jnp.where((foot >= 0) & (foot < 256), 1.0, 0.0).astype(F32)
            for f in range(3):
                inner, near, far = window(r, f)
                win[order, k, 3 * par + f] = inner * keep
                far = jnp.where(shift < LANES, far, pad[block + 2, r, pl.ds(8 * f, 8), :])
                pair = jnp.where(lane % 2 == 0, spread_out(near[:, LANES - 1 : LANES]), spread_out(far[:, 0:1]))
                packed = jnp.where(lane // 2 == 6 * level + 2 * f + par, pair * keep, packed)
        line = jnp.sum(packed, axis=0, keepdims=True)
        win[order, k, 6] = jnp.where(level == 6, jnp.broadcast_to(line, (LEV, LANES)), 0.0)

    for e, row in enumerate((ox - 1 - rows * tile, ox + 256 - rows * tile)):
        keep = jnp.where((row >= 0) & (row < rows), 1.0, 0.0).astype(F32)
        r = jnp.clip(row, 0, rows - 1)
        for f in range(3):
            extra[pl.ds(24 * e + 8 * f, 8), :] = window(r, f)[0] * keep
    for k in range(8):
        win[order, k, 6, 0:6, :] = extra[6 * k : 6 * k + 6, :]


def step_kernel(box, diffusion, wind, conversion, mix, nest, parent, parent_out, slots_out, moved_out, keep_out, pull_out, mixer_out,
                coef_out, win, edge, near, comb, gathered, summed,
                ready, sends, rowhalo, colhalo, pad, extra, coef, result, own, low, high, state_a, state_b, keep, pull, mixer,
                sem_s, sem_r, sem1_s, sem1_r, semz_s, semz_r, sem2_s, sem2_r, sem_p, sem_l):
    yl, co, tx, th, tz = (lax.axis_index(a) for a in ("yl", "co", "tx", "th", "tz"))
    mine = tx * 2 + th
    sec = yl * 2 + co
    tile = tx * 16 + th * 8 + tz
    here = dict(yl=yl, co=co, tx=tx, th=th, tz=tz)
    rows, chan, cols = parent.shape
    count = cols // LANES
    span, width = nest.shape[1], nest.shape[3]
    tall = span + 2 * NSTEP
    lane = lane_ids()
    level = level_ids()

    def tile_at(t):
        return dict(here, tx=t // 16, th=(t // 8) % 2, tz=t % 8)

    def sec_at(s):
        return dict(here, yl=s // 2, co=s % 2)

    core = dict(here, co=1 - co)
    following, before = tile_at((tile + 1) % 64), tile_at((tile + 63) % 64)
    east, west = sec_at((sec + 1) % 4), sec_at((sec + 3) % 4)
    cross = [
        (dict(here, tx=(tx + dx) % 4, th=(th + dh) % 2, yl=(yl + dl) % 2), dx, dh, dl)
        for dh, dx, dl in itertools.product((0, 1), (2, 1, 3, 0), (1, 0))
        if (dx, dh, dl) != (0, 0, 0)
    ]
    ring = [dict(here, tz=(tz + dz) % 8) for dz in (4, 3, 5, 2, 6, 1, 7)]
    greet = [core, following, before, east, west] + [c[0] for c in cross] + ring
    barrier = pltpu.get_barrier_semaphore()
    loads = [
        pltpu.make_async_copy(parent.at[:, :, pl.ds(LANES * q, LANES)], pad.at[APRON + q], sem_p.at[q]) for q in range(count)
    ]
    for copy in loads:
        copy.start()
    load_own = pltpu.make_async_copy(nest.at[0], own, sem_l.at[0])
    load_own.start()
    for device in greet:
        pl.semaphore_signal(barrier, inc=1, device_id=device, device_id_type=MESH)

    def empty(i, carry):
        for q in (0, 1, APRON + count, APRON + count + 1, APRON + count + 2):
            pad[q, i] = jnp.zeros((chan, LANES), F32)
        return carry

    lax.fori_loop(0, rows, empty, 0)
    for copy in loads:
        copy.wait()

    def pack(order, carry):
        pack_nest(order, box, pad, extra, win, rows, cols)
        return carry

    lax.fori_loop((1 - co) * 2, (1 - co) * 2 + 2, pack, 0)
    pl.semaphore_wait(barrier, len(greet))

    def make(src, dst, s, r, device):
        return pltpu.make_async_remote_copy(src_ref=src, dst_ref=dst, send_sem=s, recv_sem=r, device_id=device, device_id_type=MESH)

    def send(*parts):
        copy = make(*parts)
        copy.start()
        return copy

    first = send(win.at[pl.ds((1 - co) * 2, 2)], near, sem_s.at[0], sem_r.at[0], core)
    onward = [
        make(parent.at[rows - 1], rowhalo.at[0], sem_s.at[5], sem_r.at[5], following),
        make(nest.at[0, pl.ds(span - NSTEP, NSTEP)], low, sem_s.at[3], sem_r.at[3], following),
    ]
    backward = [
        make(parent.at[0], rowhalo.at[1], sem_s.at[6], sem_r.at[6], before),
        make(nest.at[0, pl.ds(0, NSTEP)], high, sem_s.at[4], sem_r.at[4], before),
    ]

    for copy in onward + backward:
        copy.start()
    lax.fori_loop(co * 2, co * 2 + 2, pack, 0)
    pack_edges(pad, edge, rows, count)
    columns = [
        send(edge.at[1], colhalo.at[0], sem_s.at[1], sem_r.at[1], east),
        send(edge.at[0], colhalo.at[1], sem_s.at[2], sem_r.at[2], west),
    ]
    fill_coefs(coef, diffusion, wind, conversion, mix)
    first.wait()

    def combine(k, carry):
        for l in range(2):
            comb[l, k] = win[co * 2 + l, k] + near[l, k]
        return carry

    lax.fori_loop(0, 8, combine, 0)

    copies = []
    for j, (device, dx, dh, dl) in enumerate(cross):
        to = device["tx"] * 2 + device["th"]
        copies.append(send(comb.at[device["yl"], to], gathered.at[tx, yl, th], sem1_s.at[j], sem1_r.at[j], device))
    gathered[tx, yl, th] = comb[yl, mine]

    have = [jnp.where(c, 1.0, 0.0).astype(F32) for c in (tile > 0, tile < 63, sec > 0, sec < 3)]

    def inner(i):
        return lambda f, q: pad[APRON + q, i, pl.ds(8 * f, 8), :]

    def outer(which):
        return lambda f, q: rowhalo[which, pl.ds(8 * f, 8), pl.ds(LANES * q, LANES)] * have[which]

    def parent_row(i, north, south):
        def rim(which):
            return lambda f: spread_out(
                jnp.sum(jnp.where(lane == i, colhalo[which, pl.ds(8 * f, 8), :], 0.0), axis=1, keepdims=True) * have[2 + which])

        for q, done in advance(coef, count, north, inner(i), south, rim(0), rim(1)):
            for f in range(3):
                result[i, pl.ds(8 * f, 8), pl.ds(LANES * q, LANES)] = done[f]

    def parent_rows(i, carry):
        parent_row(i, inner(i - 1), inner(i + 1))
        return carry

    for copy in columns:
        copy.wait()
    lax.fori_loop(1, rows - 1, parent_rows, 0)

    def gather(half, part):
        for copy in part:
            copy.wait()
        total = gathered[0, 0, half]
        for x, l in itertools.product(range(4), range(2)):
            if (x, l) != (0, 0):
                total = total + gathered[x, l, half]
        summed[tz, half] = total

    def around(half, which):
        return [
            send(summed.at[tz, half], summed.at[tz, half], semz_s.at[7 * which + j], semz_r.at[7 * which + j], device)
            for j, device in enumerate(ring)
        ]

    gather(th, copies[:7])
    rounds = around(th, 0)

    ox, ex, ey = box[sec, 0], box[sec, 2], box[sec, 3]
    row_id = span * tile - NSTEP + lax.broadcasted_iota(jnp.int32, (tall, width), 0)
    col_id = lax.broadcasted_iota(jnp.int32, (tall, width), 1)
    live = jnp.where((row_id >= 0) & (row_id < ex) & (col_id < ey), 1.0, 0.0).astype(F32)
    distance = jnp.minimum(jnp.minimum(row_id, col_id), jnp.minimum(ex - 1 - row_id, ey - 1 - col_id))
    nudging = 0.1 + 0.4 * jnp.exp(jnp.maximum(distance, 0).astype(F32) * (-1.0 / 3.0))
    kept, pulled = live * (1.0 - nudging), live * nudging
    for i in range(tall):
        keep[i] = jnp.broadcast_to(kept[i : i + 1, :], (LEV, width))
        pull[i] = jnp.broadcast_to(pulled[i : i + 1, :], (LEV, width))

    def begin(src, i, at):
        number = span * tile - NSTEP + at
        alive = jnp.where((number >= 0) & (number < ex) & (lax.broadcasted_iota(jnp.int32, (chan, width), 1) < ey), 1.0, 0.0)
        state_a[at] = src[i] * alive.astype(F32)

    def begin_own(i, carry):
        begin(own, i, NSTEP + i)
        return carry

    load_own.wait()
    lax.fori_loop(0, span, begin_own, 0)

    gather(1 - th, copies[7:])
    rounds += around(1 - th, 1)

    def first_row(i):
        for q, done in nest_row(coef, state_a, i):
            for f in range(3):
                state_b[i, pl.ds(8 * f, 8), pl.ds(LANES * q, LANES)] = done[f]

    def first_rows(first):
        def pair(m, carry):
            first_row(first + 2 * m)
            first_row(first + 2 * m + 1)
            return carry

        return pair

    lax.fori_loop(0, span // 2 - 1, first_rows(NSTEP + 1), 0)

    cells = lax.broadcasted_iota(jnp.int32, (LANES, width), 0)
    targets = lax.broadcasted_iota(jnp.int32, (LANES, width), 1)
    weight = (targets % 4).astype(F32) * 0.25
    low_cell = targets // 4
    high_cell = jnp.minimum(low_cell + 1, LANES - 1)
    mixed = (jnp.where(cells == low_cell, 1.0 - weight, 0.0) + jnp.where(cells == high_cell, weight, 0.0)).astype(jnp.bfloat16)
    for i in range(3):
        mixer[LANES * i : LANES * (i + 1), :] = mixed

    out_moved, out_keep, out_pull = (
        pltpu.make_async_copy(src, dst, sem_l.at[i])
        for i, (src, dst) in enumerate(((state_b, moved_out), (keep, keep_out), (pull, pull_out)), 2)
    )
    out_keep.start()
    out_pull.start()
    out_mixer = pltpu.make_async_copy(mixer, mixer_out, sem_l.at[5])
    out_mixer.start()
    out_coef = pltpu.make_async_copy(coef, coef_out, sem_l.at[6])
    out_coef.start()
    for copy in rounds:
        copy.wait()

    lines = summed[0, 0, 6]
    for z, h in itertools.product(range(8), range(2)):
        if (z, h) != (0, 0):
            lines = lines + summed[z, h, 6]

    def pick(device, where, slot):
        t = device["tx"] * 16 + device["th"] * 8 + tz
        q = ((ox + 4 * t + 254) % 256) // 2
        q = (q + (mine - q + 128) % 8) % 128
        z, h = (q // 8) % 8, q // 64
        where[slot, 0:6] = summed[z, h, 0:6]
        where[slot, 6] = jnp.where(level < 6, lines, summed[z, h, 6])

    copies = []
    j = 0
    for device, dx, dh, dl in cross[::-1]:
        if dl == 0:
            pick(device, sends, j)
            copies.append(send(sends.at[j], ready.at[mine], sem2_s.at[j], sem2_r.at[j], device))
            j += 1
    pick(here, ready, mine)

    onward[0].wait()
    backward[0].wait()
    parent_row(0, outer(0), inner(1))
    parent_row(rows - 1, inner(rows - 2), outer(1))
    state_b[0] = jnp.zeros((chan, width), F32)
    state_b[tall - 1] = jnp.zeros((chan, width), F32)
    store = pltpu.make_async_copy(result, parent_out, sem_l.at[1])
    store.start()
    onward[1].wait()
    backward[1].wait()
    for i in range(NSTEP):
        begin(low, i, i)
        begin(high, i, span + NSTEP + i)
    lax.fori_loop(0, 2, first_rows(1), 0)
    lax.fori_loop(0, 2, first_rows(span + NSTEP - 1), 0)
    out_moved.start()
    for copy in (store, out_keep, out_pull, out_mixer, out_coef, out_moved):
        copy.wait()
    for copy in copies:
        copy.wait()
    finish = pltpu.make_async_copy(ready, slots_out, sem_l.at[7])
    finish.start()
    finish.wait()


def fill_coefs(coef, diffusion, wind, conversion, mix):
    level = level_ids()

    def column(read):
        out = jnp.zeros((LEV, LANES), F32)
        for l in range(LEV):
            out = jnp.where(level == l, read(l), out)
        return out

    spread, scale = [], []
    for f in range(3):
        d = column(lambda l: diffusion[8 * f + l])
        wx = column(lambda l: wind[0, 8 * f + l])
        wy = column(lambda l: wind[1, 8 * f + l])
        coef[f, 0] = (1.0 - 4.0 * d - wx - wy) / d
        coef[f, 1] = (d + wx) / d
        coef[f, 2] = (d + wy) / d
        m = mix[f] * jnp.ones((LEV, LANES), F32)
        lower = jnp.where(level > 0, -m, 0.0)
        upper = jnp.where(level < LEV - 1, -m, 0.0)
        diag = 1.0 + m * jnp.where((level == 0) | (level == LEV - 1), 1.0, 2.0)
        steps = []
        for s in (1, 2, 4):
            alpha = -lower / pltpu.roll(diag, s, 0)
            gamma = -upper / pltpu.roll(diag, LEV - s, 0)
            new_diag = diag + alpha * pltpu.roll(upper, s, 0) + gamma * pltpu.roll(lower, LEV - s, 0)
            lower, upper = alpha * pltpu.roll(lower, s, 0), gamma * pltpu.roll(upper, LEV - s, 0)
            diag = new_diag
            steps.append((alpha, gamma))
        for n, s in enumerate((1, 2)):
            coef[f, 5 + 2 * n] = steps[n][0] * pltpu.roll(diag, s, 0) / diag
            coef[f, 6 + 2 * n] = steps[n][1] * pltpu.roll(diag, LEV - s, 0) / diag
        coef[f, 9] = (steps[2][0] + steps[2][1]) * pltpu.roll(diag, 4, 0) / diag
        spread.append(d)
        scale.append(1.0 / diag)
    c0 = column(lambda l: conversion[0, l])
    c1 = column(lambda l: conversion[1, l])
    coef[0, 3] = c0 * spread[0]
    coef[0, 4] = scale[0] * (1.0 - c0) * spread[0]
    coef[1, 3] = spread[1]
    coef[1, 4] = scale[1] * (1.0 - c1)
    coef[2, 3] = scale[2] * spread[2]
    coef[2, 4] = scale[2] * c1


def solve(coef, f, r):
    r = r + coef[f, 5] * pltpu.roll(r, 1, 0) + coef[f, 6] * pltpu.roll(r, 7, 0)
    r = r + coef[f, 7] * pltpu.roll(r, 2, 0) + coef[f, 8] * pltpu.roll(r, 6, 0)
    return r + coef[f, 9] * pltpu.roll(r, 4, 0)


def physics(coef, vapour, cloud, rain):
    wet = coef[1, 3] * cloud + coef[0, 3] * vapour
    fields = (coef[0, 4] * vapour, coef[1, 4] * wet, coef[2, 3] * rain + coef[2, 4] * wet)
    return [solve(coef, f, fields[f]) for f in range(3)]


def advance(coef, count, north, center, south, first, last):
    lane = lane_ids()
    tile, right, left = {}, {}, {}

    def read(f, q):
        if (f, q) not in tile:
            tile[f, q] = center(f, q)
            right[f, q] = pltpu.roll(tile[f, q], 1, 1)
            left[f, q] = pltpu.roll(tile[f, q], LANES - 1, 1)

    for q in range(count):
        moved = []
        for f in range(3):
            read(f, q)
            if q + 1 < count:
                read(f, q + 1)
            west = jnp.where(lane == 0, first(f) if q == 0 else right[f, q - 1], right[f, q])
            east = jnp.where(lane == LANES - 1, last(f) if q == count - 1 else left[f, q + 1], left[f, q])
            moved.append((south(f, q) + east) + coef[f, 0] * tile[f, q] + coef[f, 1] * north(f, q) + coef[f, 2] * west)
        yield q, physics(coef, *moved)


def nest_row(coef, src, i):
    zero = jnp.zeros((LEV, LANES), F32)
    read = lambda k: lambda f, q: src[k, pl.ds(8 * f, 8), pl.ds(LANES * q, LANES)]
    yield from advance(coef, src.shape[2] // LANES, read(i - 1), read(i), read(i + 1), lambda f: zero, lambda f: zero)


def nest_kernel(box, slots, moved, keep_in, pull_in, mixer_in, coef_in, parent_step, nest_out, parent_out, ready, state_b, keep, pull,
                mixer, coef, state_a, passed, extra, old, new, flat, wide, base, base_b, drift, sem):
    first = [pltpu.make_async_copy(slots, ready, sem.at[0]), pltpu.make_async_copy(coef_in, coef, sem.at[1])]
    rest = [
        pltpu.make_async_copy(moved, state_b, sem.at[2]),
        pltpu.make_async_copy(keep_in, keep, sem.at[3]),
        pltpu.make_async_copy(pull_in, pull, sem.at[4]),
        pltpu.make_async_copy(mixer_in, mixer, sem.at[5]),
    ]
    take = pltpu.make_async_copy(parent_step, passed, sem.at[6])
    give = pltpu.make_async_copy(passed, parent_out, sem.at[7])
    for copy in first + rest[3:] + rest[:3] + [take]:
        copy.start()
    tile = tile_number()
    ox = box[section(), 0]
    tall, chan, width = state_a.shape
    span = tall - 2 * NSTEP
    blocks = width // LANES
    lane = lane_ids()
    level = level_ids()
    for copy in first:
        copy.wait()

    for k in range(8):
        extra[6 * k : 6 * k + 6, :] = ready[k, 6, 0:6, :]

    def place(j):
        residue = (ox + 4 * tile + 254 + j) % 256
        return (residue // 2) % 8, residue % 2

    for j in range(9):
        k, par = place(j)
        for f in range(3):
            old[j, pl.ds(8 * f, 8), :] = ready[k, 3 * par + f]

    @pl.when(tile == 0)
    def _():
        old[1] = extra[0:24, :]

    @pl.when(tile == 63)
    def _():
        old[6] = extra[24:48, :]

    for j in range(1, 8):
        k, par = place(j)
        line = jnp.broadcast_to(ready[k, 6][6:7, :], (LEV, LANES))

        def beyond(which):
            def column(f):
                at = 12 * level + 4 * f + 2 * par + which
                return spread_out(jnp.sum(jnp.where(lane == at, line, 0.0), axis=1, keepdims=True))

            return column

        read = lambda i: lambda f, q: old[i, pl.ds(8 * f, 8), :]
        for q, done in advance(coef, 1, read(j - 1), read(j), read(j + 1), beyond(0), beyond(1)):
            for f in range(3):
                new[j - 1, pl.ds(8 * f, 8), :] = done[f]

    @pl.when(tile == 63)
    def _():
        old[6] = old[5]
        new[5] = new[4]

    for j in range(7):
        part = jnp.concatenate([old[j + 1], (new[j] - old[j + 1]) * (1.0 / NSTEP)], axis=0)
        for i in range(3):
            rounded = part.astype(jnp.bfloat16)
            flat[pl.ds(48 * j, 48), LANES * i : LANES * (i + 1)] = rounded
            part = part - rounded.astype(F32)
    rest[3].wait()
    wide[...] = jnp.dot(flat[...], mixer[...], preferred_element_type=F32).reshape(7, 2 * chan, width)

    take.wait()
    give.start()

    def pulls(u, carry):
        for q in range(blocks):
            columns = pl.ds(LANES * q, LANES)
            for f in range(3):
                at, to = pl.ds(8 * f, 8), pl.ds(chan + 8 * f, 8)
                from_old, from_change = wide[u, at, columns], wide[u, to, columns]
                over_old, over_change = wide[u + 1, at, columns] - from_old, wide[u + 1, to, columns] - from_change
                for p in range(4):
                    i = 4 * u + p
                    p_row = pull[i, :, columns]
                    now, change = (from_old, from_change) if p == 0 else (from_old + 0.25 * p * over_old, from_change + 0.25 * p * over_change)
                    now, change = p_row * now, p_row * change
                    now = now + change
                    base[i, at, columns] = now + change
                    drift[i, at, columns] = change
                    state_b[i, at, columns] = keep[i, :, columns] * state_b[i, at, columns] + now
        return carry

    for copy in rest[:3]:
        copy.wait()
    lax.fori_loop(0, tall // 4, pulls, 0)

    def step_rows(src, dst, first, group, here, there):
        def several(m, carry):
            for i in range(group):
                i = first + group * m + i
                for q, done in nest_row(coef, src, i):
                    columns = pl.ds(LANES * q, LANES)
                    k_row = keep[i, :, columns]
                    for f in range(3):
                        at = pl.ds(8 * f, 8)
                        now = here[i, at, columns]
                        dst[i, at, columns] = k_row * done[f] + now
                        if there is not None:
                            there[i, at, columns] = now + drift[i, at, columns]
            return carry

        return several

    lax.fori_loop(0, (tall - 4) // 4, step_rows(state_b, state_a, 2, 4, base, base_b), 0)
    lax.fori_loop(0, (tall - 6) // 6, step_rows(state_a, state_b, 3, 6, base_b, base), 0)
    half = span // 2
    parts = []
    for part in range(2):
        lax.fori_loop(0, half // 4, step_rows(state_b, state_a, NSTEP + half * part, 4, base, None), 0)
        parts.append(pltpu.make_async_copy(state_a.at[pl.ds(NSTEP + half * part, half)], nest_out.at[0, pl.ds(half * part, half)], sem.at[8 + part]))
        parts[-1].start()
    for copy in parts:
        copy.wait()
    give.wait()


def body(parent_old, nest_state, diffusion, wind_speed, conversion, vert_mix, nest_box):
    rows, chan, cols = parent_old.shape
    span, width = nest_state.shape[1], nest_state.shape[3]
    tall = span + 2 * NSTEP
    shape = jax.ShapeDtypeStruct
    dma = pltpu.SemaphoreType.DMA

    def room(*dims, kind=F32):
        return pltpu.VMEM(dims, kind)

    parent_step, slots, moved, keep, pull, mixer, coef = pl.pallas_call(
        step_kernel,
        out_shape=(
            shape(parent_old.shape, F32), shape((8, *SLOT), F32), shape((tall, chan, width), F32), shape((tall, LEV, width), F32),
            shape((tall, LEV, width), F32), shape((3 * LANES, width), jnp.bfloat16), shape((3, 10, LEV, LANES), F32),
        ),
        in_specs=[smem()] * 5 + [anywhere()] * 2,
        out_specs=(anywhere(),) * 7,
        scratch_shapes=[
            room(4, 8, *SLOT), room(2, chan, LANES), room(2, 8, *SLOT), room(2, 8, *SLOT), room(4, 2, 2, *SLOT), room(8, 2, *SLOT),
            room(8, *SLOT), room(7, *SLOT), room(2, chan, cols), room(2, chan, LANES),
            room(cols // LANES + 5, rows, chan, LANES), room(48, LANES), room(3, 10, LEV, LANES), room(rows, chan, cols),
            room(span, chan, width), room(NSTEP, chan, width), room(NSTEP, chan, width), room(tall, chan, width), room(tall, chan, width),
            room(tall, LEV, width), room(tall, LEV, width), room(3 * LANES, width, kind=jnp.bfloat16),
            dma((7,)), dma((7,)), dma((15,)), dma((15,)), dma((14,)), dma((14,)), dma((7,)), dma((7,)), dma((cols // LANES,)), dma((8,)),
        ],
        compiler_params=pltpu.CompilerParams(collective_id=0, has_side_effects=True),
        name="step",
    )(nest_box, diffusion, wind_speed, conversion, vert_mix, nest_state, parent_old)
    nest_new, parent_new = pl.pallas_call(
        nest_kernel,
        out_shape=(shape(nest_state.shape, F32), shape(parent_old.shape, F32)),
        in_specs=[smem()] + [anywhere()] * 7,
        out_specs=(anywhere(), anywhere()),
        scratch_shapes=[
            room(8, *SLOT), room(tall, chan, width), room(tall, LEV, width), room(tall, LEV, width),
            room(3 * LANES, width, kind=jnp.bfloat16), room(3, 10, LEV, LANES), room(tall, chan, width), room(rows, chan, cols),
            room(48, LANES), room(9, chan, LANES), room(7, chan, LANES), room(14 * chan, 3 * LANES, kind=jnp.bfloat16),
            room(7, 2 * chan, width), room(tall, chan, width), room(tall, chan, width), room(tall, chan, width), dma((10,)),
        ],
        name="nest",
    )(nest_box, slots, moved, keep, pull, mixer, coef, parent_step)
    return parent_new, nest_new


def solution(mesh):
    grid = Mesh(mesh.devices.reshape(2, 2, 4, 2, 8), SEC + TILE)
    in_specs = (P(TILE, None, SEC), P(SEC, TILE, None, None), P(), P(), P(), P(), P())
    out_specs = (P(TILE, None, SEC), P(SEC, TILE, None, None))
    return jax.shard_map(body, mesh=grid, in_specs=in_specs, out_specs=out_specs, check_vma=False)
```

```python
import itertools

import jax
import jax.numpy as jnp
from jax import lax
from jax.experimental import pallas as pl
from jax.experimental.pallas import tpu as pltpu
from jax.sharding import Mesh
from jax.sharding import PartitionSpec as P

NSTEP = 4
LEV = 8
SEC = ("yl", "co")
TILE = ("tx", "th", "tz")
LANES = 128
SLOT = (7, 8, 128)
APRON = 2
MESH = pl.DeviceIdType.MESH
F32 = jnp.float32


def vmem():
    return pl.BlockSpec(memory_space=pltpu.VMEM)


def smem():
    return pl.BlockSpec(memory_space=pltpu.SMEM)


def anywhere():
    return pl.BlockSpec(memory_space=pl.ANY)


def section():
    return lax.axis_index("yl") * 2 + lax.axis_index("co")


def tile_number():
    return lax.axis_index("tx") * 16 + lax.axis_index("th") * 8 + lax.axis_index("tz")


def lane_ids():
    return lax.broadcasted_iota(jnp.int32, (LEV, LANES), 1)


def level_ids():
    return lax.broadcasted_iota(jnp.int32, (LEV, LANES), 0)


def spread_out(column):
    return jnp.broadcast_to(column, (LEV, LANES))


def pack_edges(pad, edge, rows, count):
    lane = lane_ids()
    for which in range(2):
        block, off = (APRON, 0) if which == 0 else (APRON + count - 1, LANES - 1)
        for f in range(3):
            total = jnp.zeros((LEV, LANES), F32)
            for r in range(rows):
                piece = pad[block, r, pl.ds(8 * f, 8), :]
                total = jnp.where(lane == r, spread_out(piece[:, off : off + 1]), total)
            edge[which, pl.ds(8 * f, 8), :] = total


def pack_nest(order, box, pad, extra, win, rows, cols):
    lane = lane_ids()
    level = level_ids()
    tile = tile_number()
    nest = (order % 2) * 2 + order // 2
    ox = box[nest, 0]
    oy = box[nest, 1]
    start = jnp.clip(oy - cols * section() - 1, -APRON * LANES, cols) + APRON * LANES
    block = start // LANES
    shift = start - block * LANES + 1

    back = (LANES - shift) % LANES

    def window(r, f):
        near = pad[block, r, pl.ds(8 * f, 8), :]
        far = pad[block + 1, r, pl.ds(8 * f, 8), :]
        return pltpu.roll(jnp.where(lane >= shift, near, far), back, 1), near, far

    beyond = (shift == LANES) & (lane == 0)
    for k in range(rows // 2):
        packed = jnp.zeros((LEV, LANES), F32)
        for par in range(2):
            r = 2 * k + par
            foot = rows * tile + r - ox
            keep = jnp.where((foot >= 0) & (foot < 256), 1.0, 0.0).astype(F32)
            for f in range(3):
                inner, near, far = window(r, f)
                win[order, k, 3 * par + f] = inner * keep
                sides = jnp.where(lane < shift, near, far)
                sides = jnp.where(beyond, pad[block + 2, r, pl.ds(8 * f, 8), :], sides)
                pair = 2 * f + par
                sides = pltpu.roll(sides, (2 * pair + 1 + LANES - shift) % LANES, 1)
                packed = jnp.where(lane // 2 == pair, sides * keep, packed)
        for bit in (1, 2, 4):
            packed = jnp.where((level // bit) % 2 == 1, pltpu.roll(packed, 12 * bit, 1), packed)
        line = jnp.sum(packed, axis=0, keepdims=True)
        win[order, k, 6] = jnp.where(level == 6, jnp.broadcast_to(line, (LEV, LANES)), 0.0)

    for e, row in enumerate((ox - 1 - rows * tile, ox + 256 - rows * tile)):
        keep = jnp.where((row >= 0) & (row < rows), 1.0, 0.0).astype(F32)
        r = jnp.clip(row, 0, rows - 1)
        for f in range(3):
            extra[pl.ds(24 * e + 8 * f, 8), :] = window(r, f)[0] * keep
    for k in range(8):
        win[order, k, 6, 0:6, :] = extra[6 * k : 6 * k + 6, :]


def step_kernel(box, diffusion, wind, conversion, mix, nest, parent, parent_out, slots_out, moved_out, keep_out, pull_out, mixer_out,
                coef_out, win, edge, near, comb, gathered, summed,
                ready, sends, rowhalo, colhalo, pad, extra, coef, result, own, low, high, state_a, state_b, keep, pull, mixer,
                sem_s, sem_r, sem1_s, sem1_r, semz_s, semz_r, sem2_s, sem2_r, sem_p, sem_l):
    yl, co, tx, th, tz = (lax.axis_index(a) for a in ("yl", "co", "tx", "th", "tz"))
    mine = tx * 2 + th
    sec = yl * 2 + co
    tile = tx * 16 + th * 8 + tz
    here = dict(yl=yl, co=co, tx=tx, th=th, tz=tz)
    rows, chan, cols = parent.shape
    count = cols // LANES
    span, width = nest.shape[1], nest.shape[3]
    tall = span + 2 * NSTEP
    lane = lane_ids()
    level = level_ids()

    def tile_at(t):
        return dict(here, tx=t // 16, th=(t // 8) % 2, tz=t % 8)

    def sec_at(s):
        return dict(here, yl=s // 2, co=s % 2)

    core = dict(here, co=1 - co)
    following, before = tile_at((tile + 1) % 64), tile_at((tile + 63) % 64)
    east, west = sec_at((sec + 1) % 4), sec_at((sec + 3) % 4)
    cross = [
        (dict(here, tx=(tx + dx) % 4, th=(th + dh) % 2, yl=(yl + dl) % 2), dx, dh, dl)
        for dh, dx, dl in itertools.product((0, 1), (2, 1, 3, 0), (1, 0))
        if (dx, dh, dl) != (0, 0, 0)
    ]
    ring = [dict(here, tz=(tz + dz) % 8) for dz in (4, 3, 5, 2, 6, 1, 7)]
    greet = [core, following, before, east, west] + [c[0] for c in cross] + ring
    barrier = pltpu.get_barrier_semaphore()
    loads = [
        pltpu.make_async_copy(parent.at[:, :, pl.ds(LANES * q, LANES)], pad.at[APRON + q], sem_p.at[q]) for q in range(count)
    ]
    for copy in loads:
        copy.start()
    load_own = pltpu.make_async_copy(nest.at[0], own, sem_l.at[0])
    load_own.start()
    for device in greet:
        pl.semaphore_signal(barrier, inc=1, device_id=device, device_id_type=MESH)

    def empty(i, carry):
        for q in (0, 1, APRON + count, APRON + count + 1, APRON + count + 2):
            pad[q, i] = jnp.zeros((chan, LANES), F32)
        return carry

    lax.fori_loop(0, rows, empty, 0)
    for copy in loads:
        copy.wait()

    def pack(order, carry):
        pack_nest(order, box, pad, extra, win, rows, cols)
        return carry

    lax.fori_loop((1 - co) * 2, (1 - co) * 2 + 2, pack, 0)
    pl.semaphore_wait(barrier, len(greet))

    def make(src, dst, s, r, device):
        return pltpu.make_async_remote_copy(src_ref=src, dst_ref=dst, send_sem=s, recv_sem=r, device_id=device, device_id_type=MESH)

    def send(*parts):
        copy = make(*parts)
        copy.start()
        return copy

    first = send(win.at[pl.ds((1 - co) * 2, 2)], near, sem_s.at[0], sem_r.at[0], core)
    onward = [
        make(parent.at[rows - 1], rowhalo.at[0], sem_s.at[5], sem_r.at[5], following),
        make(nest.at[0, pl.ds(span - NSTEP, NSTEP)], low, sem_s.at[3], sem_r.at[3], following),
    ]
    backward = [
        make(parent.at[0], rowhalo.at[1], sem_s.at[6], sem_r.at[6], before),
        make(nest.at[0, pl.ds(0, NSTEP)], high, sem_s.at[4], sem_r.at[4], before),
    ]

    for copy in onward + backward:
        copy.start()
    lax.fori_loop(co * 2, co * 2 + 2, pack, 0)
    pack_edges(pad, edge, rows, count)
    columns = [
        send(edge.at[1], colhalo.at[0], sem_s.at[1], sem_r.at[1], east),
        send(edge.at[0], colhalo.at[1], sem_s.at[2], sem_r.at[2], west),
    ]
    fill_coefs(coef, diffusion, wind, conversion, mix)
    first.wait()

    def combine(k, carry):
        for l in range(2):
            comb[l, k] = win[co * 2 + l, k] + near[l, k]
        return carry

    lax.fori_loop(0, 8, combine, 0)

    copies = []
    for j, (device, dx, dh, dl) in enumerate(cross):
        to = device["tx"] * 2 + device["th"]
        copies.append(send(comb.at[device["yl"], to], gathered.at[tx, yl, th], sem1_s.at[j], sem1_r.at[j], device))
    gathered[tx, yl, th] = comb[yl, mine]

    have = [jnp.where(c, 1.0, 0.0).astype(F32) for c in (tile > 0, tile < 63, sec > 0, sec < 3)]

    def inner(i):
        return lambda f, q: pad[APRON + q, i, pl.ds(8 * f, 8), :]

    def outer(which):
        return lambda f, q: rowhalo[which, pl.ds(8 * f, 8), pl.ds(LANES * q, LANES)] * have[which]

    def parent_row(i, north, south):
        def rim(which):
            return lambda f: spread_out(
                jnp.sum(jnp.where(lane == i, colhalo[which, pl.ds(8 * f, 8), :], 0.0), axis=1, keepdims=True) * have[2 + which])

        for q, done in advance(coef, count, north, inner(i), south, rim(0), rim(1)):
            for f in range(3):
                result[i, pl.ds(8 * f, 8), pl.ds(LANES * q, LANES)] = done[f]

    def parent_rows(i, carry):
        parent_row(i, inner(i - 1), inner(i + 1))
        return carry

    for copy in columns:
        copy.wait()
    lax.fori_loop(1, rows // 2, parent_rows, 0)

    def gather(half, part):
        for copy in part:
            copy.wait()
        total = gathered[0, 0, half]
        for x, l in itertools.product(range(4), range(2)):
            if (x, l) != (0, 0):
                total = total + gathered[x, l, half]
        summed[tz, half] = total

    def around(half, which):
        return [
            send(summed.at[tz, half], summed.at[tz, half], semz_s.at[7 * which + j], semz_r.at[7 * which + j], device)
            for j, device in enumerate(ring)
        ]

    gather(th, copies[:7])
    rounds = around(th, 0)

    ox, ex, ey = box[sec, 0], box[sec, 2], box[sec, 3]
    row_id = span * tile - NSTEP + lax.broadcasted_iota(jnp.int32, (tall, width), 0)
    col_id = lax.broadcasted_iota(jnp.int32, (tall, width), 1)
    live = jnp.where((row_id >= 0) & (row_id < ex) & (col_id < ey), 1.0, 0.0).astype(F32)
    distance = jnp.minimum(jnp.minimum(row_id, col_id), jnp.minimum(ex - 1 - row_id, ey - 1 - col_id))
    nudging = 0.1 + 0.4 * jnp.exp(jnp.maximum(distance, 0).astype(F32) * (-1.0 / 3.0))
    kept, pulled = live * (1.0 - nudging), live * nudging
    for i in range(tall):
        keep[i] = jnp.broadcast_to(kept[i : i + 1, :], (LEV, width))
        pull[i] = jnp.broadcast_to(pulled[i : i + 1, :], (LEV, width))

    def begin(src, i, at):
        number = span * tile - NSTEP + at
        alive = jnp.where((number >= 0) & (number < ex) & (lax.broadcasted_iota(jnp.int32, (chan, width), 1) < ey), 1.0, 0.0)
        state_a[at] = src[i] * alive.astype(F32)

    def begin_own(i, carry):
        begin(own, i, NSTEP + i)
        return carry

    load_own.wait()
    lax.fori_loop(0, span, begin_own, 0)

    gather(1 - th, copies[7:])
    rounds += around(1 - th, 1)

    def first_row(i):
        for q, done in nest_row(coef, state_a, i):
            for f in range(3):
                state_b[i, pl.ds(8 * f, 8), pl.ds(LANES * q, LANES)] = done[f]

    def first_rows(first):
        def pair(m, carry):
            first_row(first + 2 * m)
            first_row(first + 2 * m + 1)
            return carry

        return pair

    lax.fori_loop(rows // 2, rows - 1, parent_rows, 0)
    lax.fori_loop(0, span // 2 - 1, first_rows(NSTEP + 1), 0)

    cells = lax.broadcasted_iota(jnp.int32, (LANES, width), 0)
    targets = lax.broadcasted_iota(jnp.int32, (LANES, width), 1)
    weight = (targets % 4).astype(F32) * 0.25
    low_cell = targets // 4
    high_cell = jnp.minimum(low_cell + 1, LANES - 1)
    mixed = (jnp.where(cells == low_cell, 1.0 - weight, 0.0) + jnp.where(cells == high_cell, weight, 0.0)).astype(jnp.bfloat16)
    for i in range(3):
        mixer[LANES * i : LANES * (i + 1), :] = mixed

    out_moved, out_keep, out_pull = (
        pltpu.make_async_copy(src, dst, sem_l.at[i])
        for i, (src, dst) in enumerate(((state_b, moved_out), (keep, keep_out), (pull, pull_out)), 2)
    )
    out_keep.start()
    out_pull.start()
    out_mixer = pltpu.make_async_copy(mixer, mixer_out, sem_l.at[5])
    out_mixer.start()
    out_coef = pltpu.make_async_copy(coef, coef_out, sem_l.at[6])
    out_coef.start()
    for copy in rounds:
        copy.wait()

    lines = summed[0, 0, 6]
    for z, h in itertools.product(range(8), range(2)):
        if (z, h) != (0, 0):
            lines = lines + summed[z, h, 6]

    def pick(device, where, slot):
        t = device["tx"] * 16 + device["th"] * 8 + tz
        q = ((ox + 4 * t + 254) % 256) // 2
        q = (q + (mine - q + 128) % 8) % 128
        z, h = (q // 8) % 8, q // 64
        where[slot, 0:6] = summed[z, h, 0:6]
        where[slot, 6] = jnp.where(level < 6, lines, summed[z, h, 6])

    copies = []
    j = 0
    for device, dx, dh, dl in cross[::-1]:
        if dl == 0:
            pick(device, sends, j)
            copies.append(send(sends.at[j], ready.at[mine], sem2_s.at[j], sem2_r.at[j], device))
            j += 1
    pick(here, ready, mine)

    onward[0].wait()
    backward[0].wait()
    parent_row(0, outer(0), inner(1))
    parent_row(rows - 1, inner(rows - 2), outer(1))
    state_b[0] = jnp.zeros((chan, width), F32)
    state_b[tall - 1] = jnp.zeros((chan, width), F32)
    store = pltpu.make_async_copy(result, parent_out, sem_l.at[1])
    store.start()
    onward[1].wait()
    backward[1].wait()
    for i in range(NSTEP):
        begin(low, i, i)
        begin(high, i, span + NSTEP + i)
    lax.fori_loop(0, 2, first_rows(1), 0)
    lax.fori_loop(0, 2, first_rows(span + NSTEP - 1), 0)
    out_moved.start()
    for copy in (store, out_keep, out_pull, out_mixer, out_coef, out_moved):
        copy.wait()
    for copy in copies:
        copy.wait()
    finish = pltpu.make_async_copy(ready, slots_out, sem_l.at[7])
    finish.start()
    finish.wait()


def fill_coefs(coef, diffusion, wind, conversion, mix):
    level = level_ids()

    def column(read):
        out = jnp.zeros((LEV, LANES), F32)
        for l in range(LEV):
            out = jnp.where(level == l, read(l), out)
        return out

    spread, scale = [], []
    for f in range(3):
        d = column(lambda l: diffusion[8 * f + l])
        wx = column(lambda l: wind[0, 8 * f + l])
        wy = column(lambda l: wind[1, 8 * f + l])
        coef[f, 0] = (1.0 - 4.0 * d - wx - wy) / d
        coef[f, 1] = (d + wx) / d
        coef[f, 2] = (d + wy) / d
        m = mix[f] * jnp.ones((LEV, LANES), F32)
        lower = jnp.where(level > 0, -m, 0.0)
        upper = jnp.where(level < LEV - 1, -m, 0.0)
        diag = 1.0 + m * jnp.where((level == 0) | (level == LEV - 1), 1.0, 2.0)
        steps = []
        for s in (1, 2, 4):
            alpha = -lower / pltpu.roll(diag, s, 0)
            gamma = -upper / pltpu.roll(diag, LEV - s, 0)
            new_diag = diag + alpha * pltpu.roll(upper, s, 0) + gamma * pltpu.roll(lower, LEV - s, 0)
            lower, upper = alpha * pltpu.roll(lower, s, 0), gamma * pltpu.roll(upper, LEV - s, 0)
            diag = new_diag
            steps.append((alpha, gamma))
        for n, s in enumerate((1, 2)):
            coef[f, 5 + 2 * n] = steps[n][0] * pltpu.roll(diag, s, 0) / diag
            coef[f, 6 + 2 * n] = steps[n][1] * pltpu.roll(diag, LEV - s, 0) / diag
        coef[f, 9] = (steps[2][0] + steps[2][1]) * pltpu.roll(diag, 4, 0) / diag
        spread.append(d)
        scale.append(1.0 / diag)
    c0 = column(lambda l: conversion[0, l])
    c1 = column(lambda l: conversion[1, l])
    coef[0, 3] = c0 * spread[0]
    coef[0, 4] = scale[0] * (1.0 - c0) * spread[0]
    coef[1, 3] = spread[1]
    coef[1, 4] = scale[1] * (1.0 - c1)
    coef[2, 3] = scale[2] * spread[2]
    coef[2, 4] = scale[2] * c1


def solve(coef, f, r):
    r = r + coef[f, 5] * pltpu.roll(r, 1, 0) + coef[f, 6] * pltpu.roll(r, 7, 0)
    r = r + coef[f, 7] * pltpu.roll(r, 2, 0) + coef[f, 8] * pltpu.roll(r, 6, 0)
    return r + coef[f, 9] * pltpu.roll(r, 4, 0)


def physics(coef, vapour, cloud, rain):
    wet = coef[1, 3] * cloud + coef[0, 3] * vapour
    fields = (coef[0, 4] * vapour, coef[1, 4] * wet, coef[2, 3] * rain + coef[2, 4] * wet)
    return [solve(coef, f, fields[f]) for f in range(3)]


def advance(coef, count, north, center, south, first, last):
    lane = lane_ids()
    tile, right, left = {}, {}, {}

    def read(f, q):
        if (f, q) not in tile:
            tile[f, q] = center(f, q)
            right[f, q] = pltpu.roll(tile[f, q], 1, 1)
            left[f, q] = pltpu.roll(tile[f, q], LANES - 1, 1)

    for q in range(count):
        moved = []
        for f in range(3):
            read(f, q)
            if q + 1 < count:
                read(f, q + 1)
            west = jnp.where(lane == 0, first(f) if q == 0 else right[f, q - 1], right[f, q])
            east = jnp.where(lane == LANES - 1, last(f) if q == count - 1 else left[f, q + 1], left[f, q])
            moved.append((south(f, q) + east) + coef[f, 0] * tile[f, q] + coef[f, 1] * north(f, q) + coef[f, 2] * west)
        yield q, physics(coef, *moved)


def nest_row(coef, src, i):
    zero = jnp.zeros((LEV, LANES), F32)
    read = lambda k: lambda f, q: src[k, pl.ds(8 * f, 8), pl.ds(LANES * q, LANES)]
    yield from advance(coef, src.shape[2] // LANES, read(i - 1), read(i), read(i + 1), lambda f: zero, lambda f: zero)


def nest_kernel(box, slots, moved, keep_in, pull_in, mixer_in, coef_in, parent_step, nest_out, parent_out, ready, state_b, keep, pull,
                mixer, coef, state_a, passed, extra, old, new, flat, wide, base, base_b, drift, sem):
    first = [pltpu.make_async_copy(slots, ready, sem.at[0]), pltpu.make_async_copy(coef_in, coef, sem.at[1])]
    rest = [
        pltpu.make_async_copy(moved, state_b, sem.at[2]),
        pltpu.make_async_copy(keep_in, keep, sem.at[3]),
        pltpu.make_async_copy(pull_in, pull, sem.at[4]),
        pltpu.make_async_copy(mixer_in, mixer, sem.at[5]),
    ]
    take = pltpu.make_async_copy(parent_step, passed, sem.at[6])
    give = pltpu.make_async_copy(passed, parent_out, sem.at[7])
    for copy in first + rest[3:] + rest[:3] + [take]:
        copy.start()
    tile = tile_number()
    ox = box[section(), 0]
    tall, chan, width = state_a.shape
    span = tall - 2 * NSTEP
    blocks = width // LANES
    lane = lane_ids()
    level = level_ids()
    for copy in first:
        copy.wait()

    for k in range(8):
        extra[6 * k : 6 * k + 6, :] = ready[k, 6, 0:6, :]

    def place(j):
        residue = (ox + 4 * tile + 254 + j) % 256
        return (residue // 2) % 8, residue % 2

    for j in range(9):
        k, par = place(j)
        for f in range(3):
            old[j, pl.ds(8 * f, 8), :] = ready[k, 3 * par + f]

    @pl.when(tile == 0)
    def _():
        old[1] = extra[0:24, :]

    @pl.when(tile == 63)
    def _():
        old[6] = extra[24:48, :]

    for j in range(1, 8):
        k, par = place(j)
        line = jnp.broadcast_to(ready[k, 6][6:7, :], (LEV, LANES))

        def beyond(which):
            def column(f):
                at = 12 * level + 4 * f + 2 * par + which
                return spread_out(jnp.sum(jnp.where(lane == at, line, 0.0), axis=1, keepdims=True))

            return column

        read = lambda i: lambda f, q: old[i, pl.ds(8 * f, 8), :]
        for q, done in advance(coef, 1, read(j - 1), read(j), read(j + 1), beyond(0), beyond(1)):
            for f in range(3):
                new[j - 1, pl.ds(8 * f, 8), :] = done[f]

    @pl.when(tile == 63)
    def _():
        old[6] = old[5]
        new[5] = new[4]

    for j in range(7):
        part = jnp.concatenate([old[j + 1], (new[j] - old[j + 1]) * (1.0 / NSTEP)], axis=0)
        for i in range(3):
            rounded = part.astype(jnp.bfloat16)
            flat[pl.ds(48 * j, 48), LANES * i : LANES * (i + 1)] = rounded
            part = part - rounded.astype(F32)
    rest[3].wait()
    wide[...] = jnp.dot(flat[...], mixer[...], preferred_element_type=F32).reshape(7, 2 * chan, width)

    take.wait()
    give.start()

    def pulls(u, carry):
        for q in range(blocks):
            columns = pl.ds(LANES * q, LANES)
            for f in range(3):
                at, to = pl.ds(8 * f, 8), pl.ds(chan + 8 * f, 8)
                from_old, from_change = wide[u, at, columns], wide[u, to, columns]
                over_old, over_change = wide[u + 1, at, columns] - from_old, wide[u + 1, to, columns] - from_change
                for p in range(4):
                    i = 4 * u + p
                    p_row = pull[i, :, columns]
                    now, change = (from_old, from_change) if p == 0 else (from_old + 0.25 * p * over_old, from_change + 0.25 * p * over_change)
                    now, change = p_row * now, p_row * change
                    now = now + change
                    base[i, at, columns] = now + change
                    drift[i, at, columns] = change
                    state_b[i, at, columns] = keep[i, :, columns] * state_b[i, at, columns] + now
        return carry

    for copy in rest[:3]:
        copy.wait()
    lax.fori_loop(0, tall // 4, pulls, 0)

    def step_rows(src, dst, first, group, here, there):
        def several(m, carry):
            for i in range(group):
                i = first + group * m + i
                for q, done in nest_row(coef, src, i):
                    columns = pl.ds(LANES * q, LANES)
                    k_row = keep[i, :, columns]
                    for f in range(3):
                        at = pl.ds(8 * f, 8)
                        now = here[i, at, columns]
                        dst[i, at, columns] = k_row * done[f] + now
                        if there is not None:
                            there[i, at, columns] = now + drift[i, at, columns]
            return carry

        return several

    lax.fori_loop(0, (tall - 4) // 4, step_rows(state_b, state_a, 2, 4, base, base_b), 0)
    lax.fori_loop(0, (tall - 6) // 6, step_rows(state_a, state_b, 3, 6, base_b, base), 0)
    half = span // 2
    parts = []
    for part in range(2):
        lax.fori_loop(0, half // 4, step_rows(state_b, state_a, NSTEP + half * part, 4, base, None), 0)
        parts.append(pltpu.make_async_copy(state_a.at[pl.ds(NSTEP + half * part, half)], nest_out.at[0, pl.ds(half * part, half)], sem.at[8 + part]))
        parts[-1].start()
    for copy in parts:
        copy.wait()
    give.wait()


def body(parent_old, nest_state, diffusion, wind_speed, conversion, vert_mix, nest_box):
    rows, chan, cols = parent_old.shape
    span, width = nest_state.shape[1], nest_state.shape[3]
    tall = span + 2 * NSTEP
    shape = jax.ShapeDtypeStruct
    dma = pltpu.SemaphoreType.DMA

    def room(*dims, kind=F32):
        return pltpu.VMEM(dims, kind)

    parent_step, slots, moved, keep, pull, mixer, coef = pl.pallas_call(
        step_kernel,
        out_shape=(
            shape(parent_old.shape, F32), shape((8, *SLOT), F32), shape((tall, chan, width), F32), shape((tall, LEV, width), F32),
            shape((tall, LEV, width), F32), shape((3 * LANES, width), jnp.bfloat16), shape((3, 10, LEV, LANES), F32),
        ),
        in_specs=[smem()] * 5 + [anywhere()] * 2,
        out_specs=(anywhere(),) * 7,
        scratch_shapes=[
            room(4, 8, *SLOT), room(2, chan, LANES), room(2, 8, *SLOT), room(2, 8, *SLOT), room(4, 2, 2, *SLOT), room(8, 2, *SLOT),
            room(8, *SLOT), room(7, *SLOT), room(2, chan, cols), room(2, chan, LANES),
            room(cols // LANES + 5, rows, chan, LANES), room(48, LANES), room(3, 10, LEV, LANES), room(rows, chan, cols),
            room(span, chan, width), room(NSTEP, chan, width), room(NSTEP, chan, width), room(tall, chan, width), room(tall, chan, width),
            room(tall, LEV, width), room(tall, LEV, width), room(3 * LANES, width, kind=jnp.bfloat16),
            dma((7,)), dma((7,)), dma((15,)), dma((15,)), dma((14,)), dma((14,)), dma((7,)), dma((7,)), dma((cols // LANES,)), dma((8,)),
        ],
        compiler_params=pltpu.CompilerParams(collective_id=0, has_side_effects=True),
        name="step",
    )(nest_box, diffusion, wind_speed, conversion, vert_mix, nest_state, parent_old)
    nest_new, parent_new = pl.pallas_call(
        nest_kernel,
        out_shape=(shape(nest_state.shape, F32), shape(parent_old.shape, F32)),
        in_specs=[smem()] + [anywhere()] * 7,
        out_specs=(anywhere(), anywhere()),
        scratch_shapes=[
            room(8, *SLOT), room(tall, chan, width), room(tall, LEV, width), room(tall, LEV, width),
            room(3 * LANES, width, kind=jnp.bfloat16), room(3, 10, LEV, LANES), room(tall, chan, width), room(rows, chan, cols),
            room(48, LANES), room(9, chan, LANES), room(7, chan, LANES), room(14 * chan, 3 * LANES, kind=jnp.bfloat16),
            room(7, 2 * chan, width), room(tall, chan, width), room(tall, chan, width), room(tall, chan, width), dma((10,)),
        ],
        name="nest",
    )(nest_box, slots, moved, keep, pull, mixer, coef, parent_step)
    return parent_new, nest_new


def solution(mesh):
    grid = Mesh(mesh.devices.reshape(2, 2, 4, 2, 8), SEC + TILE)
    in_specs = (P(TILE, None, SEC), P(SEC, TILE, None, None), P(), P(), P(), P(), P())
    out_specs = (P(TILE, None, SEC), P(SEC, TILE, None, None))
    return jax.shard_map(body, mesh=grid, in_specs=in_specs, out_specs=out_specs, check_vma=False)
```

```python
import itertools

import jax
import jax.numpy as jnp
from jax import lax
from jax.experimental import pallas as pl
from jax.experimental.pallas import tpu as pltpu
from jax.sharding import Mesh
from jax.sharding import PartitionSpec as P

NSTEP = 4
LEV = 8
SEC = ("yl", "co")
TILE = ("tx", "th", "tz")
LANES = 128
SLOT = (7, 8, 128)
APRON = 2
MESH = pl.DeviceIdType.MESH
F32 = jnp.float32


def vmem():
    return pl.BlockSpec(memory_space=pltpu.VMEM)


def smem():
    return pl.BlockSpec(memory_space=pltpu.SMEM)


def anywhere():
    return pl.BlockSpec(memory_space=pl.ANY)


def section():
    return lax.axis_index("yl") * 2 + lax.axis_index("co")


def tile_number():
    return lax.axis_index("tx") * 16 + lax.axis_index("th") * 8 + lax.axis_index("tz")


def lane_ids():
    return lax.broadcasted_iota(jnp.int32, (LEV, LANES), 1)


def level_ids():
    return lax.broadcasted_iota(jnp.int32, (LEV, LANES), 0)


def spread_out(column):
    return jnp.broadcast_to(column, (LEV, LANES))


def pack_edges(pad, edge, rows, count):
    lane = lane_ids()
    for which in range(2):
        block, off = (APRON, 0) if which == 0 else (APRON + count - 1, LANES - 1)
        for f in range(3):
            total = jnp.zeros((LEV, LANES), F32)
            for r in range(rows):
                piece = pad[block, r, pl.ds(8 * f, 8), :]
                total = jnp.where(lane == r, spread_out(piece[:, off : off + 1]), total)
            edge[which, pl.ds(8 * f, 8), :] = total


def pack_nest(order, box, pad, extra, win, rows, cols):
    lane = lane_ids()
    level = level_ids()
    tile = tile_number()
    nest = (order % 2) * 2 + order // 2
    ox = box[nest, 0]
    oy = box[nest, 1]
    start = jnp.clip(oy - cols * section() - 1, -APRON * LANES, cols) + APRON * LANES
    block = start // LANES
    shift = start - block * LANES + 1

    back = (LANES - shift) % LANES

    def window(r, f):
        near = pad[block, r, pl.ds(8 * f, 8), :]
        far = pad[block + 1, r, pl.ds(8 * f, 8), :]
        return pltpu.roll(jnp.where(lane >= shift, near, far), back, 1), near, far

    beyond = (shift == LANES) & (lane == 0)
    from_left = (lane - shift + 1 + LANES) % LANES
    for k in range(rows // 2):
        packed = jnp.zeros((LEV, LANES), F32)
        for par in range(2):
            r = 2 * k + par
            foot = rows * tile + r - ox
            keep = jnp.where((foot >= 0) & (foot < 256), 1.0, 0.0).astype(F32)
            for f in range(3):
                inner, near, far = window(r, f)
                win[order, k, 3 * par + f] = inner * keep
                sides = jnp.where(lane < shift, near, far)
                sides = jnp.where(beyond, pad[block + 2, r, pl.ds(8 * f, 8), :], sides)
                pair = 2 * f + par
                sides = sides * keep
                packed = jnp.where(from_left // 2 == pair, pltpu.roll(sides, 2 * pair, 1) if pair else sides, packed)
        packed = pltpu.roll(packed, (1 + LANES - shift) % LANES, 1)
        for bit in (1, 2, 4):
            packed = jnp.where((level // bit) % 2 == 1, pltpu.roll(packed, 12 * bit, 1), packed)
        line = jnp.sum(packed, axis=0, keepdims=True)
        win[order, k, 6] = jnp.where(level == 6, jnp.broadcast_to(line, (LEV, LANES)), 0.0)

    for e, row in enumerate((ox - 1 - rows * tile, ox + 256 - rows * tile)):
        keep = jnp.where((row >= 0) & (row < rows), 1.0, 0.0).astype(F32)
        r = jnp.clip(row, 0, rows - 1)
        for f in range(3):
            extra[pl.ds(24 * e + 8 * f, 8), :] = window(r, f)[0] * keep
    for k in range(8):
        win[order, k, 6, 0:6, :] = extra[6 * k : 6 * k + 6, :]


def step_kernel(box, diffusion, wind, conversion, mix, nest, parent, parent_out, slots_out, moved_out, keep_out, pull_out, mixer_out,
                coef_out, win, edge, near, comb, gathered, summed,
                sends, rowhalo, colhalo, pad, extra, coef, result, own, low, high, state_a, state_b, keep, pull, mixer,
                sem_s, sem_r, sem1_s, sem1_r, semz_s, semz_r, sem2_s, sem2_r, sem_p, sem_l):
    yl, co, tx, th, tz = (lax.axis_index(a) for a in ("yl", "co", "tx", "th", "tz"))
    mine = tx * 2 + th
    sec = yl * 2 + co
    tile = tx * 16 + th * 8 + tz
    here = dict(yl=yl, co=co, tx=tx, th=th, tz=tz)
    rows, chan, cols = parent.shape
    count = cols // LANES
    span, width = nest.shape[1], nest.shape[3]
    tall = span + 2 * NSTEP
    lane = lane_ids()
    level = level_ids()

    def tile_at(t):
        return dict(here, tx=t // 16, th=(t // 8) % 2, tz=t % 8)

    def sec_at(s):
        return dict(here, yl=s // 2, co=s % 2)

    core = dict(here, co=1 - co)
    following, before = tile_at((tile + 1) % 64), tile_at((tile + 63) % 64)
    east, west = sec_at((sec + 1) % 4), sec_at((sec + 3) % 4)
    cross = [
        (dict(here, tx=(tx + dx) % 4, th=(th + dh) % 2, yl=(yl + dl) % 2), dx, dh, dl)
        for dh, dx, dl in itertools.product((0, 1), (2, 1, 3, 0), (1, 0))
        if (dx, dh, dl) != (0, 0, 0)
    ]
    ring = [dict(here, tz=(tz + dz) % 8) for dz in (4, 3, 5, 2, 6, 1, 7)]
    greet = [core, following, before, east, west] + [c[0] for c in cross] + ring
    barrier = pltpu.get_barrier_semaphore()
    loads = [
        pltpu.make_async_copy(parent.at[:, :, pl.ds(LANES * q, LANES)], pad.at[APRON + q], sem_p.at[q]) for q in range(count)
    ]
    for copy in loads:
        copy.start()
    load_own = pltpu.make_async_copy(nest.at[0], own, sem_l.at[0])
    load_own.start()
    for device in greet:
        pl.semaphore_signal(barrier, inc=1, device_id=device, device_id_type=MESH)

    def empty(i, carry):
        for q in (0, 1, APRON + count, APRON + count + 1, APRON + count + 2):
            pad[q, i] = jnp.zeros((chan, LANES), F32)
        return carry

    lax.fori_loop(0, rows, empty, 0)
    for copy in loads:
        copy.wait()

    def pack(order, carry):
        pack_nest(order, box, pad, extra, win, rows, cols)
        return carry

    lax.fori_loop((1 - co) * 2, (1 - co) * 2 + 2, pack, 0)
    pl.semaphore_wait(barrier, len(greet))

    def make(src, dst, s, r, device):
        return pltpu.make_async_remote_copy(src_ref=src, dst_ref=dst, send_sem=s, recv_sem=r, device_id=device, device_id_type=MESH)

    def send(*parts):
        copy = make(*parts)
        copy.start()
        return copy

    first = send(win.at[pl.ds((1 - co) * 2, 2)], near, sem_s.at[0], sem_r.at[0], core)
    onward = [
        make(parent.at[rows - 1], rowhalo.at[0], sem_s.at[5], sem_r.at[5], following),
        make(nest.at[0, pl.ds(span - NSTEP, NSTEP)], low, sem_s.at[3], sem_r.at[3], following),
    ]
    backward = [
        make(parent.at[0], rowhalo.at[1], sem_s.at[6], sem_r.at[6], before),
        make(nest.at[0, pl.ds(0, NSTEP)], high, sem_s.at[4], sem_r.at[4], before),
    ]

    for copy in onward + backward:
        copy.start()
    lax.fori_loop(co * 2, co * 2 + 2, pack, 0)
    first.wait()

    def combine(k, carry):
        for l in range(2):
            comb[l, k] = win[co * 2 + l, k] + near[l, k]
        return carry

    lax.fori_loop(0, 8, combine, 0)

    copies = []
    for j, (device, dx, dh, dl) in enumerate(cross):
        to = device["tx"] * 2 + device["th"]
        copies.append(send(comb.at[device["yl"], to], gathered.at[tx, yl, th], sem1_s.at[j], sem1_r.at[j], device))
    gathered[tx, yl, th] = comb[yl, mine]
    pack_edges(pad, edge, rows, count)
    columns = [
        send(edge.at[1], colhalo.at[0], sem_s.at[1], sem_r.at[1], east),
        send(edge.at[0], colhalo.at[1], sem_s.at[2], sem_r.at[2], west),
    ]
    fill_coefs(coef, diffusion, wind, conversion, mix)

    have = [jnp.where(c, 1.0, 0.0).astype(F32) for c in (tile > 0, tile < 63, sec > 0, sec < 3)]

    def inner(i):
        return lambda f, q: pad[APRON + q, i, pl.ds(8 * f, 8), :]

    def outer(which):
        return lambda f, q: rowhalo[which, pl.ds(8 * f, 8), pl.ds(LANES * q, LANES)] * have[which]

    def parent_row(i, north, south):
        def rim(which):
            return lambda f: spread_out(
                jnp.sum(jnp.where(lane == i, colhalo[which, pl.ds(8 * f, 8), :], 0.0), axis=1, keepdims=True) * have[2 + which])

        for q, done in advance(coef, count, north, inner(i), south, rim(0), rim(1)):
            for f in range(3):
                result[i, pl.ds(8 * f, 8), pl.ds(LANES * q, LANES)] = done[f]

    def parent_rows(i, carry):
        parent_row(i, inner(i - 1), inner(i + 1))
        return carry

    ox, ex, ey = box[sec, 0], box[sec, 2], box[sec, 3]
    row_id = span * tile - NSTEP + lax.broadcasted_iota(jnp.int32, (tall, width), 0)
    col_id = lax.broadcasted_iota(jnp.int32, (tall, width), 1)
    live = jnp.where((row_id >= 0) & (row_id < ex) & (col_id < ey), 1.0, 0.0).astype(F32)
    distance = jnp.minimum(jnp.minimum(row_id, col_id), jnp.minimum(ex - 1 - row_id, ey - 1 - col_id))
    nudging = 0.1 + 0.4 * jnp.exp(jnp.maximum(distance, 0).astype(F32) * (-1.0 / 3.0))
    kept, pulled = live * (1.0 - nudging), live * nudging
    for i in range(tall):
        keep[i] = jnp.broadcast_to(kept[i : i + 1, :], (LEV, width))
        pull[i] = jnp.broadcast_to(pulled[i : i + 1, :], (LEV, width))

    def begin(src, i, at):
        number = span * tile - NSTEP + at
        alive = jnp.where((number >= 0) & (number < ex) & (lax.broadcasted_iota(jnp.int32, (chan, width), 1) < ey), 1.0, 0.0)
        state_a[at] = src[i] * alive.astype(F32)

    def begin_own(i, carry):
        begin(own, i, NSTEP + i)
        return carry

    load_own.wait()
    lax.fori_loop(0, span, begin_own, 0)

    for copy in columns:
        copy.wait()
    lax.fori_loop(1, 5, parent_rows, 0)

    def gather(half, part):
        for copy in part:
            copy.wait()
        total = gathered[0, 0, half]
        for x, l in itertools.product(range(4), range(2)):
            if (x, l) != (0, 0):
                total = total + gathered[x, l, half]
        summed[tz, half] = total

    def around(half, which):
        return [
            send(summed.at[tz, half], summed.at[tz, half], semz_s.at[7 * which + j], semz_r.at[7 * which + j], device)
            for j, device in enumerate(ring)
        ]

    gather(th, copies[:7])
    rounds = around(th, 0)

    lax.fori_loop(5, rows // 2, parent_rows, 0)
    gather(1 - th, copies[7:])
    rounds += around(1 - th, 1)

    def first_row(i):
        for q, done in nest_row(coef, state_a, i):
            for f in range(3):
                state_b[i, pl.ds(8 * f, 8), pl.ds(LANES * q, LANES)] = done[f]

    def first_rows(first):
        def pair(m, carry):
            first_row(first + 2 * m)
            first_row(first + 2 * m + 1)
            return carry

        return pair

    lax.fori_loop(rows // 2, rows - 1, parent_rows, 0)
    lax.fori_loop(0, span // 2 - 1, first_rows(NSTEP + 1), 0)

    cells = lax.broadcasted_iota(jnp.int32, (LANES, width), 0)
    targets = lax.broadcasted_iota(jnp.int32, (LANES, width), 1)
    weight = (targets % 4).astype(F32) * 0.25
    low_cell = targets // 4
    high_cell = jnp.minimum(low_cell + 1, LANES - 1)
    mixed = (jnp.where(cells == low_cell, 1.0 - weight, 0.0) + jnp.where(cells == high_cell, weight, 0.0)).astype(jnp.bfloat16)
    for i in range(3):
        mixer[LANES * i : LANES * (i + 1), :] = mixed

    out_moved, out_keep, out_pull = (
        pltpu.make_async_copy(src, dst, sem_l.at[i])
        for i, (src, dst) in enumerate(((state_b, moved_out), (keep, keep_out), (pull, pull_out)), 2)
    )
    out_keep.start()
    out_pull.start()
    out_mixer = pltpu.make_async_copy(mixer, mixer_out, sem_l.at[5])
    out_mixer.start()
    out_coef = pltpu.make_async_copy(coef, coef_out, sem_l.at[6])
    out_coef.start()
    for copy in rounds:
        copy.wait()

    lines = summed[0, 0, 6]
    for z, h in itertools.product(range(8), range(2)):
        if (z, h) != (0, 0):
            lines = lines + summed[z, h, 6]

    def pick(device, where, slot):
        t = device["tx"] * 16 + device["th"] * 8 + tz
        q = ((ox + 4 * t + 254) % 256) // 2
        q = (q + (mine - q + 128) % 8) % 128
        z, h = (q // 8) % 8, q // 64
        where[slot, 0:6] = summed[z, h, 0:6]
        where[slot, 6] = jnp.where(level < 6, lines, summed[z, h, 6])

    copies = []
    j = 0
    for device, dx, dh, dl in cross[::-1]:
        if dl == 0:
            pick(device, sends, j)
            copies.append(send(sends.at[j], slots_out.at[mine], sem2_s.at[j], sem2_r.at[j], device))
            j += 1
    pick(here, sends, 7)
    finish = pltpu.make_async_copy(sends.at[7], slots_out.at[mine], sem_l.at[7])
    finish.start()

    onward[0].wait()
    backward[0].wait()
    parent_row(0, outer(0), inner(1))
    parent_row(rows - 1, inner(rows - 2), outer(1))
    state_b[0] = jnp.zeros((chan, width), F32)
    state_b[tall - 1] = jnp.zeros((chan, width), F32)
    store = pltpu.make_async_copy(result, parent_out, sem_l.at[1])
    store.start()
    onward[1].wait()
    backward[1].wait()
    for i in range(NSTEP):
        begin(low, i, i)
        begin(high, i, span + NSTEP + i)
    lax.fori_loop(0, 2, first_rows(1), 0)
    lax.fori_loop(0, 2, first_rows(span + NSTEP - 1), 0)
    out_moved.start()
    for copy in (store, out_keep, out_pull, out_mixer, out_coef, out_moved):
        copy.wait()
    for copy in copies:
        copy.wait()
    finish.wait()


def fill_coefs(coef, diffusion, wind, conversion, mix):
    level = level_ids()

    def column(read):
        out = jnp.zeros((LEV, LANES), F32)
        for l in range(LEV):
            out = jnp.where(level == l, read(l), out)
        return out

    spread, scale = [], []
    for f in range(3):
        d = column(lambda l: diffusion[8 * f + l])
        wx = column(lambda l: wind[0, 8 * f + l])
        wy = column(lambda l: wind[1, 8 * f + l])
        coef[f, 0] = (1.0 - 4.0 * d - wx - wy) / d
        coef[f, 1] = (d + wx) / d
        coef[f, 2] = (d + wy) / d
        m = mix[f] * jnp.ones((LEV, LANES), F32)
        lower = jnp.where(level > 0, -m, 0.0)
        upper = jnp.where(level < LEV - 1, -m, 0.0)
        diag = 1.0 + m * jnp.where((level == 0) | (level == LEV - 1), 1.0, 2.0)
        steps = []
        for s in (1, 2, 4):
            alpha = -lower / pltpu.roll(diag, s, 0)
            gamma = -upper / pltpu.roll(diag, LEV - s, 0)
            new_diag = diag + alpha * pltpu.roll(upper, s, 0) + gamma * pltpu.roll(lower, LEV - s, 0)
            lower, upper = alpha * pltpu.roll(lower, s, 0), gamma * pltpu.roll(upper, LEV - s, 0)
            diag = new_diag
            steps.append((alpha, gamma))
        for n, s in enumerate((1, 2)):
            coef[f, 5 + 2 * n] = steps[n][0] * pltpu.roll(diag, s, 0) / diag
            coef[f, 6 + 2 * n] = steps[n][1] * pltpu.roll(diag, LEV - s, 0) / diag
        coef[f, 9] = (steps[2][0] + steps[2][1]) * pltpu.roll(diag, 4, 0) / diag
        spread.append(d)
        scale.append(1.0 / diag)
    c0 = column(lambda l: conversion[0, l])
    c1 = column(lambda l: conversion[1, l])
    coef[0, 3] = c0 * spread[0]
    coef[0, 4] = scale[0] * (1.0 - c0) * spread[0]
    coef[1, 3] = spread[1]
    coef[1, 4] = scale[1] * (1.0 - c1)
    coef[2, 3] = scale[2] * spread[2]
    coef[2, 4] = scale[2] * c1


def solve(coef, f, r):
    r = r + coef[f, 5] * pltpu.roll(r, 1, 0) + coef[f, 6] * pltpu.roll(r, 7, 0)
    r = r + coef[f, 7] * pltpu.roll(r, 2, 0) + coef[f, 8] * pltpu.roll(r, 6, 0)
    return r + coef[f, 9] * pltpu.roll(r, 4, 0)


def physics(coef, vapour, cloud, rain):
    wet = coef[1, 3] * cloud + coef[0, 3] * vapour
    fields = (coef[0, 4] * vapour, coef[1, 4] * wet, coef[2, 3] * rain + coef[2, 4] * wet)
    return [solve(coef, f, fields[f]) for f in range(3)]


def advance(coef, count, north, center, south, first, last):
    lane = lane_ids()
    tile, right, left = {}, {}, {}

    def read(f, q):
        if (f, q) not in tile:
            tile[f, q] = center(f, q)
            right[f, q] = pltpu.roll(tile[f, q], 1, 1)
            left[f, q] = pltpu.roll(tile[f, q], LANES - 1, 1)

    for q in range(count):
        moved = []
        for f in range(3):
            read(f, q)
            if q + 1 < count:
                read(f, q + 1)
            west = jnp.where(lane == 0, first(f) if q == 0 else right[f, q - 1], right[f, q])
            east = jnp.where(lane == LANES - 1, last(f) if q == count - 1 else left[f, q + 1], left[f, q])
            moved.append((south(f, q) + east) + coef[f, 0] * tile[f, q] + coef[f, 1] * north(f, q) + coef[f, 2] * west)
        yield q, physics(coef, *moved)


def nest_row(coef, src, i):
    zero = jnp.zeros((LEV, LANES), F32)
    read = lambda k: lambda f, q: src[k, pl.ds(8 * f, 8), pl.ds(LANES * q, LANES)]
    yield from advance(coef, src.shape[2] // LANES, read(i - 1), read(i), read(i + 1), lambda f: zero, lambda f: zero)


def nest_kernel(box, slots, moved, keep_in, pull_in, mixer_in, coef_in, parent_step, nest_out, parent_out, ready, state_b, keep, pull,
                mixer, coef, state_a, passed, extra, old, new, flat, wide, base, base_b, drift, sem):
    first = [pltpu.make_async_copy(slots, ready, sem.at[0]), pltpu.make_async_copy(coef_in, coef, sem.at[1])]
    rest = [
        pltpu.make_async_copy(moved, state_b, sem.at[2]),
        pltpu.make_async_copy(keep_in, keep, sem.at[3]),
        pltpu.make_async_copy(pull_in, pull, sem.at[4]),
        pltpu.make_async_copy(mixer_in, mixer, sem.at[5]),
    ]
    take = pltpu.make_async_copy(parent_step, passed, sem.at[6])
    give = pltpu.make_async_copy(passed, parent_out, sem.at[7])
    for copy in first + rest[3:] + rest[:3] + [take]:
        copy.start()
    tile = tile_number()
    ox = box[section(), 0]
    tall, chan, width = state_a.shape
    span = tall - 2 * NSTEP
    blocks = width // LANES
    lane = lane_ids()
    level = level_ids()
    for copy in first:
        copy.wait()

    for k in range(8):
        extra[6 * k : 6 * k + 6, :] = ready[k, 6, 0:6, :]

    def place(j):
        residue = (ox + 4 * tile + 254 + j) % 256
        return (residue // 2) % 8, residue % 2

    for j in range(9):
        k, par = place(j)
        for f in range(3):
            old[j, pl.ds(8 * f, 8), :] = ready[k, 3 * par + f]

    @pl.when(tile == 0)
    def _():
        old[1] = extra[0:24, :]

    @pl.when(tile == 63)
    def _():
        old[6] = extra[24:48, :]

    for j in range(1, 8):
        k, par = place(j)
        line = jnp.broadcast_to(ready[k, 6][6:7, :], (LEV, LANES))

        def beyond(which):
            def column(f):
                at = 12 * level + 4 * f + 2 * par + which
                return spread_out(jnp.sum(jnp.where(lane == at, line, 0.0), axis=1, keepdims=True))

            return column

        read = lambda i: lambda f, q: old[i, pl.ds(8 * f, 8), :]
        for q, done in advance(coef, 1, read(j - 1), read(j), read(j + 1), beyond(0), beyond(1)):
            for f in range(3):
                new[j - 1, pl.ds(8 * f, 8), :] = done[f]

    @pl.when(tile == 63)
    def _():
        old[6] = old[5]
        new[5] = new[4]

    for j in range(7):
        part = jnp.concatenate([old[j + 1], (new[j] - old[j + 1]) * (1.0 / NSTEP)], axis=0)
        for i in range(3):
            rounded = part.astype(jnp.bfloat16)
            flat[pl.ds(48 * j, 48), LANES * i : LANES * (i + 1)] = rounded
            part = part - rounded.astype(F32)
    rest[3].wait()
    wide[...] = jnp.dot(flat[...], mixer[...], preferred_element_type=F32).reshape(7, 2 * chan, width)

    take.wait()
    give.start()

    def pulls(u, carry):
        for q in range(blocks):
            columns = pl.ds(LANES * q, LANES)
            for f in range(3):
                at, to = pl.ds(8 * f, 8), pl.ds(chan + 8 * f, 8)
                from_old, from_change = wide[u, at, columns], wide[u, to, columns]
                over_old, over_change = wide[u + 1, at, columns] - from_old, wide[u + 1, to, columns] - from_change
                for p in range(4):
                    i = 4 * u + p
                    p_row = pull[i, :, columns]
                    now, change = (from_old, from_change) if p == 0 else (from_old + 0.25 * p * over_old, from_change + 0.25 * p * over_change)
                    now, change = p_row * now, p_row * change
                    now = now + change
                    base[i, at, columns] = now + change
                    drift[i, at, columns] = change
                    state_b[i, at, columns] = keep[i, :, columns] * state_b[i, at, columns] + now
        return carry

    for copy in rest[:3]:
        copy.wait()
    lax.fori_loop(0, tall // 4, pulls, 0)

    def step_rows(src, dst, first, group, here, there):
        def several(m, carry):
            for i in range(group):
                i = first + group * m + i
                for q, done in nest_row(coef, src, i):
                    columns = pl.ds(LANES * q, LANES)
                    k_row = keep[i, :, columns]
                    for f in range(3):
                        at = pl.ds(8 * f, 8)
                        now = here[i, at, columns]
                        dst[i, at, columns] = k_row * done[f] + now
                        if there is not None:
                            there[i, at, columns] = now + drift[i, at, columns]
            return carry

        return several

    lax.fori_loop(0, (tall - 4) // 10, step_rows(state_b, state_a, 2, 10, base, base_b), 0)
    lax.fori_loop(0, (tall - 6) // 6, step_rows(state_a, state_b, 3, 6, base_b, base), 0)
    half = span // 2
    parts = []
    for part in range(2):
        lax.fori_loop(0, half // 8, step_rows(state_b, state_a, NSTEP + half * part, 8, base, None), 0)
        parts.append(pltpu.make_async_copy(state_a.at[pl.ds(NSTEP + half * part, half)], nest_out.at[0, pl.ds(half * part, half)], sem.at[8 + part]))
        parts[-1].start()
    for copy in parts:
        copy.wait()
    give.wait()


def body(parent_old, nest_state, diffusion, wind_speed, conversion, vert_mix, nest_box):
    rows, chan, cols = parent_old.shape
    span, width = nest_state.shape[1], nest_state.shape[3]
    tall = span + 2 * NSTEP
    shape = jax.ShapeDtypeStruct
    dma = pltpu.SemaphoreType.DMA

    def room(*dims, kind=F32):
        return pltpu.VMEM(dims, kind)

    parent_step, slots, moved, keep, pull, mixer, coef = pl.pallas_call(
        step_kernel,
        out_shape=(
            shape(parent_old.shape, F32), shape((8, *SLOT), F32), shape((tall, chan, width), F32), shape((tall, LEV, width), F32),
            shape((tall, LEV, width), F32), shape((3 * LANES, width), jnp.bfloat16), shape((3, 10, LEV, LANES), F32),
        ),
        in_specs=[smem()] * 5 + [anywhere()] * 2,
        out_specs=(anywhere(),) * 7,
        scratch_shapes=[
            room(4, 8, *SLOT), room(2, chan, LANES), room(2, 8, *SLOT), room(2, 8, *SLOT), room(4, 2, 2, *SLOT), room(8, 2, *SLOT),
            room(8, *SLOT), room(2, chan, cols), room(2, chan, LANES),
            room(cols // LANES + 5, rows, chan, LANES), room(48, LANES), room(3, 10, LEV, LANES), room(rows, chan, cols),
            room(span, chan, width), room(NSTEP, chan, width), room(NSTEP, chan, width), room(tall, chan, width), room(tall, chan, width),
            room(tall, LEV, width), room(tall, LEV, width), room(3 * LANES, width, kind=jnp.bfloat16),
            dma((7,)), dma((7,)), dma((15,)), dma((15,)), dma((14,)), dma((14,)), dma((7,)), dma((7,)), dma((cols // LANES,)), dma((8,)),
        ],
        compiler_params=pltpu.CompilerParams(collective_id=0, has_side_effects=True),
        name="step",
    )(nest_box, diffusion, wind_speed, conversion, vert_mix, nest_state, parent_old)
    nest_new, parent_new = pl.pallas_call(
        nest_kernel,
        out_shape=(shape(nest_state.shape, F32), shape(parent_old.shape, F32)),
        in_specs=[smem()] + [anywhere()] * 7,
        out_specs=(anywhere(), anywhere()),
        scratch_shapes=[
            room(8, *SLOT), room(tall, chan, width), room(tall, LEV, width), room(tall, LEV, width),
            room(3 * LANES, width, kind=jnp.bfloat16), room(3, 10, LEV, LANES), room(tall, chan, width), room(rows, chan, cols),
            room(48, LANES), room(9, chan, LANES), room(7, chan, LANES), room(14 * chan, 3 * LANES, kind=jnp.bfloat16),
            room(7, 2 * chan, width), room(tall, chan, width), room(tall, chan, width), room(tall, chan, width), dma((10,)),
        ],
        name="nest",
    )(nest_box, slots, moved, keep, pull, mixer, coef, parent_step)
    return parent_new, nest_new


def solution(mesh):
    grid = Mesh(mesh.devices.reshape(2, 2, 4, 2, 8), SEC + TILE)
    in_specs = (P(TILE, None, SEC), P(SEC, TILE, None, None), P(), P(), P(), P(), P())
    out_specs = (P(TILE, None, SEC), P(SEC, TILE, None, None))
    return jax.shard_map(body, mesh=grid, in_specs=in_specs, out_specs=out_specs, check_vma=False)
```

```python
import itertools

import jax
import jax.numpy as jnp
from jax import lax
from jax.experimental import pallas as pl
from jax.experimental.pallas import tpu as pltpu
from jax.sharding import Mesh
from jax.sharding import PartitionSpec as P

NSTEP = 4
LEV = 8
SEC = ("yl", "co")
TILE = ("tx", "th", "tz")
LANES = 128
SLOT = (7, 8, 128)
APRON = 2
MESH = pl.DeviceIdType.MESH
F32 = jnp.float32


def vmem():
    return pl.BlockSpec(memory_space=pltpu.VMEM)


def smem():
    return pl.BlockSpec(memory_space=pltpu.SMEM)


def anywhere():
    return pl.BlockSpec(memory_space=pl.ANY)


def section():
    return lax.axis_index("yl") * 2 + lax.axis_index("co")


def tile_number():
    return lax.axis_index("tx") * 16 + lax.axis_index("th") * 8 + lax.axis_index("tz")


def lane_ids():
    return lax.broadcasted_iota(jnp.int32, (LEV, LANES), 1)


def level_ids():
    return lax.broadcasted_iota(jnp.int32, (LEV, LANES), 0)


def spread_out(column):
    return jnp.broadcast_to(column, (LEV, LANES))


def pack_edges(pad, edge, rows, count):
    lane = lane_ids()
    for which in range(2):
        block, off = (APRON, 0) if which == 0 else (APRON + count - 1, LANES - 1)
        for f in range(3):
            total = jnp.zeros((LEV, LANES), F32)
            for r in range(rows):
                piece = pad[block, r, pl.ds(8 * f, 8), :]
                total = jnp.where(lane == r, spread_out(piece[:, off : off + 1]), total)
            edge[which, pl.ds(8 * f, 8), :] = total


def pack_nest(order, box, pad, extra, win, rows, cols):
    lane = lane_ids()
    level = level_ids()
    tile = tile_number()
    nest = (order % 2) * 2 + order // 2
    ox = box[nest, 0]
    oy = box[nest, 1]
    start = jnp.clip(oy - cols * section() - 1, -APRON * LANES, cols) + APRON * LANES
    block = start // LANES
    shift = start - block * LANES + 1

    back = (LANES - shift) % LANES

    def window(r, f):
        near = pad[block, r, pl.ds(8 * f, 8), :]
        far = pad[block + 1, r, pl.ds(8 * f, 8), :]
        return pltpu.roll(jnp.where(lane >= shift, near, far), back, 1), near, far

    beyond = (shift == LANES) & (lane == 0)
    from_left = (lane - shift + 1 + LANES) % LANES
    for k in range(rows // 2):
        packed = jnp.zeros((LEV, LANES), F32)
        for par in range(2):
            r = 2 * k + par
            foot = rows * tile + r - ox
            keep = jnp.where((foot >= 0) & (foot < 256), 1.0, 0.0).astype(F32)
            for f in range(3):
                inner, near, far = window(r, f)
                win[order, k, 3 * par + f] = inner * keep
                sides = jnp.where(lane < shift, near, far)
                sides = jnp.where(beyond, pad[block + 2, r, pl.ds(8 * f, 8), :], sides)
                pair = 2 * f + par
                sides = sides * keep
                packed = jnp.where(from_left // 2 == pair, pltpu.roll(sides, 2 * pair, 1) if pair else sides, packed)
        packed = pltpu.roll(packed, (1 + LANES - shift) % LANES, 1)
        for bit in (1, 2, 4):
            packed = jnp.where((level // bit) % 2 == 1, pltpu.roll(packed, 12 * bit, 1), packed)
        line = jnp.sum(packed, axis=0, keepdims=True)
        win[order, k, 6] = jnp.where(level == 6, jnp.broadcast_to(line, (LEV, LANES)), 0.0)

    for e, row in enumerate((ox - 1 - rows * tile, ox + 256 - rows * tile)):
        keep = jnp.where((row >= 0) & (row < rows), 1.0, 0.0).astype(F32)
        r = jnp.clip(row, 0, rows - 1)
        for f in range(3):
            extra[pl.ds(24 * e + 8 * f, 8), :] = window(r, f)[0] * keep
    for k in range(8):
        win[order, k, 6, 0:6, :] = extra[6 * k : 6 * k + 6, :]


def step_kernel(box, diffusion, wind, conversion, mix, nest, parent, parent_out, slots_out, moved_out, keep_out, pull_out, mixer_out,
                coef_out, win, edge, near, comb, gathered, summed,
                ready, sends, rowhalo, colhalo, pad, extra, coef, result, own, low, high, state_a, state_b, keep, pull, mixer,
                sem_s, sem_r, sem1_s, sem1_r, semz_s, semz_r, sem2_s, sem2_r, sem_p, sem_l):
    yl, co, tx, th, tz = (lax.axis_index(a) for a in ("yl", "co", "tx", "th", "tz"))
    mine = tx * 2 + th
    sec = yl * 2 + co
    tile = tx * 16 + th * 8 + tz
    here = dict(yl=yl, co=co, tx=tx, th=th, tz=tz)
    rows, chan, cols = parent.shape
    count = cols // LANES
    span, width = nest.shape[1], nest.shape[3]
    tall = span + 2 * NSTEP
    lane = lane_ids()
    level = level_ids()

    def tile_at(t):
        return dict(here, tx=t // 16, th=(t // 8) % 2, tz=t % 8)

    def sec_at(s):
        return dict(here, yl=s // 2, co=s % 2)

    core = dict(here, co=1 - co)
    following, before = tile_at((tile + 1) % 64), tile_at((tile + 63) % 64)
    east, west = sec_at((sec + 1) % 4), sec_at((sec + 3) % 4)
    cross = [
        (dict(here, tx=(tx + dx) % 4, th=(th + dh) % 2, yl=(yl + dl) % 2), dx, dh, dl)
        for dh, dx, dl in itertools.product((0, 1), (2, 1, 3, 0), (1, 0))
        if (dx, dh, dl) != (0, 0, 0)
    ]
    ring = [dict(here, tz=(tz + dz) % 8) for dz in (4, 3, 5, 2, 6, 1, 7)]
    greet = [core, following, before, east, west] + [c[0] for c in cross] + ring
    barrier = pltpu.get_barrier_semaphore()
    loads = [
        pltpu.make_async_copy(parent.at[:, :, pl.ds(LANES * q, LANES)], pad.at[APRON + q], sem_p.at[q]) for q in range(count)
    ]
    for copy in loads:
        copy.start()
    load_own = pltpu.make_async_copy(nest.at[0], own, sem_l.at[0])
    load_own.start()
    for device in greet:
        pl.semaphore_signal(barrier, inc=1, device_id=device, device_id_type=MESH)

    def empty(i, carry):
        for q in (0, 1, APRON + count, APRON + count + 1, APRON + count + 2):
            pad[q, i] = jnp.zeros((chan, LANES), F32)
        return carry

    lax.fori_loop(0, rows, empty, 0)
    for copy in loads:
        copy.wait()

    def pack(order, carry):
        pack_nest(order, box, pad, extra, win, rows, cols)
        return carry

    lax.fori_loop((1 - co) * 2, (1 - co) * 2 + 2, pack, 0)
    pl.semaphore_wait(barrier, len(greet))

    def make(src, dst, s, r, device):
        return pltpu.make_async_remote_copy(src_ref=src, dst_ref=dst, send_sem=s, recv_sem=r, device_id=device, device_id_type=MESH)

    def send(*parts):
        copy = make(*parts)
        copy.start()
        return copy

    first = send(win.at[pl.ds((1 - co) * 2, 2)], near, sem_s.at[0], sem_r.at[0], core)
    onward = [
        make(parent.at[rows - 1], rowhalo.at[0], sem_s.at[5], sem_r.at[5], following),
        make(nest.at[0, pl.ds(span - NSTEP, NSTEP)], low, sem_s.at[3], sem_r.at[3], following),
    ]
    backward = [
        make(parent.at[0], rowhalo.at[1], sem_s.at[6], sem_r.at[6], before),
        make(nest.at[0, pl.ds(0, NSTEP)], high, sem_s.at[4], sem_r.at[4], before),
    ]

    for copy in onward + backward:
        copy.start()
    lax.fori_loop(co * 2, co * 2 + 2, pack, 0)
    pack_edges(pad, edge, rows, count)
    columns = [
        send(edge.at[1], colhalo.at[0], sem_s.at[1], sem_r.at[1], east),
        send(edge.at[0], colhalo.at[1], sem_s.at[2], sem_r.at[2], west),
    ]
    fill_coefs(coef, diffusion, wind, conversion, mix)
    first.wait()

    def combine(k, carry):
        for l in range(2):
            comb[l, k] = win[co * 2 + l, k] + near[l, k]
        return carry

    lax.fori_loop(0, 8, combine, 0)

    copies = []
    for j, (device, dx, dh, dl) in enumerate(cross):
        to = device["tx"] * 2 + device["th"]
        copies.append(send(comb.at[device["yl"], to], gathered.at[tx, yl, th], sem1_s.at[j], sem1_r.at[j], device))
    gathered[tx, yl, th] = comb[yl, mine]

    have = [jnp.where(c, 1.0, 0.0).astype(F32) for c in (tile > 0, tile < 63, sec > 0, sec < 3)]

    def inner(i):
        return lambda f, q: pad[APRON + q, i, pl.ds(8 * f, 8), :]

    def outer(which):
        return lambda f, q: rowhalo[which, pl.ds(8 * f, 8), pl.ds(LANES * q, LANES)] * have[which]

    def parent_row(i, north, south):
        def rim(which):
            return lambda f: spread_out(
                jnp.sum(jnp.where(lane == i, colhalo[which, pl.ds(8 * f, 8), :], 0.0), axis=1, keepdims=True) * have[2 + which])

        for q, done in advance(coef, count, north, inner(i), south, rim(0), rim(1)):
            for f in range(3):
                result[i, pl.ds(8 * f, 8), pl.ds(LANES * q, LANES)] = done[f]

    def parent_rows(i, carry):
        parent_row(i, inner(i - 1), inner(i + 1))
        return carry

    for copy in columns:
        copy.wait()
    lax.fori_loop(1, rows // 2, parent_rows, 0)

    def gather(half, part):
        for copy in part:
            copy.wait()
        total = gathered[0, 0, half]
        for x, l in itertools.product(range(4), range(2)):
            if (x, l) != (0, 0):
                total = total + gathered[x, l, half]
        summed[tz, half] = total

    def around(half, which):
        return [
            send(summed.at[tz, half], summed.at[tz, half], semz_s.at[7 * which + j], semz_r.at[7 * which + j], device)
            for j, device in enumerate(ring)
        ]

    gather(th, copies[:7])
    rounds = around(th, 0)

    ox, ex, ey = box[sec, 0], box[sec, 2], box[sec, 3]
    row_id = span * tile - NSTEP + lax.broadcasted_iota(jnp.int32, (tall, width), 0)
    col_id = lax.broadcasted_iota(jnp.int32, (tall, width), 1)
    live = jnp.where((row_id >= 0) & (row_id < ex) & (col_id < ey), 1.0, 0.0).astype(F32)
    distance = jnp.minimum(jnp.minimum(row_id, col_id), jnp.minimum(ex - 1 - row_id, ey - 1 - col_id))
    nudging = 0.1 + 0.4 * jnp.exp(jnp.maximum(distance, 0).astype(F32) * (-1.0 / 3.0))
    kept, pulled = live * (1.0 - nudging), live * nudging
    for i in range(tall):
        keep[i] = jnp.broadcast_to(kept[i : i + 1, :], (LEV, width))
        pull[i] = jnp.broadcast_to(pulled[i : i + 1, :], (LEV, width))

    def begin(src, i, at):
        number = span * tile - NSTEP + at
        alive = jnp.where((number >= 0) & (number < ex) & (lax.broadcasted_iota(jnp.int32, (chan, width), 1) < ey), 1.0, 0.0)
        state_a[at] = src[i] * alive.astype(F32)

    def begin_own(i, carry):
        begin(own, i, NSTEP + i)
        return carry

    load_own.wait()
    lax.fori_loop(0, span, begin_own, 0)

    gather(1 - th, copies[7:])
    rounds += around(1 - th, 1)

    def first_row(i):
        for q, done in nest_row(coef, state_a, i):
            for f in range(3):
                state_b[i, pl.ds(8 * f, 8), pl.ds(LANES * q, LANES)] = done[f]

    def first_rows(first):
        def pair(m, carry):
            first_row(first + 2 * m)
            first_row(first + 2 * m + 1)
            return carry

        return pair

    lax.fori_loop(rows // 2, rows - 1, parent_rows, 0)
    lax.fori_loop(0, span // 2 - 1, first_rows(NSTEP + 1), 0)

    cells = lax.broadcasted_iota(jnp.int32, (LANES, width), 0)
    targets = lax.broadcasted_iota(jnp.int32, (LANES, width), 1)
    weight = (targets % 4).astype(F32) * 0.25
    low_cell = targets // 4
    high_cell = jnp.minimum(low_cell + 1, LANES - 1)
    mixed = (jnp.where(cells == low_cell, 1.0 - weight, 0.0) + jnp.where(cells == high_cell, weight, 0.0)).astype(jnp.bfloat16)
    for i in range(3):
        mixer[LANES * i : LANES * (i + 1), :] = mixed

    out_moved, out_keep, out_pull = (
        pltpu.make_async_copy(src, dst, sem_l.at[i])
        for i, (src, dst) in enumerate(((state_b, moved_out), (keep, keep_out), (pull, pull_out)), 2)
    )
    out_keep.start()
    out_pull.start()
    out_mixer = pltpu.make_async_copy(mixer, mixer_out, sem_l.at[5])
    out_mixer.start()
    out_coef = pltpu.make_async_copy(coef, coef_out, sem_l.at[6])
    out_coef.start()
    for copy in rounds:
        copy.wait()

    lines = summed[0, 0, 6]
    for z, h in itertools.product(range(8), range(2)):
        if (z, h) != (0, 0):
            lines = lines + summed[z, h, 6]

    def pick(device, where, slot):
        t = device["tx"] * 16 + device["th"] * 8 + tz
        q = ((ox + 4 * t + 254) % 256) // 2
        q = (q + (mine - q + 128) % 8) % 128
        z, h = (q // 8) % 8, q // 64
        where[slot, 0:6] = summed[z, h, 0:6]
        where[slot, 6] = jnp.where(level < 6, lines, summed[z, h, 6])

    copies = []
    j = 0
    for device, dx, dh, dl in cross[::-1]:
        if dl == 0:
            pick(device, sends, j)
            copies.append(send(sends.at[j], ready.at[mine], sem2_s.at[j], sem2_r.at[j], device))
            j += 1
    pick(here, ready, mine)

    onward[0].wait()
    backward[0].wait()
    parent_row(0, outer(0), inner(1))
    parent_row(rows - 1, inner(rows - 2), outer(1))
    state_b[0] = jnp.zeros((chan, width), F32)
    state_b[tall - 1] = jnp.zeros((chan, width), F32)
    store = pltpu.make_async_copy(result, parent_out, sem_l.at[1])
    store.start()
    onward[1].wait()
    backward[1].wait()
    for i in range(NSTEP):
        begin(low, i, i)
        begin(high, i, span + NSTEP + i)
    lax.fori_loop(0, 2, first_rows(1), 0)
    lax.fori_loop(0, 2, first_rows(span + NSTEP - 1), 0)
    out_moved.start()
    for copy in (store, out_keep, out_pull, out_mixer, out_coef, out_moved):
        copy.wait()
    for copy in copies:
        copy.wait()
    finish = pltpu.make_async_copy(ready, slots_out, sem_l.at[7])
    finish.start()
    finish.wait()


def fill_coefs(coef, diffusion, wind, conversion, mix):
    level = level_ids()

    def column(read):
        out = jnp.zeros((LEV, LANES), F32)
        for l in range(LEV):
            out = jnp.where(level == l, read(l), out)
        return out

    spread, scale = [], []
    for f in range(3):
        d = column(lambda l: diffusion[8 * f + l])
        wx = column(lambda l: wind[0, 8 * f + l])
        wy = column(lambda l: wind[1, 8 * f + l])
        coef[f, 0] = (1.0 - 4.0 * d - wx - wy) / d
        coef[f, 1] = (d + wx) / d
        coef[f, 2] = (d + wy) / d
        m = mix[f] * jnp.ones((LEV, LANES), F32)
        lower = jnp.where(level > 0, -m, 0.0)
        upper = jnp.where(level < LEV - 1, -m, 0.0)
        diag = 1.0 + m * jnp.where((level == 0) | (level == LEV - 1), 1.0, 2.0)
        steps = []
        for s in (1, 2, 4):
            alpha = -lower / pltpu.roll(diag, s, 0)
            gamma = -upper / pltpu.roll(diag, LEV - s, 0)
            new_diag = diag + alpha * pltpu.roll(upper, s, 0) + gamma * pltpu.roll(lower, LEV - s, 0)
            lower, upper = alpha * pltpu.roll(lower, s, 0), gamma * pltpu.roll(upper, LEV - s, 0)
            diag = new_diag
            steps.append((alpha, gamma))
        for n, s in enumerate((1, 2)):
            coef[f, 5 + 2 * n] = steps[n][0] * pltpu.roll(diag, s, 0) / diag
            coef[f, 6 + 2 * n] = steps[n][1] * pltpu.roll(diag, LEV - s, 0) / diag
        coef[f, 9] = (steps[2][0] + steps[2][1]) * pltpu.roll(diag, 4, 0) / diag
        spread.append(d)
        scale.append(1.0 / diag)
    c0 = column(lambda l: conversion[0, l])
    c1 = column(lambda l: conversion[1, l])
    coef[0, 3] = c0 * spread[0]
    coef[0, 4] = scale[0] * (1.0 - c0) * spread[0]
    coef[1, 3] = spread[1]
    coef[1, 4] = scale[1] * (1.0 - c1)
    coef[2, 3] = scale[2] * spread[2]
    coef[2, 4] = scale[2] * c1


def solve(coef, f, r):
    r = r + coef[f, 5] * pltpu.roll(r, 1, 0) + coef[f, 6] * pltpu.roll(r, 7, 0)
    r = r + coef[f, 7] * pltpu.roll(r, 2, 0) + coef[f, 8] * pltpu.roll(r, 6, 0)
    return r + coef[f, 9] * pltpu.roll(r, 4, 0)


def physics(coef, vapour, cloud, rain):
    wet = coef[1, 3] * cloud + coef[0, 3] * vapour
    fields = (coef[0, 4] * vapour, coef[1, 4] * wet, coef[2, 3] * rain + coef[2, 4] * wet)
    return [solve(coef, f, fields[f]) for f in range(3)]


def advance(coef, count, north, center, south, first, last):
    lane = lane_ids()
    tile, right, left = {}, {}, {}

    def read(f, q):
        if (f, q) not in tile:
            tile[f, q] = center(f, q)
            right[f, q] = pltpu.roll(tile[f, q], 1, 1)
            left[f, q] = pltpu.roll(tile[f, q], LANES - 1, 1)

    for q in range(count):
        moved = []
        for f in range(3):
            read(f, q)
            if q + 1 < count:
                read(f, q + 1)
            west = jnp.where(lane == 0, first(f) if q == 0 else right[f, q - 1], right[f, q])
            east = jnp.where(lane == LANES - 1, last(f) if q == count - 1 else left[f, q + 1], left[f, q])
            moved.append((south(f, q) + east) + coef[f, 0] * tile[f, q] + coef[f, 1] * north(f, q) + coef[f, 2] * west)
        yield q, physics(coef, *moved)


def nest_row(coef, src, i):
    zero = jnp.zeros((LEV, LANES), F32)
    read = lambda k: lambda f, q: src[k, pl.ds(8 * f, 8), pl.ds(LANES * q, LANES)]
    yield from advance(coef, src.shape[2] // LANES, read(i - 1), read(i), read(i + 1), lambda f: zero, lambda f: zero)


def nest_kernel(box, slots, moved, keep_in, pull_in, mixer_in, coef_in, parent_step, nest_out, parent_out, ready, state_b, keep, pull,
                mixer, coef, state_a, passed, extra, old, new, flat, wide, base, base_b, drift, sem):
    first = [pltpu.make_async_copy(slots, ready, sem.at[0]), pltpu.make_async_copy(coef_in, coef, sem.at[1])]
    rest = [
        pltpu.make_async_copy(moved, state_b, sem.at[2]),
        pltpu.make_async_copy(keep_in, keep, sem.at[3]),
        pltpu.make_async_copy(pull_in, pull, sem.at[4]),
        pltpu.make_async_copy(mixer_in, mixer, sem.at[5]),
    ]
    take = pltpu.make_async_copy(parent_step, passed, sem.at[6])
    give = pltpu.make_async_copy(passed, parent_out, sem.at[7])
    for copy in first + rest[3:] + rest[:3] + [take]:
        copy.start()
    tile = tile_number()
    ox = box[section(), 0]
    tall, chan, width = state_a.shape
    span = tall - 2 * NSTEP
    blocks = width // LANES
    lane = lane_ids()
    level = level_ids()
    for copy in first:
        copy.wait()

    for k in range(8):
        extra[6 * k : 6 * k + 6, :] = ready[k, 6, 0:6, :]

    def place(j):
        residue = (ox + 4 * tile + 254 + j) % 256
        return (residue // 2) % 8, residue % 2

    for j in range(9):
        k, par = place(j)
        for f in range(3):
            old[j, pl.ds(8 * f, 8), :] = ready[k, 3 * par + f]

    @pl.when(tile == 0)
    def _():
        old[1] = extra[0:24, :]

    @pl.when(tile == 63)
    def _():
        old[6] = extra[24:48, :]

    for j in range(1, 8):
        k, par = place(j)
        line = jnp.broadcast_to(ready[k, 6][6:7, :], (LEV, LANES))

        def beyond(which):
            def column(f):
                at = 12 * level + 4 * f + 2 * par + which
                return spread_out(jnp.sum(jnp.where(lane == at, line, 0.0), axis=1, keepdims=True))

            return column

        read = lambda i: lambda f, q: old[i, pl.ds(8 * f, 8), :]
        for q, done in advance(coef, 1, read(j - 1), read(j), read(j + 1), beyond(0), beyond(1)):
            for f in range(3):
                new[j - 1, pl.ds(8 * f, 8), :] = done[f]

    @pl.when(tile == 63)
    def _():
        old[6] = old[5]
        new[5] = new[4]

    for j in range(7):
        part = jnp.concatenate([old[j + 1], (new[j] - old[j + 1]) * (1.0 / NSTEP)], axis=0)
        for i in range(3):
            rounded = part.astype(jnp.bfloat16)
            flat[pl.ds(48 * j, 48), LANES * i : LANES * (i + 1)] = rounded
            part = part - rounded.astype(F32)
    rest[3].wait()
    wide[...] = jnp.dot(flat[...], mixer[...], preferred_element_type=F32).reshape(7, 2 * chan, width)

    take.wait()
    give.start()

    def pulls(u, carry):
        for q in range(blocks):
            columns = pl.ds(LANES * q, LANES)
            for f in range(3):
                at, to = pl.ds(8 * f, 8), pl.ds(chan + 8 * f, 8)
                from_old, from_change = wide[u, at, columns], wide[u, to, columns]
                over_old, over_change = wide[u + 1, at, columns] - from_old, wide[u + 1, to, columns] - from_change
                for p in range(4):
                    i = 4 * u + p
                    p_row = pull[i, :, columns]
                    now, change = (from_old, from_change) if p == 0 else (from_old + 0.25 * p * over_old, from_change + 0.25 * p * over_change)
                    now, change = p_row * now, p_row * change
                    now = now + change
                    base[i, at, columns] = now + change
                    drift[i, at, columns] = change
                    state_b[i, at, columns] = keep[i, :, columns] * state_b[i, at, columns] + now
        return carry

    for copy in rest[:3]:
        copy.wait()
    lax.fori_loop(0, tall // 4, pulls, 0)

    def step_rows(src, dst, first, group, here, there):
        def several(m, carry):
            for i in range(group):
                i = first + group * m + i
                for q, done in nest_row(coef, src, i):
                    columns = pl.ds(LANES * q, LANES)
                    k_row = keep[i, :, columns]
                    for f in range(3):
                        at = pl.ds(8 * f, 8)
                        now = here[i, at, columns]
                        dst[i, at, columns] = k_row * done[f] + now
                        if there is not None:
                            there[i, at, columns] = now + drift[i, at, columns]
            return carry

        return several

    lax.fori_loop(0, (tall - 4) // 10, step_rows(state_b, state_a, 2, 10, base, base_b), 0)
    lax.fori_loop(0, (tall - 6) // 6, step_rows(state_a, state_b, 3, 6, base_b, base), 0)
    half = span // 2
    parts = []
    for part in range(2):
        lax.fori_loop(0, half // 8, step_rows(state_b, state_a, NSTEP + half * part, 8, base, None), 0)
        parts.append(pltpu.make_async_copy(state_a.at[pl.ds(NSTEP + half * part, half)], nest_out.at[0, pl.ds(half * part, half)], sem.at[8 + part]))
        parts[-1].start()
    for copy in parts:
        copy.wait()
    give.wait()


def body(parent_old, nest_state, diffusion, wind_speed, conversion, vert_mix, nest_box):
    rows, chan, cols = parent_old.shape
    span, width = nest_state.shape[1], nest_state.shape[3]
    tall = span + 2 * NSTEP
    shape = jax.ShapeDtypeStruct
    dma = pltpu.SemaphoreType.DMA

    def room(*dims, kind=F32):
        return pltpu.VMEM(dims, kind)

    parent_step, slots, moved, keep, pull, mixer, coef = pl.pallas_call(
        step_kernel,
        out_shape=(
            shape(parent_old.shape, F32), shape((8, *SLOT), F32), shape((tall, chan, width), F32), shape((tall, LEV, width), F32),
            shape((tall, LEV, width), F32), shape((3 * LANES, width), jnp.bfloat16), shape((3, 10, LEV, LANES), F32),
        ),
        in_specs=[smem()] * 5 + [anywhere()] * 2,
        out_specs=(anywhere(),) * 7,
        scratch_shapes=[
            room(4, 8, *SLOT), room(2, chan, LANES), room(2, 8, *SLOT), room(2, 8, *SLOT), room(4, 2, 2, *SLOT), room(8, 2, *SLOT),
            room(8, *SLOT), room(7, *SLOT), room(2, chan, cols), room(2, chan, LANES),
            room(cols // LANES + 5, rows, chan, LANES), room(48, LANES), room(3, 10, LEV, LANES), room(rows, chan, cols),
            room(span, chan, width), room(NSTEP, chan, width), room(NSTEP, chan, width), room(tall, chan, width), room(tall, chan, width),
            room(tall, LEV, width), room(tall, LEV, width), room(3 * LANES, width, kind=jnp.bfloat16),
            dma((7,)), dma((7,)), dma((15,)), dma((15,)), dma((14,)), dma((14,)), dma((7,)), dma((7,)), dma((cols // LANES,)), dma((8,)),
        ],
        compiler_params=pltpu.CompilerParams(collective_id=0, has_side_effects=True),
        name="step",
    )(nest_box, diffusion, wind_speed, conversion, vert_mix, nest_state, parent_old)
    nest_new, parent_new = pl.pallas_call(
        nest_kernel,
        out_shape=(shape(nest_state.shape, F32), shape(parent_old.shape, F32)),
        in_specs=[smem()] + [anywhere()] * 7,
        out_specs=(anywhere(), anywhere()),
        scratch_shapes=[
            room(8, *SLOT), room(tall, chan, width), room(tall, LEV, width), room(tall, LEV, width),
            room(3 * LANES, width, kind=jnp.bfloat16), room(3, 10, LEV, LANES), room(tall, chan, width), room(rows, chan, cols),
            room(48, LANES), room(9, chan, LANES), room(7, chan, LANES), room(14 * chan, 3 * LANES, kind=jnp.bfloat16),
            room(7, 2 * chan, width), room(tall, chan, width), room(tall, chan, width), room(tall, chan, width), dma((10,)),
        ],
        name="nest",
    )(nest_box, slots, moved, keep, pull, mixer, coef, parent_step)
    return parent_new, nest_new


def solution(mesh):
    grid = Mesh(mesh.devices.reshape(2, 2, 4, 2, 8), SEC + TILE)
    in_specs = (P(TILE, None, SEC), P(SEC, TILE, None, None), P(), P(), P(), P(), P())
    out_specs = (P(TILE, None, SEC), P(SEC, TILE, None, None))
    return jax.shard_map(body, mesh=grid, in_specs=in_specs, out_specs=out_specs, check_vma=False)
```
